32 devices in a mesh: expert: 8 (over y, x, core), dp: 4 (over z).
Axes of the slice: x: 2, y: 2, z: 4, core: 2. Of those that a mesh axis runs over, the one named last changes fastest.
Arguments:
- trunk: bfloat16 [768, 4096], P(('dp', 'expert')), may hold values from -6 to 6
- w_first: bfloat16 [8, 4096, 2048], P('expert'), may hold values from -0.09375 to 0.09375
- w_second: bfloat16 [8, 2048, 1024], P('expert'), may hold values from -0.125 to 0.125
- gates: bfloat16 [8, 8, 768], P('expert', None, 'dp'), may hold values from 0.049804688 to 1
- d_mixed: bfloat16 [768, 8, 1024], P(('dp', 'expert')), may hold values from -6 to 6
Outputs:
- mixed: bfloat16 [768, 8, 1024], P(('dp', 'expert'))
- d_trunk: bfloat16 [768, 4096], P(('dp', 'expert'))
- d_gates: bfloat16 [8, 8, 768], P('expert', None, 'dp')
- d_w_first: bfloat16 [8, 4096, 2048], P('expert', 'dp')
- d_w_second: bfloat16 [8, 2048, 1024], P('expert', 'dp')
The draws below stay inside these ranges and needn't reach their ends.
All inputs are finite; a program needn't handle non-finite values.
Results may differ from the reference program's by a relative error of at most 0.015.
Values may be sent and summed in bfloat16 or wider, within the bound.
A program may use at most 128 MiB of HBM per device.

```python
import math
import jax
import jax.numpy as jnp
from jax import lax

D = 4096
H = 2048
O = 1024
TASKS = 8
EXPERTS = 8
GROUP = 192
SAMPLES = 768
N_DP = 4


def level_of(stream_key, shape, shards, smallest, high):
    factor_of, own = 1.0, jax.random.fold_in(stream_key, 6)
    for dim, blocks in shards:
        steps = jnp.exp(jax.random.uniform(jax.random.fold_in(own, dim), (blocks,), jnp.float32, smallest / len(shards), high / len(shards)))
        factor_of = factor_of * jnp.repeat(steps, shape[dim] // blocks).reshape([-1 if axis == dim else 1 for axis in range(len(shape))])
    return factor_of


def normal_values(own_key, dims, width, bound, cuts=(), dtype=jnp.bfloat16):
    entries = width * jax.random.normal(own_key, dims, jnp.float32)
    if cuts:
        entries = entries * level_of(own_key, dims, cuts, -0.22, 0.18)
    return jnp.clip(entries, -bound, bound).astype(dtype)


def setup_inputs(seed: int = 0) -> dict:
    arg_keys = jax.random.split(jax.random.key(seed), 6)
    return {
        "trunk": normal_values(arg_keys[0], (SAMPLES, D), 1.0, 6.0, ((0, 32),)),
        "w_first": normal_values(arg_keys[1], (EXPERTS, D, H), D ** -0.5, 0.09375, ((0, 8),)),
        "w_second": normal_values(arg_keys[2], (EXPERTS, H, O), H ** -0.5, 0.125, ((0, 8),)),
        "gates": jnp.clip(jnp.exp(math.log(1.0) - 2.9996462 * jax.random.uniform(arg_keys[3], (EXPERTS, TASKS, SAMPLES), jnp.float32) ** level_of(arg_keys[3], (EXPERTS, TASKS, SAMPLES), ((0, 8), (2, 4)), -0.2, 0.2)), 0.049804688, 1.0).astype(jnp.bfloat16),
        "d_mixed": normal_values(arg_keys[4], (SAMPLES, TASKS, O), 1.0, 6.0, ((0, 32),)),
    }


def reference(trunk, w_first, w_second, gates, d_mixed):
    cot = d_mixed.astype(jnp.float32)
    trunk_blocks = trunk.astype(jnp.float32).reshape(N_DP, GROUP, D)

    def per_expert(carry, packed):
        mixed_acc, trunk_acc = carry
        first, second, gate = packed
        pre = jnp.dot(trunk, first, preferred_element_type=jnp.float32)
        hidden = jax.nn.silu(pre).astype(jnp.bfloat16)
        output = jnp.dot(hidden, second, preferred_element_type=jnp.float32).astype(jnp.bfloat16)
        weight = gate.astype(jnp.float32)
        out_f = output.astype(jnp.float32)
        mixed_acc = mixed_acc + weight.T[:, :, None] * out_f[:, None, :]
        d_output = jnp.einsum("ts,sto->so", weight, cot).astype(jnp.bfloat16)
        d_gate = jnp.einsum("sto,so->ts", cot, out_f).astype(jnp.bfloat16)
        d_hidden = lax.dot_general(d_output, second, (((1,), (1,)), ((), ())), preferred_element_type=jnp.float32)
        sig = jax.nn.sigmoid(pre)
        d_pre = (d_hidden * sig * (1.0 + pre * (1.0 - sig))).astype(jnp.bfloat16)
        trunk_acc = trunk_acc + lax.dot_general(d_pre, first, (((1,), (1,)), ((), ())), preferred_element_type=jnp.float32)
        pre_blocks = d_pre.astype(jnp.float32).reshape(N_DP, GROUP, H)
        part_first = jnp.einsum("gsd,gsh->gdh", trunk_blocks, pre_blocks).astype(jnp.bfloat16)
        part_first = lax.optimization_barrier(part_first).astype(jnp.float32)
        d_first = jnp.sum(part_first, axis=0).astype(jnp.bfloat16)
        hid_blocks = hidden.astype(jnp.float32).reshape(N_DP, GROUP, H)
        dout_blocks = d_output.astype(jnp.float32).reshape(N_DP, GROUP, O)
        part_second = jnp.einsum("gsh,gso->gho", hid_blocks, dout_blocks).astype(jnp.bfloat16)
        part_second = lax.optimization_barrier(part_second).astype(jnp.float32)
        d_second = jnp.sum(part_second, axis=0).astype(jnp.bfloat16)
        return (mixed_acc, trunk_acc), (d_gate, d_first, d_second)

    init = (jnp.zeros((SAMPLES, TASKS, O), jnp.float32), jnp.zeros((SAMPLES, D), jnp.float32))
    (mixed_acc, trunk_acc), (d_gates, d_w_first, d_w_second) = lax.scan(per_expert, init, (w_first, w_second, gates))
    return (mixed_acc.astype(jnp.bfloat16), trunk_acc.astype(jnp.bfloat16), d_gates, d_w_first, d_w_second)
```

```python
import functools

import jax
import jax.numpy as jnp
from jax import lax
from jax.experimental import pallas as pl
from jax.experimental.pallas import tpu as pltpu
from jax.sharding import PartitionSpec as P

F32 = jnp.float32
BF16 = jnp.bfloat16


MESH = pl.DeviceIdType.MESH


def gather_kernel(n_e, n_d, trunk, gates, cot, first, second, rows, d_out, pre, gate_each,
                  outs, weights, later, hidden, made, m_send, m_recv, later_sem, piece, block, tall, w_sem, load_sem, store_sem,
                  g_send, g_recv, t_send, t_recv, o_send, o_recv, z_send, z_recv,
                  own_sem):
    e = lax.axis_index("expert")
    z = lax.axis_index("dp")
    partner = e + 1 - 2 * lax.rem(e, 2)
    pairs = n_e // 2

    def plane(s):
        return lax.rem(e + s, n_e)

    def along(i):
        return lax.rem(z + i, n_d)

    def remote(src, dst, send, recv, where):
        return pltpu.make_async_remote_copy(
            src_ref=src, dst_ref=dst, send_sem=send, recv_sem=recv,
            device_id=where, device_id_type=MESH)

    load_weights = pltpu.make_async_copy(first, weights, w_sem)
    load_weights.start()
    load_later = pltpu.make_async_copy(second, later, later_sem)
    load_later.start()

    barrier = pltpu.get_barrier_semaphore()
    for s in range(1, n_e):
        pl.semaphore_signal(barrier, inc=1, device_id={"expert": plane(s)}, device_id_type=MESH)
    for i in range(1, n_d):
        pl.semaphore_signal(barrier, inc=1, device_id={"dp": along(i)}, device_id_type=MESH)
    pl.semaphore_wait(barrier, n_e - 1 + n_d - 1)

    sent = []

    def go(copy):
        copy.start()
        sent.append(copy)

    for s in range(1, n_e):
        j = plane(s)
        go(remote(gates.at[j], gate_each.at[e], g_send.at[s], g_recv.at[e], {"expert": j}))
    own_gate = pltpu.make_async_copy(gates.at[e], gate_each.at[e], own_sem.at[0])
    own_gate.start()
    own_rows = pltpu.make_async_copy(trunk, rows.at[z, e], own_sem.at[1])
    own_rows.start()

    def spread(i):
        zi = along(i)
        src = trunk if i == 0 else rows.at[zi, e]
        for s in range(1, pairs):
            go(remote(src, rows.at[zi, e], t_send.at[i, s], t_recv.at[zi, e],
                      {"expert": plane(2 * s)}))
        go(remote(src, rows.at[zi, e], t_send.at[i, 0], t_recv.at[zi, e], {"expert": partner}))

    def arrived(zi, j):
        remote(trunk, rows.at[zi, j], t_send.at[0, 0], t_recv.at[zi, j],
               {"expert": partner}).wait_recv()

    for i in range(1, n_d):
        go(remote(trunk, rows.at[z, e], t_send.at[i, n_e - 1], t_recv.at[z, e], {"dp": along(i)}))
    spread(0)

    for s in range(1, n_e):
        j = plane(s)
        remote(gates.at[j], gate_each.at[j], g_send.at[0], g_recv.at[j], {"expert": j}).wait_recv()
    own_gate.wait()
    tasks = cot.shape[0]

    @pl.loop(0, n_e)
    def _(j):
        weight = gate_each[j]
        total = weight[:, 0:1] * cot[0].astype(F32)
        for t in range(1, tasks):
            total = total + weight[:, t:t + 1] * cot[t].astype(F32)
        piece[j] = total.astype(BF16)

    own_piece = pltpu.make_async_copy(piece.at[e], d_out.at[z, e], own_sem.at[2])
    own_piece.start()
    for s in range(1, n_e):
        j = plane(s)
        go(remote(piece.at[j], d_out.at[z, e], o_send.at[s], o_recv.at[e], {"expert": j}))

    def send_outputs():
        own_made.start()
        for s in range(1, n_e):
            j = plane(s)
            go(remote(made.at[j], outs.at[e], m_send.at[s], m_recv.at[e], {"expert": j}))

    own_made = pltpu.make_async_copy(made.at[e], outs.at[e], own_sem.at[3])
    stores = []
    for i in range(n_d):
        zi = along(i)
        if i + 1 < n_d:
            arrived(along(i + 1), e)
            spread(i + 1)
        if i == 1:
            send_outputs()
        if i == 0:
            for s in range(1, n_e):
                j = plane(s)
                remote(piece.at[j], d_out.at[z, j], o_send.at[0], o_recv.at[j],
                       {"expert": j}).wait_recv()
            own_piece.wait()
            for k in range(1, n_d):
                go(remote(d_out.at[z], d_out.at[z], z_send.at[k], z_recv.at[z], {"dp": along(k)}))
            own_rows.wait()
        for s in range(1, pairs):
            j = plane(2 * s)
            arrived(zi, j)
            go(remote(rows.at[zi, j], rows.at[zi, j], t_send.at[i, pairs - 1 + s],
                      t_recv.at[zi, j], {"expert": partner}))
        for s in range(pairs):
            arrived(zi, lax.rem(partner + 2 * s, n_e))
        load = pltpu.make_async_copy(rows.at[zi], block, load_sem)
        load.start()
        if i == 0:
            load_weights.wait()
        else:
            stores[-1].wait()
        load.wait()
        height = block.shape[0] * block.shape[1]
        tile = 256
        left = block[...].reshape(height, block.shape[2])

        @pl.loop(0, tall.shape[1] // tile)
        def _(c):
            here = pl.ds(pl.multiple_of(c * tile, tile), tile)
            value = jnp.dot(left, weights[:, here], preferred_element_type=F32)
            tall[:, here] = value
            if i == 0:
                hidden[:, here] = (value * jax.nn.sigmoid(value)).astype(BF16)

        store = pltpu.make_async_copy(tall, pre.at[zi], store_sem)
        store.start()
        stores.append(store)
        if i == 0:
            load_later.wait()

            @pl.loop(0, made.shape[2] // tile)
            def _(c):
                here = pl.ds(pl.multiple_of(c * tile, tile), tile)
                value = jnp.dot(hidden[...], later[:, here], preferred_element_type=F32)
                made[:, :, here] = value.astype(BF16).reshape(n_e, -1, tile)

    stores[-1].wait()
    if n_d == 1:
        send_outputs()
    own_made.wait()
    for s in range(1, n_e):
        j = plane(s)
        remote(made.at[j], outs.at[j], m_send.at[0], m_recv.at[j], {"expert": j}).wait_recv()
    for i in range(1, n_d):
        zi = along(i)
        remote(d_out.at[zi], d_out.at[zi], z_send.at[0], z_recv.at[zi], {"dp": zi}).wait_recv()
    for copy in sent:
        copy.wait_send()


def gather_all(trunk, gates, cot, first, second):
    n_e, n_d = lax.axis_size("expert"), lax.axis_size("dp")
    share, depth = trunk.shape
    width = first.shape[1]
    out = cot.shape[2]
    anywhere = pl.BlockSpec(memory_space=pl.ANY)
    hbm = pl.BlockSpec(memory_space=pltpu.HBM)
    vmem = pl.BlockSpec(memory_space=pltpu.VMEM)
    dma = pltpu.SemaphoreType.DMA
    return pl.pallas_call(
        functools.partial(gather_kernel, n_e, n_d),
        out_shape=(
            jax.ShapeDtypeStruct((n_d, n_e, share, depth), BF16),
            jax.ShapeDtypeStruct((n_d, n_e, share, out), BF16),
            jax.ShapeDtypeStruct((n_d, n_e * share, width), F32),
            jax.ShapeDtypeStruct(gates.shape, F32),
            jax.ShapeDtypeStruct((n_e, share, out), BF16),
        ),
        in_specs=[vmem, vmem, vmem, hbm, hbm],
        out_specs=(hbm, hbm, hbm, vmem, hbm),
        scratch_shapes=[
            pltpu.VMEM(first.shape, BF16),
            pltpu.VMEM(second.shape, BF16),
            pltpu.VMEM((n_e * share, width), BF16),
            pltpu.VMEM((n_e, share, out), BF16),
            dma((n_e,)), dma((n_e,)), dma,
            pltpu.VMEM((n_e, share, out), BF16),
            pltpu.VMEM((n_e, share, depth), BF16),
            pltpu.VMEM((n_e * share, width), F32),
            dma, dma, dma,
            dma((n_e,)), dma((n_e,)),
            dma((n_d, n_e)), dma((n_d, n_e)),
            dma((n_e,)), dma((n_e,)),
            dma((n_d,)), dma((n_d,)),
            dma((4,)),
        ],
        compiler_params=pltpu.CompilerParams(
            collective_id=0, has_side_effects=True, vmem_limit_bytes=48 * 1024 * 1024),
    )(trunk, gates, cot, first, second)


def return_kernel(n_e, d_pre, first, d_gate, d_trunk, gate_back, weights, part, near, pair, got,
                  w_sem, n_send, n_recv, p_send, p_recv, g_send, g_recv, own_sem):
    e = lax.axis_index("expert")
    core, seat, pairs = lax.rem(e, 2), e // 2, n_e // 2
    partner = e + 1 - 2 * core
    tiles, tile, _ = weights.shape

    def plane(s):
        return lax.rem(e + s, n_e)

    def remote(src, dst, send, recv, j):
        return pltpu.make_async_remote_copy(
            src_ref=src, dst_ref=dst, send_sem=send, recv_sem=recv,
            device_id={"expert": j}, device_id_type=MESH)

    def load(c):
        return pltpu.make_async_copy(first.at[c], weights.at[c], w_sem.at[c])

    for c in range(tiles):
        load(c).start()
    barrier = pltpu.get_barrier_semaphore()
    for s in range(1, n_e):
        pl.semaphore_signal(barrier, inc=1, device_id={"expert": plane(s)}, device_id_type=MESH)
    pl.semaphore_wait(barrier, n_e - 1)

    own = pltpu.make_async_copy(d_gate.at[e], gate_back.at[e], own_sem)
    own.start()

    def gate_out(s):
        j = plane(s)
        return remote(d_gate.at[j], gate_back.at[e], g_send.at[s], g_recv.at[e], j)

    def near_out(c):
        return remote(part.at[c, :, 1 - core], near.at[c], n_send.at[c], n_recv.at[c], partner)

    def part_out(c, s):
        k = lax.rem(seat + s, pairs)
        return remote(pair.at[c, k], got.at[c, seat], p_send.at[c, s], p_recv.at[c, seat],
                      2 * k + core)

    for s in range(1, n_e):
        gate_out(s).start()

    def compute(c):
        load(c).wait()
        value = lax.dot_general(
            d_pre[...], weights[c], (((1,), (1,)), ((), ())), preferred_element_type=F32)
        part[c] = value.astype(BF16).reshape(pairs, 2, -1, tile)

    def combine(c):
        near_out(c).wait_recv()
        pair[c] = (part[c, :, core].astype(F32) + near[c].astype(F32)).astype(BF16)

    def send(c):
        for s in range(1, pairs):
            part_out(c, s).start()

    compute(0)
    near_out(0).start()
    compute(1)
    combine(0)

    @pl.loop(2, tiles)
    def _(c):
        near_out(c - 1).start()
        send(c - 2)
        compute(c)
        combine(c - 1)

    near_out(tiles - 1).start()
    send(tiles - 2)
    combine(tiles - 1)
    send(tiles - 1)

    @pl.loop(0, tiles)
    def _(c):
        total = pair[c, seat].astype(F32)
        for s in range(1, pairs):
            k = lax.rem(seat + s, pairs)
            remote(pair.at[c, k], got.at[c, k], p_send.at[c, 0], p_recv.at[c, k],
                   2 * k + core).wait_recv()
            total = total + got[c, k].astype(F32)
        d_trunk[:, pl.ds(pl.multiple_of(c * tile, tile), tile)] = total.astype(BF16)

    own.wait()
    for s in range(1, n_e):
        j = plane(s)
        remote(d_gate.at[j], gate_back.at[j], g_send.at[0], g_recv.at[j], j).wait_recv()
    for s in range(1, n_e):
        gate_out(s).wait_send()

    @pl.loop(0, tiles)
    def _(c):
        near_out(c).wait_send()
        for s in range(1, pairs):
            part_out(c, s).wait_send()


def return_all(d_pre, first, d_gate):
    n_e = lax.axis_size("expert")
    tile = 512
    depth, width = first.shape
    tiles = depth // tile
    share = d_pre.shape[0] // n_e
    hbm = pl.BlockSpec(memory_space=pltpu.HBM)
    vmem = pl.BlockSpec(memory_space=pltpu.VMEM)
    dma = pltpu.SemaphoreType.DMA
    return pl.pallas_call(
        functools.partial(return_kernel, n_e),
        out_shape=(
            jax.ShapeDtypeStruct((share, depth), BF16),
            jax.ShapeDtypeStruct(d_gate.shape, F32),
        ),
        in_specs=[vmem, hbm, vmem],
        out_specs=(vmem, vmem),
        scratch_shapes=[
            pltpu.VMEM((tiles, tile, width), BF16),
            pltpu.VMEM((tiles, n_e // 2, 2, share, tile), BF16),
            pltpu.VMEM((tiles, n_e // 2, share, tile), BF16),
            pltpu.VMEM((tiles, n_e // 2, share, tile), BF16),
            pltpu.VMEM((tiles, n_e // 2, share, tile), BF16),
            dma((tiles,)), dma((tiles,)), dma((tiles,)),
            dma((tiles, n_e // 2)), dma((tiles, n_e // 2)),
            dma((n_e,)), dma((n_e,)), dma,
        ],
        compiler_params=pltpu.CompilerParams(
            collective_id=1, has_side_effects=True, vmem_limit_bytes=48 * 1024 * 1024),
    )(d_pre, first.reshape(tiles, tile, width), d_gate)


def on_device(trunk, w_first, w_second, gates, d_mixed):
    rank = lax.axis_index("dp")
    first = w_first[0]
    second = w_second[0]
    gate_here = gates[0]
    n_dp = lax.axis_size("dp")
    depth = first.shape[0] // n_dp
    units = second.shape[0] // n_dp
    group = gate_here.shape[1]

    n_e = lax.axis_size("expert")
    gate_parts = gate_here.T.astype(F32).reshape(n_e, -1, gate_here.shape[0])
    rows_all, d_output_all, pre, gates_each, outs_each = gather_all(
        trunk, gate_parts, jnp.transpose(d_mixed, (1, 0, 2)), first, second)
    rows_all = rows_all.reshape(-1, trunk.shape[1])
    d_output_all = d_output_all.reshape(-1, second.shape[1])
    pre = pre.reshape(-1, first.shape[1])
    gates_each = gates_each.astype(BF16)
    d_hidden = lax.dot_general(
        d_output_all, second, (((1,), (1,)), ((), ())), preferred_element_type=F32
    )
    sig = jax.nn.sigmoid(pre)
    d_pre = (d_hidden * sig * (1.0 + pre * (1.0 - sig))).astype(BF16)
    d_pre_here = lax.dynamic_slice_in_dim(d_pre, rank * group, group, 0)
    mixed = jnp.einsum(
        "ert,ero->rto", gates_each, outs_each, preferred_element_type=F32
    ).astype(BF16)
    d_gate_each = jnp.einsum(
        "rto,ero->ert", d_mixed, outs_each, preferred_element_type=F32
    ).astype(BF16)
    d_trunk, back_gate = return_all(d_pre_here, first, d_gate_each.astype(F32))
    d_gate = back_gate.reshape(group, -1).T.astype(BF16)[None]

    columns = lax.dynamic_slice_in_dim(rows_all, rank * depth, depth, 1)
    d_first = lax.dot_general(
        columns, d_pre, (((0,), (0,)), ((), ())), preferred_element_type=F32
    ).astype(BF16)
    some_pre = lax.dynamic_slice_in_dim(pre, rank * units, units, 1)
    some_hidden = jax.nn.silu(some_pre).astype(BF16)
    d_second = lax.dot_general(
        some_hidden, d_output_all, (((0,), (0,)), ((), ())), preferred_element_type=F32
    ).astype(BF16)
    return (mixed, d_trunk, d_gate, d_first[None], d_second[None])


SIDE, LINE, LANES = 2, 4, 128


def tiled(count, body, hooks=()):
    @pl.loop(0, count)
    def _(c):
        body(c)
        for at, hook in hooks:
            pl.when(c == at)(hook)


def step_kernel(n_e, n_d, trunk, gates, cot_in, first, second,
                rows, d_out, d_pre, some_hidden, mixed, d_trunk, gate_back,
                weights, later, cot, gate_each, mix, piece, tall, hidden, made, outs, d_gate,
                part, near, pair, got,
                load_sem, own_sem, g_send, g_recv, t_send, t_recv, o_send, o_recv, z_send, z_recv,
                m_send, m_recv, n_send, n_recv, p_send, p_recv, b_send, b_recv):
    e = lax.axis_index("expert")
    z = lax.axis_index("dp")
    core, seat, pairs = lax.rem(e, 2), e // 2, n_e // 2
    partner = e + 1 - 2 * core
    side, up = lax.rem(seat, SIDE), seat // SIDE
    across = e + 2 - 4 * side
    over = e + 2 * SIDE - 4 * SIDE * up
    corner = across + over - e
    bridge = across * (1 - core) + over * core
    other = across * core + over * (1 - core)
    middle = (z * (n_d - 1 - z)) // 2
    inner = middle == 1
    mate = z + 1 - 2 * lax.rem(z, 2)
    mirror = n_d - 1 - z
    skip = lax.rem(z + 2, n_d)
    order = [z, mate, middle * mirror + (1 - middle) * skip, middle * skip + (1 - middle) * mirror]
    tasks = cot.shape[0] // rows.shape[2]
    share, depth = rows.shape[2], rows.shape[3]
    width = tall.shape[2]
    group = n_e * share
    units = some_hidden.shape[2]

    def plane(s):
        return lax.rem(e + s, n_e)

    def remote(src, dst, send, recv, where):
        return pltpu.make_async_remote_copy(
            src_ref=src, dst_ref=dst, send_sem=send, recv_sem=recv,
            device_id=where, device_id_type=MESH)

    def load(k):
        src, dst = [(second, later), (cot_in, cot), (first, weights)][k]
        return pltpu.make_async_copy(src, dst, load_sem.at[k])

    def own(k):
        src, dst = [(gates.at[e], gate_each.at[e]), (trunk, rows.at[z, e]),
                    (piece.at[e], d_out.at[z, e]), (made.at[e], outs.at[e]),
                    (d_gate.at[e], gate_back.at[e])][k]
        return pltpu.make_async_copy(src, dst, own_sem.at[k])

    def at_plane(j):
        return {"expert": j}

    def gate_out(s):
        j = plane(s)
        return remote(gates.at[j], gate_each.at[e], g_send.at[s], g_recv.at[e], at_plane(j))

    def trunk_out(g, k):
        zi = order[g]
        j, where = [
            (e, at_plane(across)), (e, at_plane(over)), (e, at_plane(partner)),
            (bridge, at_plane(over * (1 - core) + across * core)),
            (bridge, at_plane(partner)), (other, at_plane(partner)), (corner, at_plane(partner)),
            (e, {"dp": mate}), (e, {"dp": mirror})][k]
        src = trunk if g == 0 and k in (0, 1, 2, 7, 8) else rows.at[zi, j]
        return remote(src, rows.at[zi, j], t_send.at[g, k], t_recv.at[zi, j], where)

    def trunk_in(g, j):
        zi = order[g]
        remote(trunk, rows.at[zi, j], t_send.at[0, 0], t_recv.at[zi, j],
               at_plane(partner)).wait_recv()

    def piece_out(s):
        j = plane(s)
        return remote(piece.at[j], d_out.at[z, e], o_send.at[s], o_recv.at[e], at_plane(j))

    def line_out(g, k):
        zi = order[g]
        return remote(d_out.at[zi], d_out.at[zi], z_send.at[g, k], z_recv.at[zi],
                      {"dp": mate if k == 0 else mirror})

    def made_out(s):
        j = plane(s)
        return remote(made.at[j], outs.at[e], m_send.at[s], m_recv.at[e], at_plane(j))

    def back_out(s):
        j = plane(s)
        return remote(d_gate.at[j], gate_back.at[e], b_send.at[s], b_recv.at[e], at_plane(j))

    def near_out(c):
        return remote(part.at[c, :, 1 - core], near.at[c], n_send.at[c], n_recv.at[c],
                      at_plane(partner))

    def part_out(c, s):
        k = lax.rem(seat + s, pairs)
        return remote(pair.at[c, k], got.at[c, seat], p_send.at[c, s], p_recv.at[c, seat],
                      at_plane(2 * k + core))

    def spread(g):
        for k in range(3):
            trunk_out(g, k).start()

    def bridge_on(g):
        trunk_in(g, bridge)
        trunk_out(g, 3).start()
        trunk_out(g, 4).start()
        trunk_in(g, other)
        trunk_out(g, 5).start()

    def corner_on(g):
        trunk_in(g, corner)
        trunk_out(g, 6).start()

    def complete(g):
        for shift in (0, across - e, over - e, corner - e):
            trunk_in(g, partner + shift)

    def arrive(g):
        trunk_in(g, e)
        if g == 1:
            pl.when(inner)(lambda: trunk_out(1, 8).start())
        else:
            pl.when(inner)(lambda: trunk_out(g, 7).start())

    def line_in(g):
        zi = order[g]
        remote(d_out.at[zi], d_out.at[zi], z_send.at[0, 0], z_recv.at[zi],
               {"dp": mate}).wait_recv()

    def line_arrive(g):
        line_in(g)
        pl.when(inner)(lambda: line_out(g, 1 if g == 1 else 0).start())

    def in_middle(call, g):
        pl.when(inner)(lambda: call(g))

    def at_end(call, g):
        pl.when(middle == 0)(lambda: call(g))

    for k in range(3):
        load(k).start()
    barrier = pltpu.get_barrier_semaphore()
    for s in range(1, n_e):
        pl.semaphore_signal(barrier, inc=1, device_id=at_plane(plane(s)), device_id_type=MESH)
    for i in range(1, n_d):
        pl.semaphore_signal(barrier, inc=1, device_id={"dp": lax.rem(z + i, n_d)},
                            device_id_type=MESH)
    pl.semaphore_wait(barrier, n_e - 1 + n_d - 1)

    for s in range(1, n_e):
        gate_out(s).start()
    own(0).start()
    own(1).start()
    trunk_out(0, 7).start()
    pl.when(inner)(lambda: trunk_out(0, 8).start())
    spread(0)

    def task_of():
        shape = (LANES, share * tasks)
        return jnp.where(
            lax.broadcasted_iota(jnp.int32, shape, 0)
            == lax.rem(lax.broadcasted_iota(jnp.int32, shape, 1), tasks), 1.0, 0.0).astype(BF16)

    def same_sample():
        shape = (n_e, share, share * tasks)
        match = (lax.broadcasted_iota(jnp.int32, shape, 1)
                 == lax.div(lax.broadcasted_iota(jnp.int32, shape, 2), tasks))
        return jnp.where(match, 1.0, 0.0).reshape(group, share * tasks)

    for s in range(1, n_e):
        j = plane(s)
        remote(gates.at[j], gate_each.at[j], g_send.at[0], g_recv.at[j],
               at_plane(j)).wait_recv()
    own(0).wait()
    load(1).wait()
    each = gate_each[...].reshape(group, LANES).astype(BF16)
    mix[...] = (jnp.dot(each, task_of(), preferred_element_type=F32)
                * same_sample()).astype(BF16)
    piece[...] = jnp.dot(mix[...], cot[...], preferred_element_type=F32).astype(BF16).reshape(
        piece.shape)
    for s in range(1, n_e):
        piece_out(s).start()
    own(2).start()

    bridge_on(0)
    arrive(1)
    in_middle(arrive, 2)
    for s in range(1, n_e):
        j = plane(s)
        remote(piece.at[j], d_out.at[z, j], o_send.at[0], o_recv.at[j], at_plane(j)).wait_recv()
    own(2).wait()
    line_out(0, 0).start()
    pl.when(inner)(lambda: line_out(0, 1).start())
    spread(1)

    tile = 512

    def part_of(c):
        return pl.ds(pl.multiple_of(c * tile, tile), tile)

    def back_hidden(g, c):
        left = d_out[order[g]].reshape(group, d_out.shape[3])
        return lax.dot_general(left, later[part_of(c), :], (((1,), (1,)), ((), ())),
                               preferred_element_type=F32)

    def forward_pre(g, c):
        left = rows[order[g]].reshape(group, depth)
        return jnp.dot(left, weights[:, part_of(c)], preferred_element_type=F32)

    def store_d_pre(g, c, d_hidden, value):
        sig = jax.nn.sigmoid(value)
        d_pre[order[g], :, part_of(c)] = (
            d_hidden * sig * (1.0 + value * (1.0 - sig))).astype(BF16)
        return sig

    def first_hidden(c):
        tall[0, :, part_of(c)] = back_hidden(0, c)

    def first_pre(c):
        value = forward_pre(0, c)
        sig = store_d_pre(0, c, tall[0, :, part_of(c)], value)
        hidden[:, part_of(c)] = (value * sig).astype(BF16)

    def later_pre(g):
        def body(c):
            tall[g, :, part_of(c)] = forward_pre(g, c)
        return body

    def later_hidden(g):
        def body(c):
            store_d_pre(g, c, back_hidden(g, c), tall[g, :, part_of(c)])
        return body

    units_here = pl.ds(pl.multiple_of(z * units, units), units)

    def keep_units(g):
        value = tall[g, :, units_here]
        some_hidden[order[g]] = (value * jax.nn.sigmoid(value)).astype(BF16)

    load(0).wait()
    tiled(width // tile, first_hidden)
    corner_on(0)
    own(1).wait()
    complete(0)
    load(2).wait()

    def hook_a():
        in_middle(arrive, 3)
        at_end(arrive, 2)
        spread(2)

    tiled(width // tile, first_pre, [(1, hook_a)])
    some_hidden[z] = hidden[:, units_here]
    bridge_on(1)

    def first_output(c):
        value = jnp.dot(hidden[...], later[:, part_of(c)], preferred_element_type=F32)
        made[:, :, part_of(c)] = value.astype(BF16).reshape(n_e, share, tile)

    tiled(made.shape[2] // tile, first_output)
    own(3).start()
    for s in range(1, n_e):
        made_out(s).start()

    def compute(c):
        value = lax.dot_general(d_pre[z], weights[part_of(c), :], (((1,), (1,)), ((), ())),
                                preferred_element_type=F32)
        part[c] = value.astype(BF16).reshape(pairs, 2, share, tile)

    def combine(c):
        near_out(c).wait_recv()
        pair[c] = (part[c, :, core].astype(F32) + near[c].astype(F32)).astype(BF16)

    def send(c):
        for s in range(1, pairs):
            part_out(c, s).start()

    count = depth // tile
    compute(0)
    near_out(0).start()
    compute(1)
    combine(0)
    corner_on(1)

    def hook_b():
        line_arrive(1)
        in_middle(line_arrive, 2)

    def hook_c():
        at_end(arrive, 3)
        spread(3)

    def middle_tile(c):
        near_out(c - 1).start()
        send(c - 2)
        compute(c)
        combine(c - 1)

    hooks = [(2, hook_b), (3, lambda: bridge_on(2)), (4, hook_c)]

    @pl.loop(2, count)
    def _(c):
        middle_tile(c)
        for at, hook in hooks:
            pl.when(c == at)(hook)

    near_out(count - 1).start()
    send(count - 2)
    combine(count - 1)
    send(count - 1)
    complete(1)
    tiled(width // tile, later_pre(1), [(1, lambda: corner_on(2))])

    def hook_d():
        in_middle(line_arrive, 3)
        at_end(line_arrive, 2)

    tiled(width // tile, later_hidden(1), [(1, lambda: bridge_on(3))])
    keep_units(1)
    complete(2)
    tiled(width // tile, later_pre(2), [(1, hook_d), (2, lambda: corner_on(3))])
    keep_units(2)
    tiled(width // tile, later_hidden(2))
    complete(3)
    tiled(width // tile, later_pre(3))
    keep_units(3)

    own(3).wait()
    for s in range(1, n_e):
        j = plane(s)
        remote(made.at[j], outs.at[j], m_send.at[0], m_recv.at[j], at_plane(j)).wait_recv()
    each_out = outs[...].reshape(group, outs.shape[2])
    product = lax.dot_general(each_out, cot[...], (((1,), (1,)), ((), ())),
                              preferred_element_type=F32)
    product = (product * same_sample()).astype(BF16)
    d_gate[...] = lax.dot_general(product, task_of(), (((1,), (1,)), ((), ())),
                                  preferred_element_type=F32).reshape(d_gate.shape)
    own(4).start()
    for s in range(1, n_e):
        back_out(s).start()
    mixed[...] = lax.dot_general(mix[...], each_out, (((0,), (0,)), ((), ())),
                                 preferred_element_type=F32).astype(BF16)

    @pl.loop(0, count)
    def _(c):
        total = pair[c, seat].astype(F32)
        for s in range(1, pairs):
            k = lax.rem(seat + s, pairs)
            remote(pair.at[c, k], got.at[c, k], p_send.at[c, 0], p_recv.at[c, k],
                   at_plane(2 * k + core)).wait_recv()
            total = total + got[c, k].astype(F32)
        d_trunk[:, part_of(c)] = total.astype(BF16)

    at_end(line_arrive, 3)
    tiled(width // tile, later_hidden(3))

    own(4).wait()
    for s in range(1, n_e):
        j = plane(s)
        remote(d_gate.at[j], gate_back.at[j], b_send.at[0], b_recv.at[j], at_plane(j)).wait_recv()
    for s in range(1, n_e):
        gate_out(s).wait_send()
        piece_out(s).wait_send()
        made_out(s).wait_send()
        back_out(s).wait_send()
    for g in range(n_d):
        for k in range(7):
            trunk_out(g, k).wait_send()
    trunk_out(0, 7).wait_send()
    line_out(0, 0).wait_send()

    @pl.when(inner)
    def _():
        trunk_out(0, 8).wait_send()
        line_out(0, 1).wait_send()
        trunk_out(1, 8).wait_send()
        line_out(1, 1).wait_send()
        for g in range(2, n_d):
            trunk_out(g, 7).wait_send()
            line_out(g, 0).wait_send()

    @pl.loop(0, count)
    def _(c):
        near_out(c).wait_send()
        for s in range(1, pairs):
            part_out(c, s).wait_send()


def step_all(trunk, gates, cot, first, second):
    n_e, n_d = lax.axis_size("expert"), lax.axis_size("dp")
    share, depth = trunk.shape
    width = first.shape[1]
    out = second.shape[1]
    group = n_e * share
    count, pairs, tile = depth // 512, n_e // 2, 512
    anywhere = pl.BlockSpec(memory_space=pl.ANY)
    hbm = pl.BlockSpec(memory_space=pltpu.HBM)
    vmem = pl.BlockSpec(memory_space=pltpu.VMEM)
    dma = pltpu.SemaphoreType.DMA
    return pl.pallas_call(
        functools.partial(step_kernel, n_e, n_d),
        out_shape=(
            jax.ShapeDtypeStruct((n_d, n_e, share, depth), BF16),
            jax.ShapeDtypeStruct((n_d, n_e, share, out), BF16),
            jax.ShapeDtypeStruct((n_d, group, width), BF16),
            jax.ShapeDtypeStruct((n_d, group, width // n_d), BF16),
            jax.ShapeDtypeStruct((cot.shape[0], out), BF16),
            jax.ShapeDtypeStruct((share, depth), BF16),
            jax.ShapeDtypeStruct(gates.shape, F32),
        ),
        in_specs=[hbm, vmem, hbm, hbm, hbm],
        out_specs=(vmem,) * 7,
        scratch_shapes=[
            pltpu.VMEM(first.shape, BF16),
            pltpu.VMEM(second.shape, BF16),
            pltpu.VMEM(cot.shape, BF16),
            pltpu.VMEM(gates.shape, F32),
            pltpu.VMEM((group, cot.shape[0]), BF16),
            pltpu.VMEM((n_e, share, out), BF16),
            pltpu.VMEM((n_d, group, width), F32),
            pltpu.VMEM((group, width), BF16),
            pltpu.VMEM((n_e, share, out), BF16),
            pltpu.VMEM((n_e, share, out), BF16),
            pltpu.VMEM(gates.shape, F32),
            pltpu.VMEM((count, pairs, 2, share, tile), BF16),
            pltpu.VMEM((count, pairs, share, tile), BF16),
            pltpu.VMEM((count, pairs, share, tile), BF16),
            pltpu.VMEM((count, pairs, share, tile), BF16),
            dma((3,)), dma((5,)),
            dma((n_e,)), dma((n_e,)),
            dma((n_d, 9)), dma((n_d, n_e)),
            dma((n_e,)), dma((n_e,)),
            dma((n_d, 2)), dma((n_d,)),
            dma((n_e,)), dma((n_e,)),
            dma((count,)), dma((count,)),
            dma((count, pairs)), dma((count, pairs)),
            dma((n_e,)), dma((n_e,)),
        ],
        compiler_params=pltpu.CompilerParams(
            collective_id=2, has_side_effects=True, vmem_limit_bytes=48 * 1024 * 1024),
    )(trunk, gates, cot, first, second)


def on_square(trunk, w_first, w_second, gates, d_mixed):
    rank = lax.axis_index("dp")
    n_e, n_d = lax.axis_size("expert"), lax.axis_size("dp")
    first, second, gate_here = w_first[0], w_second[0], gates[0]
    tasks, group = gate_here.shape
    share = group // n_e
    depth = first.shape[0] // n_d
    gate_parts = jnp.pad(gate_here.T.astype(F32).reshape(n_e, share, tasks),
                         ((0, 0), (0, 0), (0, LANES - tasks)))
    rows, d_out, d_pre, some_hidden, mixed, d_trunk, back = step_all(
        trunk, gate_parts, d_mixed.reshape(share * tasks, -1), first, second)
    d_gate = back[:, :, :tasks].reshape(group, tasks).T.astype(BF16)[None]
    columns = lax.dynamic_slice_in_dim(rows.reshape(-1, first.shape[0]), rank * depth, depth, 1)
    d_first = lax.dot_general(
        columns, d_pre.reshape(-1, first.shape[1]), (((0,), (0,)), ((), ())),
        preferred_element_type=F32).astype(BF16)
    d_second = lax.dot_general(
        some_hidden.reshape(-1, some_hidden.shape[2]), d_out.reshape(-1, second.shape[1]),
        (((0,), (0,)), ((), ())), preferred_element_type=F32).astype(BF16)
    return (mixed.reshape(d_mixed.shape), d_trunk, d_gate, d_first[None], d_second[None])


def solution(mesh):
    in_specs = (
        P(("dp", "expert"), None),
        P("expert", None, None),
        P("expert", None, None),
        P("expert", None, "dp"),
        P(("dp", "expert"), None, None),
    )
    out_specs = (
        P(("dp", "expert"), None, None),
        P(("dp", "expert"), None),
        P("expert", None, "dp"),
        P("expert", "dp", None),
        P("expert", "dp", None),
    )
    fits = mesh.shape["expert"] == 2 * SIDE * SIDE and mesh.shape["dp"] == LINE
    return jax.shard_map(
        on_square if fits else on_device, mesh=mesh, in_specs=in_specs, out_specs=out_specs, check_vma=False
    )
```

```python
import functools

import jax
import jax.numpy as jnp
from jax import lax
from jax.experimental import pallas as pl
from jax.experimental.pallas import tpu as pltpu
from jax.sharding import PartitionSpec as P

F32 = jnp.float32
BF16 = jnp.bfloat16


MESH = pl.DeviceIdType.MESH


def gather_kernel(n_e, n_d, trunk, gates, cot, first, second, rows, d_out, pre, gate_each,
                  outs, weights, later, hidden, made, m_send, m_recv, later_sem, piece, block, tall, w_sem, load_sem, store_sem,
                  g_send, g_recv, t_send, t_recv, o_send, o_recv, z_send, z_recv,
                  own_sem):
    e = lax.axis_index("expert")
    z = lax.axis_index("dp")
    partner = e + 1 - 2 * lax.rem(e, 2)
    pairs = n_e // 2

    def plane(s):
        return lax.rem(e + s, n_e)

    def along(i):
        return lax.rem(z + i, n_d)

    def remote(src, dst, send, recv, where):
        return pltpu.make_async_remote_copy(
            src_ref=src, dst_ref=dst, send_sem=send, recv_sem=recv,
            device_id=where, device_id_type=MESH)

    load_weights = pltpu.make_async_copy(first, weights, w_sem)
    load_weights.start()
    load_later = pltpu.make_async_copy(second, later, later_sem)
    load_later.start()

    barrier = pltpu.get_barrier_semaphore()
    for s in range(1, n_e):
        pl.semaphore_signal(barrier, inc=1, device_id={"expert": plane(s)}, device_id_type=MESH)
    for i in range(1, n_d):
        pl.semaphore_signal(barrier, inc=1, device_id={"dp": along(i)}, device_id_type=MESH)
    pl.semaphore_wait(barrier, n_e - 1 + n_d - 1)

    sent = []

    def go(copy):
        copy.start()
        sent.append(copy)

    for s in range(1, n_e):
        j = plane(s)
        go(remote(gates.at[j], gate_each.at[e], g_send.at[s], g_recv.at[e], {"expert": j}))
    own_gate = pltpu.make_async_copy(gates.at[e], gate_each.at[e], own_sem.at[0])
    own_gate.start()
    own_rows = pltpu.make_async_copy(trunk, rows.at[z, e], own_sem.at[1])
    own_rows.start()

    def spread(i):
        zi = along(i)
        src = trunk if i == 0 else rows.at[zi, e]
        for s in range(1, pairs):
            go(remote(src, rows.at[zi, e], t_send.at[i, s], t_recv.at[zi, e],
                      {"expert": plane(2 * s)}))
        go(remote(src, rows.at[zi, e], t_send.at[i, 0], t_recv.at[zi, e], {"expert": partner}))

    def arrived(zi, j):
        remote(trunk, rows.at[zi, j], t_send.at[0, 0], t_recv.at[zi, j],
               {"expert": partner}).wait_recv()

    for i in range(1, n_d):
        go(remote(trunk, rows.at[z, e], t_send.at[i, n_e - 1], t_recv.at[z, e], {"dp": along(i)}))
    spread(0)

    for s in range(1, n_e):
        j = plane(s)
        remote(gates.at[j], gate_each.at[j], g_send.at[0], g_recv.at[j], {"expert": j}).wait_recv()
    own_gate.wait()
    tasks = cot.shape[0]

    @pl.loop(0, n_e)
    def _(j):
        weight = gate_each[j]
        total = weight[:, 0:1] * cot[0].astype(F32)
        for t in range(1, tasks):
            total = total + weight[:, t:t + 1] * cot[t].astype(F32)
        piece[j] = total.astype(BF16)

    own_piece = pltpu.make_async_copy(piece.at[e], d_out.at[z, e], own_sem.at[2])
    own_piece.start()
    for s in range(1, n_e):
        j = plane(s)
        go(remote(piece.at[j], d_out.at[z, e], o_send.at[s], o_recv.at[e], {"expert": j}))

    def send_outputs():
        own_made.start()
        for s in range(1, n_e):
            j = plane(s)
            go(remote(made.at[j], outs.at[e], m_send.at[s], m_recv.at[e], {"expert": j}))

    own_made = pltpu.make_async_copy(made.at[e], outs.at[e], own_sem.at[3])
    stores = []
    for i in range(n_d):
        zi = along(i)
        if i + 1 < n_d:
            arrived(along(i + 1), e)
            spread(i + 1)
        if i == 1:
            send_outputs()
        if i == 0:
            for s in range(1, n_e):
                j = plane(s)
                remote(piece.at[j], d_out.at[z, j], o_send.at[0], o_recv.at[j],
                       {"expert": j}).wait_recv()
            own_piece.wait()
            for k in range(1, n_d):
                go(remote(d_out.at[z], d_out.at[z], z_send.at[k], z_recv.at[z], {"dp": along(k)}))
            own_rows.wait()
        for s in range(1, pairs):
            j = plane(2 * s)
            arrived(zi, j)
            go(remote(rows.at[zi, j], rows.at[zi, j], t_send.at[i, pairs - 1 + s],
                      t_recv.at[zi, j], {"expert": partner}))
        for s in range(pairs):
            arrived(zi, lax.rem(partner + 2 * s, n_e))
        load = pltpu.make_async_copy(rows.at[zi], block, load_sem)
        load.start()
        if i == 0:
            load_weights.wait()
        else:
            stores[-1].wait()
        load.wait()
        height = block.shape[0] * block.shape[1]
        tile = 256
        left = block[...].reshape(height, block.shape[2])

        @pl.loop(0, tall.shape[1] // tile)
        def _(c):
            here = pl.ds(pl.multiple_of(c * tile, tile), tile)
            value = jnp.dot(left, weights[:, here], preferred_element_type=F32)
            tall[:, here] = value
            if i == 0:
                hidden[:, here] = (value * jax.nn.sigmoid(value)).astype(BF16)

        store = pltpu.make_async_copy(tall, pre.at[zi], store_sem)
        store.start()
        stores.append(store)
        if i == 0:
            load_later.wait()

            @pl.loop(0, made.shape[2] // tile)
            def _(c):
                here = pl.ds(pl.multiple_of(c * tile, tile), tile)
                value = jnp.dot(hidden[...], later[:, here], preferred_element_type=F32)
                made[:, :, here] = value.astype(BF16).reshape(n_e, -1, tile)

    stores[-1].wait()
    if n_d == 1:
        send_outputs()
    own_made.wait()
    for s in range(1, n_e):
        j = plane(s)
        remote(made.at[j], outs.at[j], m_send.at[0], m_recv.at[j], {"expert": j}).wait_recv()
    for i in range(1, n_d):
        zi = along(i)
        remote(d_out.at[zi], d_out.at[zi], z_send.at[0], z_recv.at[zi], {"dp": zi}).wait_recv()
    for copy in sent:
        copy.wait_send()


def gather_all(trunk, gates, cot, first, second):
    n_e, n_d = lax.axis_size("expert"), lax.axis_size("dp")
    share, depth = trunk.shape
    width = first.shape[1]
    out = cot.shape[2]
    anywhere = pl.BlockSpec(memory_space=pl.ANY)
    hbm = pl.BlockSpec(memory_space=pltpu.HBM)
    vmem = pl.BlockSpec(memory_space=pltpu.VMEM)
    dma = pltpu.SemaphoreType.DMA
    return pl.pallas_call(
        functools.partial(gather_kernel, n_e, n_d),
        out_shape=(
            jax.ShapeDtypeStruct((n_d, n_e, share, depth), BF16),
            jax.ShapeDtypeStruct((n_d, n_e, share, out), BF16),
            jax.ShapeDtypeStruct((n_d, n_e * share, width), F32),
            jax.ShapeDtypeStruct(gates.shape, F32),
            jax.ShapeDtypeStruct((n_e, share, out), BF16),
        ),
        in_specs=[vmem, vmem, vmem, hbm, hbm],
        out_specs=(hbm, hbm, hbm, vmem, hbm),
        scratch_shapes=[
            pltpu.VMEM(first.shape, BF16),
            pltpu.VMEM(second.shape, BF16),
            pltpu.VMEM((n_e * share, width), BF16),
            pltpu.VMEM((n_e, share, out), BF16),
            dma((n_e,)), dma((n_e,)), dma,
            pltpu.VMEM((n_e, share, out), BF16),
            pltpu.VMEM((n_e, share, depth), BF16),
            pltpu.VMEM((n_e * share, width), F32),
            dma, dma, dma,
            dma((n_e,)), dma((n_e,)),
            dma((n_d, n_e)), dma((n_d, n_e)),
            dma((n_e,)), dma((n_e,)),
            dma((n_d,)), dma((n_d,)),
            dma((4,)),
        ],
        compiler_params=pltpu.CompilerParams(
            collective_id=0, has_side_effects=True, vmem_limit_bytes=48 * 1024 * 1024),
    )(trunk, gates, cot, first, second)


def return_kernel(n_e, d_pre, first, d_gate, d_trunk, gate_back, weights, part, near, pair, got,
                  w_sem, n_send, n_recv, p_send, p_recv, g_send, g_recv, own_sem):
    e = lax.axis_index("expert")
    core, seat, pairs = lax.rem(e, 2), e // 2, n_e // 2
    partner = e + 1 - 2 * core
    tiles, tile, _ = weights.shape

    def plane(s):
        return lax.rem(e + s, n_e)

    def remote(src, dst, send, recv, j):
        return pltpu.make_async_remote_copy(
            src_ref=src, dst_ref=dst, send_sem=send, recv_sem=recv,
            device_id={"expert": j}, device_id_type=MESH)

    def load(c):
        return pltpu.make_async_copy(first.at[c], weights.at[c], w_sem.at[c])

    for c in range(tiles):
        load(c).start()
    barrier = pltpu.get_barrier_semaphore()
    for s in range(1, n_e):
        pl.semaphore_signal(barrier, inc=1, device_id={"expert": plane(s)}, device_id_type=MESH)
    pl.semaphore_wait(barrier, n_e - 1)

    own = pltpu.make_async_copy(d_gate.at[e], gate_back.at[e], own_sem)
    own.start()

    def gate_out(s):
        j = plane(s)
        return remote(d_gate.at[j], gate_back.at[e], g_send.at[s], g_recv.at[e], j)

    def near_out(c):
        return remote(part.at[c, :, 1 - core], near.at[c], n_send.at[c], n_recv.at[c], partner)

    def part_out(c, s):
        k = lax.rem(seat + s, pairs)
        return remote(pair.at[c, k], got.at[c, seat], p_send.at[c, s], p_recv.at[c, seat],
                      2 * k + core)

    for s in range(1, n_e):
        gate_out(s).start()

    def compute(c):
        load(c).wait()
        value = lax.dot_general(
            d_pre[...], weights[c], (((1,), (1,)), ((), ())), preferred_element_type=F32)
        part[c] = value.astype(BF16).reshape(pairs, 2, -1, tile)

    def combine(c):
        near_out(c).wait_recv()
        pair[c] = (part[c, :, core].astype(F32) + near[c].astype(F32)).astype(BF16)

    def send(c):
        for s in range(1, pairs):
            part_out(c, s).start()

    compute(0)
    near_out(0).start()
    compute(1)
    combine(0)

    @pl.loop(2, tiles)
    def _(c):
        near_out(c - 1).start()
        send(c - 2)
        compute(c)
        combine(c - 1)

    near_out(tiles - 1).start()
    send(tiles - 2)
    combine(tiles - 1)
    send(tiles - 1)

    @pl.loop(0, tiles)
    def _(c):
        total = pair[c, seat].astype(F32)
        for s in range(1, pairs):
            k = lax.rem(seat + s, pairs)
            remote(pair.at[c, k], got.at[c, k], p_send.at[c, 0], p_recv.at[c, k],
                   2 * k + core).wait_recv()
            total = total + got[c, k].astype(F32)
        d_trunk[:, pl.ds(pl.multiple_of(c * tile, tile), tile)] = total.astype(BF16)

    own.wait()
    for s in range(1, n_e):
        j = plane(s)
        remote(d_gate.at[j], gate_back.at[j], g_send.at[0], g_recv.at[j], j).wait_recv()
    for s in range(1, n_e):
        gate_out(s).wait_send()

    @pl.loop(0, tiles)
    def _(c):
        near_out(c).wait_send()
        for s in range(1, pairs):
            part_out(c, s).wait_send()


def return_all(d_pre, first, d_gate):
    n_e = lax.axis_size("expert")
    tile = 512
    depth, width = first.shape
    tiles = depth // tile
    share = d_pre.shape[0] // n_e
    hbm = pl.BlockSpec(memory_space=pltpu.HBM)
    vmem = pl.BlockSpec(memory_space=pltpu.VMEM)
    dma = pltpu.SemaphoreType.DMA
    return pl.pallas_call(
        functools.partial(return_kernel, n_e),
        out_shape=(
            jax.ShapeDtypeStruct((share, depth), BF16),
            jax.ShapeDtypeStruct(d_gate.shape, F32),
        ),
        in_specs=[vmem, hbm, vmem],
        out_specs=(vmem, vmem),
        scratch_shapes=[
            pltpu.VMEM((tiles, tile, width), BF16),
            pltpu.VMEM((tiles, n_e // 2, 2, share, tile), BF16),
            pltpu.VMEM((tiles, n_e // 2, share, tile), BF16),
            pltpu.VMEM((tiles, n_e // 2, share, tile), BF16),
            pltpu.VMEM((tiles, n_e // 2, share, tile), BF16),
            dma((tiles,)), dma((tiles,)), dma((tiles,)),
            dma((tiles, n_e // 2)), dma((tiles, n_e // 2)),
            dma((n_e,)), dma((n_e,)), dma,
        ],
        compiler_params=pltpu.CompilerParams(
            collective_id=1, has_side_effects=True, vmem_limit_bytes=48 * 1024 * 1024),
    )(d_pre, first.reshape(tiles, tile, width), d_gate)


def on_device(trunk, w_first, w_second, gates, d_mixed):
    rank = lax.axis_index("dp")
    first = w_first[0]
    second = w_second[0]
    gate_here = gates[0]
    n_dp = lax.axis_size("dp")
    depth = first.shape[0] // n_dp
    units = second.shape[0] // n_dp
    group = gate_here.shape[1]

    n_e = lax.axis_size("expert")
    gate_parts = gate_here.T.astype(F32).reshape(n_e, -1, gate_here.shape[0])
    rows_all, d_output_all, pre, gates_each, outs_each = gather_all(
        trunk, gate_parts, jnp.transpose(d_mixed, (1, 0, 2)), first, second)
    rows_all = rows_all.reshape(-1, trunk.shape[1])
    d_output_all = d_output_all.reshape(-1, second.shape[1])
    pre = pre.reshape(-1, first.shape[1])
    gates_each = gates_each.astype(BF16)
    d_hidden = lax.dot_general(
        d_output_all, second, (((1,), (1,)), ((), ())), preferred_element_type=F32
    )
    sig = jax.nn.sigmoid(pre)
    d_pre = (d_hidden * sig * (1.0 + pre * (1.0 - sig))).astype(BF16)
    d_pre_here = lax.dynamic_slice_in_dim(d_pre, rank * group, group, 0)
    mixed = jnp.einsum(
        "ert,ero->rto", gates_each, outs_each, preferred_element_type=F32
    ).astype(BF16)
    d_gate_each = jnp.einsum(
        "rto,ero->ert", d_mixed, outs_each, preferred_element_type=F32
    ).astype(BF16)
    d_trunk, back_gate = return_all(d_pre_here, first, d_gate_each.astype(F32))
    d_gate = back_gate.reshape(group, -1).T.astype(BF16)[None]

    columns = lax.dynamic_slice_in_dim(rows_all, rank * depth, depth, 1)
    d_first = lax.dot_general(
        columns, d_pre, (((0,), (0,)), ((), ())), preferred_element_type=F32
    ).astype(BF16)
    some_pre = lax.dynamic_slice_in_dim(pre, rank * units, units, 1)
    some_hidden = jax.nn.silu(some_pre).astype(BF16)
    d_second = lax.dot_general(
        some_hidden, d_output_all, (((0,), (0,)), ((), ())), preferred_element_type=F32
    ).astype(BF16)
    return (mixed, d_trunk, d_gate, d_first[None], d_second[None])


SIDE, LINE, LANES = 2, 4, 128
VMEM_BYTES = 62 * 1024 * 1024


def tiled(count, body, hooks=()):
    @pl.loop(0, count)
    def _(c):
        body(c)
        for at, hook in hooks:
            pl.when(c == at)(hook)


def step_kernel(n_e, n_d, trunk, gates, cot_in, first, second,
                columns_out, d_out_out, d_pre_out, units_out, mixed_out, d_trunk_out, back_out_ref,
                rows, d_out, d_pre, some_hidden, mixed, d_trunk, gate_back, gate_in, gate_piece,
                weights, later, cot, gate_each, mix, piece, tall, hidden, made, outs, d_gate,
                part, near, pair, got,
                load_sem, own_sem, g_send, g_recv, t_send, t_recv, o_send, o_recv, z_send, z_recv,
                m_send, m_recv, n_send, n_recv, p_send, p_recv, b_send, b_recv, out_sem):
    e = lax.axis_index("expert")
    z = lax.axis_index("dp")
    core, seat, pairs = lax.rem(e, 2), e // 2, n_e // 2
    partner = e + 1 - 2 * core
    side, up = lax.rem(seat, SIDE), seat // SIDE
    across = e + 2 - 4 * side
    over = e + 2 * SIDE - 4 * SIDE * up
    corner = across + over - e
    bridge = across * (1 - core) + over * core
    other = across * core + over * (1 - core)
    middle = (z * (n_d - 1 - z)) // 2
    inner = middle == 1
    mate = z + 1 - 2 * lax.rem(z, 2)
    mirror = n_d - 1 - z
    skip = lax.rem(z + 2, n_d)
    order = [z, mate, middle * mirror + (1 - middle) * skip, middle * skip + (1 - middle) * mirror]
    tasks = cot.shape[0] // rows.shape[2]
    share, depth = rows.shape[2], rows.shape[3]
    width = tall.shape[2]
    group = n_e * share
    units = some_hidden.shape[2]
    part_depth = depth // n_d
    depth_here = pl.ds(pl.multiple_of(z * part_depth, part_depth), part_depth)

    def plane(s):
        return lax.rem(e + s, n_e)

    def remote(src, dst, send, recv, where):
        return pltpu.make_async_remote_copy(
            src_ref=src, dst_ref=dst, send_sem=send, recv_sem=recv,
            device_id=where, device_id_type=MESH)

    def load(k):
        src, dst = [(second, later), (cot_in, cot), (first, weights), (gates, gate_in)][k]
        return pltpu.make_async_copy(src, dst, load_sem.at[k])

    def own(k):
        src, dst = [(gate_piece.at[e], gate_each.at[e]), (trunk, rows.at[z, e]),
                    (piece.at[e], d_out.at[z, e]), (made.at[e], outs.at[e]),
                    (d_gate.at[e], gate_back.at[e])][k]
        return pltpu.make_async_copy(src, dst, own_sem.at[k])

    def at_plane(j):
        return {"expert": j}

    def gate_out(s):
        j = plane(s)
        return remote(gate_piece.at[j], gate_each.at[e], g_send.at[s], g_recv.at[e], at_plane(j))

    def trunk_out(g, k):
        zi = order[g]
        j, where = [
            (e, at_plane(across)), (e, at_plane(over)), (e, at_plane(partner)),
            (bridge, at_plane(over * (1 - core) + across * core)),
            (bridge, at_plane(partner)), (other, at_plane(partner)), (corner, at_plane(partner)),
            (e, {"dp": mate}), (e, {"dp": mirror})][k]
        src = trunk if g == 0 and k in (0, 1, 2, 7, 8) else rows.at[zi, j]
        return remote(src, rows.at[zi, j], t_send.at[g, k], t_recv.at[zi, j], where)

    def trunk_in(g, j):
        zi = order[g]
        remote(trunk, rows.at[zi, j], t_send.at[0, 0], t_recv.at[zi, j],
               at_plane(partner)).wait_recv()

    def piece_out(s):
        j = plane(s)
        return remote(piece.at[j], d_out.at[z, e], o_send.at[s], o_recv.at[e], at_plane(j))

    def half(zi, h):
        return d_out.at[zi, h * (n_e // 2):(h + 1) * (n_e // 2)]

    def line_out(g, k, h):
        zi = order[g]
        return remote(half(zi, h), half(zi, h), z_send.at[g, k, h], z_recv.at[zi, h],
                      {"dp": mate if k == 0 else mirror})

    def keep(k):
        src, dst = ([(rows.at[zi, :, :, depth_here], columns_out.at[zi]) for zi in order]
                    + [(d_pre.at[zi], d_pre_out.at[zi]) for zi in order]
                    + [(d_out, d_out_out), (some_hidden, units_out), (mixed, mixed_out),
                       (d_trunk, d_trunk_out), (gate_back, back_out_ref)])[k]
        return pltpu.make_async_copy(src, dst, out_sem.at[k])

    def made_out(s):
        j = plane(s)
        return remote(made.at[j], outs.at[e], m_send.at[s], m_recv.at[e], at_plane(j))

    def back_out(s):
        j = plane(s)
        return remote(d_gate.at[j], gate_back.at[e], b_send.at[s], b_recv.at[e], at_plane(j))

    def near_out(c):
        return remote(part.at[c, :, 1 - core], near.at[c], n_send.at[c], n_recv.at[c],
                      at_plane(partner))

    def part_out(c, s):
        k = lax.rem(seat + s, pairs)
        return remote(pair.at[c, k], got.at[c, seat], p_send.at[c, s], p_recv.at[c, seat],
                      at_plane(2 * k + core))

    def spread(g):
        for k in range(3):
            trunk_out(g, k).start()

    def bridge_on(g):
        trunk_in(g, bridge)
        trunk_out(g, 3).start()
        trunk_out(g, 4).start()
        trunk_in(g, other)
        trunk_out(g, 5).start()

    def corner_on(g):
        trunk_in(g, corner)
        trunk_out(g, 6).start()

    def complete(g):
        for shift in (0, across - e, over - e, corner - e):
            trunk_in(g, partner + shift)

    def arrive(g):
        trunk_in(g, e)
        if g == 1:
            pl.when(inner)(lambda: trunk_out(1, 8).start())
        else:
            pl.when(inner)(lambda: trunk_out(g, 7).start())

    def line_arrive(g, h):
        zi = order[g]
        remote(half(zi, h), half(zi, h), z_send.at[0, 0, h], z_recv.at[zi, h],
               {"dp": mate}).wait_recv()
        pl.when(inner)(lambda: line_out(g, 1 if g == 1 else 0, h).start())

    def in_middle(call, *g):
        pl.when(inner)(lambda: call(*g))

    def at_end(call, *g):
        pl.when(middle == 0)(lambda: call(*g))

    for k in (3, 1, 0, 2):
        load(k).start()
    barrier = pltpu.get_barrier_semaphore()
    for s in range(1, n_e):
        pl.semaphore_signal(barrier, inc=1, device_id=at_plane(plane(s)), device_id_type=MESH)
    for i in range(1, n_d):
        pl.semaphore_signal(barrier, inc=1, device_id={"dp": lax.rem(z + i, n_d)},
                            device_id_type=MESH)
    load(3).wait()
    task_eye = jnp.where(
        lax.broadcasted_iota(jnp.int32, (tasks, LANES), 0)
        == lax.broadcasted_iota(jnp.int32, (tasks, LANES), 1), 1.0, 0.0).astype(BF16)
    gate_piece[...] = lax.dot_general(
        gate_in[...], task_eye, (((0,), (0,)), ((), ())),
        preferred_element_type=F32).reshape(gate_piece.shape)
    own(0).start()
    own(1).start()
    pl.semaphore_wait(barrier, n_e - 1 + n_d - 1)

    for s in range(1, n_e):
        gate_out(s).start()
    trunk_out(0, 7).start()
    pl.when(inner)(lambda: trunk_out(0, 8).start())
    spread(0)

    def task_of():
        shape = (LANES, share * tasks)
        return jnp.where(
            lax.broadcasted_iota(jnp.int32, shape, 0)
            == lax.rem(lax.broadcasted_iota(jnp.int32, shape, 1), tasks), 1.0, 0.0).astype(BF16)

    def same_sample():
        shape = (n_e, share, share * tasks)
        match = (lax.broadcasted_iota(jnp.int32, shape, 1)
                 == lax.div(lax.broadcasted_iota(jnp.int32, shape, 2), tasks))
        return jnp.where(match, 1.0, 0.0).reshape(group, share * tasks)

    for s in range(1, n_e):
        j = plane(s)
        remote(gate_piece.at[j], gate_each.at[j], g_send.at[0], g_recv.at[j],
               at_plane(j)).wait_recv()
    own(0).wait()
    load(1).wait()
    each = gate_each[...].reshape(group, LANES).astype(BF16)
    mix[...] = (jnp.dot(each, task_of(), preferred_element_type=F32)
                * same_sample()).astype(BF16)
    piece[...] = jnp.dot(mix[...], cot[...], preferred_element_type=F32).astype(BF16).reshape(
        piece.shape)
    bridge_on(0)
    for s in range(1, n_e):
        piece_out(s).start()
    own(2).start()
    arrive(1)
    in_middle(arrive, 2)

    tile = 512

    def part_of(c):
        return pl.ds(pl.multiple_of(c * tile, tile), tile)

    def back_hidden(g, c):
        left = d_out[order[g]].reshape(group, d_out.shape[3])
        return lax.dot_general(left, later[part_of(c), :], (((1,), (1,)), ((), ())),
                               preferred_element_type=F32)

    def forward_pre(g, c):
        left = rows[order[g]].reshape(group, depth)
        return jnp.dot(left, weights[:, part_of(c)], preferred_element_type=F32)

    def store_d_pre(g, c, d_hidden, value):
        sig = jax.nn.sigmoid(value)
        d_pre[order[g], :, part_of(c)] = (
            d_hidden * sig * (1.0 + value * (1.0 - sig))).astype(BF16)

    def first_pre(c):
        value = forward_pre(0, c)
        tall[0, :, part_of(c)] = value
        hidden[:, part_of(c)] = (value * jax.nn.sigmoid(value)).astype(BF16)

    def later_pre(g):
        def body(c):
            tall[g, :, part_of(c)] = forward_pre(g, c)
        return body

    def later_hidden(g):
        def body(c):
            store_d_pre(g, c, back_hidden(g, c), tall[g, :, part_of(c)])
        return body

    units_here = pl.ds(pl.multiple_of(z * units, units), units)

    def keep_units(g):
        value = tall[g, :, units_here]
        some_hidden[order[g]] = (value * jax.nn.sigmoid(value)).astype(BF16)

    corner_on(0)
    own(1).wait()
    complete(0)
    load(2).wait()

    def hook_a():
        spread(1)

    def hook_b():
        for s in range(1, n_e):
            j = plane(s)
            remote(piece.at[j], d_out.at[z, j], o_send.at[0], o_recv.at[j],
                   at_plane(j)).wait_recv()
        own(2).wait()
        for h in range(2):
            line_out(0, 0, h).start()
            in_middle(lambda: line_out(0, 1, h).start())

    tiled(width // tile, first_pre, [(1, hook_a), (2, hook_b)])
    keep(0).start()
    in_middle(arrive, 3)
    at_end(arrive, 2)
    load(0).wait()

    def first_output(c):
        value = jnp.dot(hidden[...], later[:, part_of(c)], preferred_element_type=F32)
        made[:, :, part_of(c)] = value.astype(BF16).reshape(n_e, share, tile)

    tiled(made.shape[2] // tile, first_output)
    own(3).start()
    for s in range(1, n_e):
        made_out(s).start()
    spread(2)
    some_hidden[z] = hidden[:, units_here]
    tiled(width // tile, later_hidden(0))
    keep(4).start()

    def compute(c):
        value = lax.dot_general(d_pre[z], weights[part_of(c), :], (((1,), (1,)), ((), ())),
                                preferred_element_type=F32)
        part[c] = value.astype(BF16).reshape(pairs, 2, share, tile)

    def combine(c):
        near_out(c).wait_recv()
        pair[c] = (part[c, :, core].astype(F32) + near[c].astype(F32)).astype(BF16)

    def send(c):
        for s in range(1, pairs):
            part_out(c, s).start()

    count = depth // tile
    compute(0)
    near_out(0).start()
    compute(1)
    combine(0)
    bridge_on(1)

    def hook_c(h):
        def hook():
            line_arrive(1, h)
            in_middle(line_arrive, 2, h)
        return hook

    def hook_d():
        at_end(arrive, 3)
        spread(3)

    hooks = [(2, hook_c(0)), (5, hook_d), (6, hook_c(1)), (7, lambda: corner_on(1))]

    @pl.loop(2, count)
    def _(c):
        near_out(c - 1).start()
        send(c - 2)
        compute(c)
        combine(c - 1)
        for at, hook in hooks:
            pl.when(c == at)(hook)

    near_out(count - 1).start()
    send(count - 2)
    combine(count - 1)
    send(count - 1)
    complete(1)
    keep(1).start()
    tiled(width // tile, later_pre(1), [(0, lambda: bridge_on(2)),
                                        (2, lambda: in_middle(line_arrive, 3, 0)),
                                        (3, lambda: corner_on(2))])
    keep_units(1)
    tiled(width // tile, later_hidden(1), [(2, lambda: bridge_on(3)),
                                           (3, lambda: in_middle(line_arrive, 3, 1))])
    keep(5).start()
    complete(2)
    keep(2).start()
    tiled(width // tile, later_pre(2), [(2, lambda: corner_on(3))])
    keep_units(2)
    complete(3)
    keep(3).start()
    tiled(width // tile, later_pre(3))
    keep_units(3)
    keep(9).start()
    at_end(line_arrive, 2, 0)
    at_end(line_arrive, 2, 1)
    tiled(width // tile, later_hidden(2))
    keep(6).start()

    own(3).wait()
    for s in range(1, n_e):
        j = plane(s)
        remote(made.at[j], outs.at[j], m_send.at[0], m_recv.at[j], at_plane(j)).wait_recv()
    each_out = outs[...].reshape(group, outs.shape[2])
    product = lax.dot_general(each_out, cot[...], (((1,), (1,)), ((), ())),
                              preferred_element_type=F32)
    product = (product * same_sample()).astype(BF16)
    d_gate[...] = lax.dot_general(product, task_of(), (((1,), (1,)), ((), ())),
                                  preferred_element_type=F32).reshape(d_gate.shape)
    own(4).start()
    for s in range(1, n_e):
        back_out(s).start()
    mixed[...] = lax.dot_general(mix[...], each_out, (((0,), (0,)), ((), ())),
                                 preferred_element_type=F32).astype(BF16)

    @pl.loop(0, count)
    def _(c):
        total = pair[c, seat].astype(F32)
        for s in range(1, pairs):
            k = lax.rem(seat + s, pairs)
            remote(pair.at[c, k], got.at[c, k], p_send.at[c, 0], p_recv.at[c, k],
                   at_plane(2 * k + core)).wait_recv()
            total = total + got[c, k].astype(F32)
        d_trunk[:, part_of(c)] = total.astype(BF16)

    keep(10).start()
    keep(11).start()
    at_end(line_arrive, 3, 0)
    at_end(line_arrive, 3, 1)
    keep(8).start()
    tiled(width // tile, later_hidden(3))
    keep(7).start()

    own(4).wait()
    for s in range(1, n_e):
        j = plane(s)
        remote(d_gate.at[j], gate_back.at[j], b_send.at[0], b_recv.at[j], at_plane(j)).wait_recv()
    for s in range(1, n_e):
        gate_out(s).wait_send()
        piece_out(s).wait_send()
        made_out(s).wait_send()
        back_out(s).wait_send()
    for g in range(n_d):
        for k in range(7):
            trunk_out(g, k).wait_send()
    keep(12).start()
    trunk_out(0, 7).wait_send()
    for h in range(2):
        line_out(0, 0, h).wait_send()

    @pl.when(inner)
    def _():
        trunk_out(0, 8).wait_send()
        trunk_out(1, 8).wait_send()
        for g in range(2, n_d):
            trunk_out(g, 7).wait_send()
        for h in range(2):
            line_out(0, 1, h).wait_send()
            line_out(1, 1, h).wait_send()
            for g in range(2, n_d):
                line_out(g, 0, h).wait_send()

    @pl.loop(0, count)
    def _(c):
        near_out(c).wait_send()
        for s in range(1, pairs):
            part_out(c, s).wait_send()

    for k in range(13):
        keep(k).wait()


def step_all(trunk, gates, cot, first, second):
    n_e, n_d = lax.axis_size("expert"), lax.axis_size("dp")
    share, depth = trunk.shape
    width = first.shape[1]
    out = second.shape[1]
    group = n_e * share
    count, pairs, tile = depth // 512, n_e // 2, 512
    hbm = pl.BlockSpec(memory_space=pltpu.HBM)
    dma = pltpu.SemaphoreType.DMA
    gate_shape = (n_e, share, LANES)
    return pl.pallas_call(
        functools.partial(step_kernel, n_e, n_d),
        out_shape=(
            jax.ShapeDtypeStruct((n_d, n_e, share, depth // n_d), BF16),
            jax.ShapeDtypeStruct((n_d, n_e, share, out), BF16),
            jax.ShapeDtypeStruct((n_d, group, width), BF16),
            jax.ShapeDtypeStruct((n_d, group, width // n_d), BF16),
            jax.ShapeDtypeStruct((cot.shape[0], out), BF16),
            jax.ShapeDtypeStruct((share, depth), BF16),
            jax.ShapeDtypeStruct(gate_shape, F32),
        ),
        in_specs=[hbm] * 5,
        out_specs=(hbm,) * 7,
        scratch_shapes=[
            pltpu.VMEM((n_d, n_e, share, depth), BF16),
            pltpu.VMEM((n_d, n_e, share, out), BF16),
            pltpu.VMEM((n_d, group, width), BF16),
            pltpu.VMEM((n_d, group, width // n_d), BF16),
            pltpu.VMEM((cot.shape[0], out), BF16),
            pltpu.VMEM((share, depth), BF16),
            pltpu.VMEM(gate_shape, F32),
            pltpu.VMEM(gates.shape, BF16),
            pltpu.VMEM(gate_shape, F32),
            pltpu.VMEM(first.shape, BF16),
            pltpu.VMEM(second.shape, BF16),
            pltpu.VMEM(cot.shape, BF16),
            pltpu.VMEM(gate_shape, F32),
            pltpu.VMEM((group, cot.shape[0]), BF16),
            pltpu.VMEM((n_e, share, out), BF16),
            pltpu.VMEM((n_d, group, width), F32),
            pltpu.VMEM((group, width), BF16),
            pltpu.VMEM((n_e, share, out), BF16),
            pltpu.VMEM((n_e, share, out), BF16),
            pltpu.VMEM(gate_shape, F32),
            pltpu.VMEM((count, pairs, 2, share, tile), BF16),
            pltpu.VMEM((count, pairs, share, tile), BF16),
            pltpu.VMEM((count, pairs, share, tile), BF16),
            pltpu.VMEM((count, pairs, share, tile), BF16),
            dma((4,)), dma((5,)),
            dma((n_e,)), dma((n_e,)),
            dma((n_d, 9)), dma((n_d, n_e)),
            dma((n_e,)), dma((n_e,)),
            dma((n_d, 2, 2)), dma((n_d, 2)),
            dma((n_e,)), dma((n_e,)),
            dma((count,)), dma((count,)),
            dma((count, pairs)), dma((count, pairs)),
            dma((n_e,)), dma((n_e,)), dma((13,)),
        ],
        compiler_params=pltpu.CompilerParams(
            collective_id=2, has_side_effects=True, vmem_limit_bytes=VMEM_BYTES),
    )(trunk, gates, cot, first, second)


def finish_kernel(columns, d_pre, units, d_out, mixed, d_trunk, back,
                  d_first, d_second, mixed_out, d_trunk_out, d_gate,
                  columns_v, d_pre_v, units_v, d_out_v, mixed_v, d_trunk_v, back_v,
                  first_v, second_v, gate_v, in_sem, out_sem, tile_sem, wide_sem):
    pairs = [(units, units_v), (d_out, d_out_v), (columns, columns_v), (mixed, mixed_v),
             (d_trunk, d_trunk_v), (back, back_v)]
    steps = d_pre.shape[0]

    def take(k):
        return pltpu.make_async_copy(*pairs[k], in_sem.at[k])

    def wide(k):
        return pltpu.make_async_copy(d_pre.at[k], d_pre_v.at[k], wide_sem.at[k])

    def give(k):
        src, dst = [(second_v, d_second), (mixed_v, mixed_out), (d_trunk_v, d_trunk_out),
                    (gate_v, d_gate)][k]
        return pltpu.make_async_copy(src, dst, out_sem.at[k])

    for k in range(3):
        take(k).start()
    for k in range(steps):
        wide(k).start()
    for k in range(3, len(pairs)):
        take(k).start()
    take(0).wait()
    take(1).wait()
    second_v[...] = lax.dot_general(
        units_v[...], d_out_v[...], (((0,), (0,)), ((), ())),
        preferred_element_type=F32).astype(BF16)
    give(0).start()
    take(2).wait()
    for k in range(steps):
        wide(k).wait()
    tile = first_v.shape[1]
    count = first_v.shape[0]

    def store(c):
        here = pl.ds(pl.multiple_of(c * tile, tile), tile)
        return pltpu.make_async_copy(first_v.at[c], d_first.at[here], tile_sem.at[c])

    @pl.loop(0, count)
    def _(c):
        here = pl.ds(pl.multiple_of(c * tile, tile), tile)
        right = d_pre_v[...].reshape(-1, d_pre_v.shape[2])
        first_v[c] = lax.dot_general(
            columns_v[:, here], right, (((0,), (0,)), ((), ())),
            preferred_element_type=F32).astype(BF16)
        store(c).start()

        @pl.when(c == 0)
        def _():
            take(3).wait()
            give(1).start()
            take(4).wait()
            give(2).start()
            take(5).wait()
            tasks = d_gate.shape[0]
            eye = jnp.where(
                lax.broadcasted_iota(jnp.int32, (tasks, LANES), 0)
                == lax.broadcasted_iota(jnp.int32, (tasks, LANES), 1), 1.0, 0.0).astype(BF16)
            gate_v[...] = lax.dot_general(
                eye, back_v[...].astype(BF16), (((1,), (1,)), ((), ())),
                preferred_element_type=F32).astype(BF16)
            give(3).start()

    for k in range(4):
        give(k).wait()

    @pl.loop(0, count)
    def _(c):
        store(c).wait()


def finish_all(columns, d_pre, units, d_out, mixed, d_trunk, back, tasks):
    hbm = pl.BlockSpec(memory_space=pltpu.HBM)
    dma = pltpu.SemaphoreType.DMA
    rows, depth = columns.shape
    steps, group, width = d_pre.shape
    unit, out = units.shape[1], d_out.shape[1]
    tile = 256
    ins = (columns, d_pre, units, d_out, mixed, d_trunk, back)
    return pl.pallas_call(
        finish_kernel,
        out_shape=(
            jax.ShapeDtypeStruct((depth, width), BF16),
            jax.ShapeDtypeStruct((unit, out), BF16),
            jax.ShapeDtypeStruct(mixed.shape, BF16),
            jax.ShapeDtypeStruct(d_trunk.shape, BF16),
            jax.ShapeDtypeStruct((tasks, back.shape[0]), BF16),
        ),
        in_specs=[hbm] * 7,
        out_specs=(hbm,) * 5,
        scratch_shapes=[pltpu.VMEM(x.shape, x.dtype) for x in ins] + [
            pltpu.VMEM((depth // tile, tile, width), BF16),
            pltpu.VMEM((unit, out), BF16),
            pltpu.VMEM((tasks, back.shape[0]), BF16),
            dma((6,)), dma((4,)), dma((depth // tile,)), dma((steps,)),
        ],
        compiler_params=pltpu.CompilerParams(vmem_limit_bytes=VMEM_BYTES),
    )(*ins)


def on_square(trunk, w_first, w_second, gates, d_mixed):
    first, second, gate_here = w_first[0], w_second[0], gates[0]
    tasks, group = gate_here.shape
    columns, d_out, d_pre, units, mixed, d_trunk, back = step_all(
        trunk, gate_here, d_mixed.reshape(-1, d_mixed.shape[2]), first, second)
    d_first, d_second, mixed, d_trunk, d_gate = finish_all(
        columns.reshape(-1, columns.shape[3]), d_pre, units.reshape(-1, units.shape[2]),
        d_out.reshape(-1, d_out.shape[3]), mixed, d_trunk, back.reshape(group, -1), tasks)
    return (mixed.reshape(d_mixed.shape), d_trunk, d_gate[None], d_first[None], d_second[None])


def solution(mesh):
    in_specs = (
        P(("dp", "expert"), None),
        P("expert", None, None),
        P("expert", None, None),
        P("expert", None, "dp"),
        P(("dp", "expert"), None, None),
    )
    out_specs = (
        P(("dp", "expert"), None, None),
        P(("dp", "expert"), None),
        P("expert", None, "dp"),
        P("expert", "dp", None),
        P("expert", "dp", None),
    )
    fits = mesh.shape["expert"] == 2 * SIDE * SIDE and mesh.shape["dp"] == LINE
    return jax.shard_map(
        on_square if fits else on_device, mesh=mesh, in_specs=in_specs, out_specs=out_specs, check_vma=False
    )
```

```python
import functools

import jax
import jax.numpy as jnp
from jax import lax
from jax.experimental import pallas as pl
from jax.experimental.pallas import tpu as pltpu
from jax.sharding import PartitionSpec as P

F32 = jnp.float32
BF16 = jnp.bfloat16


MESH = pl.DeviceIdType.MESH


def gather_kernel(n_e, n_d, trunk, gates, cot, first, second, rows, d_out, pre, gate_each,
                  outs, weights, later, hidden, made, m_send, m_recv, later_sem, piece, block, tall, w_sem, load_sem, store_sem,
                  g_send, g_recv, t_send, t_recv, o_send, o_recv, z_send, z_recv,
                  own_sem):
    e = lax.axis_index("expert")
    z = lax.axis_index("dp")
    partner = e + 1 - 2 * lax.rem(e, 2)
    pairs = n_e // 2

    def plane(s):
        return lax.rem(e + s, n_e)

    def along(i):
        return lax.rem(z + i, n_d)

    def remote(src, dst, send, recv, where):
        return pltpu.make_async_remote_copy(
            src_ref=src, dst_ref=dst, send_sem=send, recv_sem=recv,
            device_id=where, device_id_type=MESH)

    load_weights = pltpu.make_async_copy(first, weights, w_sem)
    load_weights.start()
    load_later = pltpu.make_async_copy(second, later, later_sem)
    load_later.start()

    barrier = pltpu.get_barrier_semaphore()
    for s in range(1, n_e):
        pl.semaphore_signal(barrier, inc=1, device_id={"expert": plane(s)}, device_id_type=MESH)
    for i in range(1, n_d):
        pl.semaphore_signal(barrier, inc=1, device_id={"dp": along(i)}, device_id_type=MESH)
    pl.semaphore_wait(barrier, n_e - 1 + n_d - 1)

    sent = []

    def go(copy):
        copy.start()
        sent.append(copy)

    for s in range(1, n_e):
        j = plane(s)
        go(remote(gates.at[j], gate_each.at[e], g_send.at[s], g_recv.at[e], {"expert": j}))
    own_gate = pltpu.make_async_copy(gates.at[e], gate_each.at[e], own_sem.at[0])
    own_gate.start()
    own_rows = pltpu.make_async_copy(trunk, rows.at[z, e], own_sem.at[1])
    own_rows.start()

    def spread(i):
        zi = along(i)
        src = trunk if i == 0 else rows.at[zi, e]
        for s in range(1, pairs):
            go(remote(src, rows.at[zi, e], t_send.at[i, s], t_recv.at[zi, e],
                      {"expert": plane(2 * s)}))
        go(remote(src, rows.at[zi, e], t_send.at[i, 0], t_recv.at[zi, e], {"expert": partner}))

    def arrived(zi, j):
        remote(trunk, rows.at[zi, j], t_send.at[0, 0], t_recv.at[zi, j],
               {"expert": partner}).wait_recv()

    for i in range(1, n_d):
        go(remote(trunk, rows.at[z, e], t_send.at[i, n_e - 1], t_recv.at[z, e], {"dp": along(i)}))
    spread(0)

    for s in range(1, n_e):
        j = plane(s)
        remote(gates.at[j], gate_each.at[j], g_send.at[0], g_recv.at[j], {"expert": j}).wait_recv()
    own_gate.wait()
    tasks = cot.shape[0]

    @pl.loop(0, n_e)
    def _(j):
        weight = gate_each[j]
        total = weight[:, 0:1] * cot[0].astype(F32)
        for t in range(1, tasks):
            total = total + weight[:, t:t + 1] * cot[t].astype(F32)
        piece[j] = total.astype(BF16)

    own_piece = pltpu.make_async_copy(piece.at[e], d_out.at[z, e], own_sem.at[2])
    own_piece.start()
    for s in range(1, n_e):
        j = plane(s)
        go(remote(piece.at[j], d_out.at[z, e], o_send.at[s], o_recv.at[e], {"expert": j}))

    def send_outputs():
        own_made.start()
        for s in range(1, n_e):
            j = plane(s)
            go(remote(made.at[j], outs.at[e], m_send.at[s], m_recv.at[e], {"expert": j}))

    own_made = pltpu.make_async_copy(made.at[e], outs.at[e], own_sem.at[3])
    stores = []
    for i in range(n_d):
        zi = along(i)
        if i + 1 < n_d:
            arrived(along(i + 1), e)
            spread(i + 1)
        if i == 1:
            send_outputs()
        if i == 0:
            for s in range(1, n_e):
                j = plane(s)
                remote(piece.at[j], d_out.at[z, j], o_send.at[0], o_recv.at[j],
                       {"expert": j}).wait_recv()
            own_piece.wait()
            for k in range(1, n_d):
                go(remote(d_out.at[z], d_out.at[z], z_send.at[k], z_recv.at[z], {"dp": along(k)}))
            own_rows.wait()
        for s in range(1, pairs):
            j = plane(2 * s)
            arrived(zi, j)
            go(remote(rows.at[zi, j], rows.at[zi, j], t_send.at[i, pairs - 1 + s],
                      t_recv.at[zi, j], {"expert": partner}))
        for s in range(pairs):
            arrived(zi, lax.rem(partner + 2 * s, n_e))
        load = pltpu.make_async_copy(rows.at[zi], block, load_sem)
        load.start()
        if i == 0:
            load_weights.wait()
        else:
            stores[-1].wait()
        load.wait()
        height = block.shape[0] * block.shape[1]
        tile = 256
        left = block[...].reshape(height, block.shape[2])

        @pl.loop(0, tall.shape[1] // tile)
        def _(c):
            here = pl.ds(pl.multiple_of(c * tile, tile), tile)
            value = jnp.dot(left, weights[:, here], preferred_element_type=F32)
            tall[:, here] = value
            if i == 0:
                hidden[:, here] = (value * jax.nn.sigmoid(value)).astype(BF16)

        store = pltpu.make_async_copy(tall, pre.at[zi], store_sem)
        store.start()
        stores.append(store)
        if i == 0:
            load_later.wait()

            @pl.loop(0, made.shape[2] // tile)
            def _(c):
                here = pl.ds(pl.multiple_of(c * tile, tile), tile)
                value = jnp.dot(hidden[...], later[:, here], preferred_element_type=F32)
                made[:, :, here] = value.astype(BF16).reshape(n_e, -1, tile)

    stores[-1].wait()
    if n_d == 1:
        send_outputs()
    own_made.wait()
    for s in range(1, n_e):
        j = plane(s)
        remote(made.at[j], outs.at[j], m_send.at[0], m_recv.at[j], {"expert": j}).wait_recv()
    for i in range(1, n_d):
        zi = along(i)
        remote(d_out.at[zi], d_out.at[zi], z_send.at[0], z_recv.at[zi], {"dp": zi}).wait_recv()
    for copy in sent:
        copy.wait_send()


def gather_all(trunk, gates, cot, first, second):
    n_e, n_d = lax.axis_size("expert"), lax.axis_size("dp")
    share, depth = trunk.shape
    width = first.shape[1]
    out = cot.shape[2]
    anywhere = pl.BlockSpec(memory_space=pl.ANY)
    hbm = pl.BlockSpec(memory_space=pltpu.HBM)
    vmem = pl.BlockSpec(memory_space=pltpu.VMEM)
    dma = pltpu.SemaphoreType.DMA
    return pl.pallas_call(
        functools.partial(gather_kernel, n_e, n_d),
        out_shape=(
            jax.ShapeDtypeStruct((n_d, n_e, share, depth), BF16),
            jax.ShapeDtypeStruct((n_d, n_e, share, out), BF16),
            jax.ShapeDtypeStruct((n_d, n_e * share, width), F32),
            jax.ShapeDtypeStruct(gates.shape, F32),
            jax.ShapeDtypeStruct((n_e, share, out), BF16),
        ),
        in_specs=[vmem, vmem, vmem, hbm, hbm],
        out_specs=(hbm, hbm, hbm, vmem, hbm),
        scratch_shapes=[
            pltpu.VMEM(first.shape, BF16),
            pltpu.VMEM(second.shape, BF16),
            pltpu.VMEM((n_e * share, width), BF16),
            pltpu.VMEM((n_e, share, out), BF16),
            dma((n_e,)), dma((n_e,)), dma,
            pltpu.VMEM((n_e, share, out), BF16),
            pltpu.VMEM((n_e, share, depth), BF16),
            pltpu.VMEM((n_e * share, width), F32),
            dma, dma, dma,
            dma((n_e,)), dma((n_e,)),
            dma((n_d, n_e)), dma((n_d, n_e)),
            dma((n_e,)), dma((n_e,)),
            dma((n_d,)), dma((n_d,)),
            dma((4,)),
        ],
        compiler_params=pltpu.CompilerParams(
            collective_id=0, has_side_effects=True, vmem_limit_bytes=48 * 1024 * 1024),
    )(trunk, gates, cot, first, second)


def return_kernel(n_e, d_pre, first, d_gate, d_trunk, gate_back, weights, part, near, pair, got,
                  w_sem, n_send, n_recv, p_send, p_recv, g_send, g_recv, own_sem):
    e = lax.axis_index("expert")
    core, seat, pairs = lax.rem(e, 2), e // 2, n_e // 2
    partner = e + 1 - 2 * core
    tiles, tile, _ = weights.shape

    def plane(s):
        return lax.rem(e + s, n_e)

    def remote(src, dst, send, recv, j):
        return pltpu.make_async_remote_copy(
            src_ref=src, dst_ref=dst, send_sem=send, recv_sem=recv,
            device_id={"expert": j}, device_id_type=MESH)

    def load(c):
        return pltpu.make_async_copy(first.at[c], weights.at[c], w_sem.at[c])

    for c in range(tiles):
        load(c).start()
    barrier = pltpu.get_barrier_semaphore()
    for s in range(1, n_e):
        pl.semaphore_signal(barrier, inc=1, device_id={"expert": plane(s)}, device_id_type=MESH)
    pl.semaphore_wait(barrier, n_e - 1)

    own = pltpu.make_async_copy(d_gate.at[e], gate_back.at[e], own_sem)
    own.start()

    def gate_out(s):
        j = plane(s)
        return remote(d_gate.at[j], gate_back.at[e], g_send.at[s], g_recv.at[e], j)

    def near_out(c):
        return remote(part.at[c, :, 1 - core], near.at[c], n_send.at[c], n_recv.at[c], partner)

    def part_out(c, s):
        k = lax.rem(seat + s, pairs)
        return remote(pair.at[c, k], got.at[c, seat], p_send.at[c, s], p_recv.at[c, seat],
                      2 * k + core)

    for s in range(1, n_e):
        gate_out(s).start()

    def compute(c):
        load(c).wait()
        value = lax.dot_general(
            d_pre[...], weights[c], (((1,), (1,)), ((), ())), preferred_element_type=F32)
        part[c] = value.astype(BF16).reshape(pairs, 2, -1, tile)

    def combine(c):
        near_out(c).wait_recv()
        pair[c] = (part[c, :, core].astype(F32) + near[c].astype(F32)).astype(BF16)

    def send(c):
        for s in range(1, pairs):
            part_out(c, s).start()

    compute(0)
    near_out(0).start()
    compute(1)
    combine(0)

    @pl.loop(2, tiles)
    def _(c):
        near_out(c - 1).start()
        send(c - 2)
        compute(c)
        combine(c - 1)

    near_out(tiles - 1).start()
    send(tiles - 2)
    combine(tiles - 1)
    send(tiles - 1)

    @pl.loop(0, tiles)
    def _(c):
        total = pair[c, seat].astype(F32)
        for s in range(1, pairs):
            k = lax.rem(seat + s, pairs)
            remote(pair.at[c, k], got.at[c, k], p_send.at[c, 0], p_recv.at[c, k],
                   2 * k + core).wait_recv()
            total = total + got[c, k].astype(F32)
        d_trunk[:, pl.ds(pl.multiple_of(c * tile, tile), tile)] = total.astype(BF16)

    own.wait()
    for s in range(1, n_e):
        j = plane(s)
        remote(d_gate.at[j], gate_back.at[j], g_send.at[0], g_recv.at[j], j).wait_recv()
    for s in range(1, n_e):
        gate_out(s).wait_send()

    @pl.loop(0, tiles)
    def _(c):
        near_out(c).wait_send()
        for s in range(1, pairs):
            part_out(c, s).wait_send()


def return_all(d_pre, first, d_gate):
    n_e = lax.axis_size("expert")
    tile = 512
    depth, width = first.shape
    tiles = depth // tile
    share = d_pre.shape[0] // n_e
    hbm = pl.BlockSpec(memory_space=pltpu.HBM)
    vmem = pl.BlockSpec(memory_space=pltpu.VMEM)
    dma = pltpu.SemaphoreType.DMA
    return pl.pallas_call(
        functools.partial(return_kernel, n_e),
        out_shape=(
            jax.ShapeDtypeStruct((share, depth), BF16),
            jax.ShapeDtypeStruct(d_gate.shape, F32),
        ),
        in_specs=[vmem, hbm, vmem],
        out_specs=(vmem, vmem),
        scratch_shapes=[
            pltpu.VMEM((tiles, tile, width), BF16),
            pltpu.VMEM((tiles, n_e // 2, 2, share, tile), BF16),
            pltpu.VMEM((tiles, n_e // 2, share, tile), BF16),
            pltpu.VMEM((tiles, n_e // 2, share, tile), BF16),
            pltpu.VMEM((tiles, n_e // 2, share, tile), BF16),
            dma((tiles,)), dma((tiles,)), dma((tiles,)),
            dma((tiles, n_e // 2)), dma((tiles, n_e // 2)),
            dma((n_e,)), dma((n_e,)), dma,
        ],
        compiler_params=pltpu.CompilerParams(
            collective_id=1, has_side_effects=True, vmem_limit_bytes=48 * 1024 * 1024),
    )(d_pre, first.reshape(tiles, tile, width), d_gate)


def on_device(trunk, w_first, w_second, gates, d_mixed):
    rank = lax.axis_index("dp")
    first = w_first[0]
    second = w_second[0]
    gate_here = gates[0]
    n_dp = lax.axis_size("dp")
    depth = first.shape[0] // n_dp
    units = second.shape[0] // n_dp
    group = gate_here.shape[1]

    n_e = lax.axis_size("expert")
    gate_parts = gate_here.T.astype(F32).reshape(n_e, -1, gate_here.shape[0])
    rows_all, d_output_all, pre, gates_each, outs_each = gather_all(
        trunk, gate_parts, jnp.transpose(d_mixed, (1, 0, 2)), first, second)
    rows_all = rows_all.reshape(-1, trunk.shape[1])
    d_output_all = d_output_all.reshape(-1, second.shape[1])
    pre = pre.reshape(-1, first.shape[1])
    gates_each = gates_each.astype(BF16)
    d_hidden = lax.dot_general(
        d_output_all, second, (((1,), (1,)), ((), ())), preferred_element_type=F32
    )
    sig = jax.nn.sigmoid(pre)
    d_pre = (d_hidden * sig * (1.0 + pre * (1.0 - sig))).astype(BF16)
    d_pre_here = lax.dynamic_slice_in_dim(d_pre, rank * group, group, 0)
    mixed = jnp.einsum(
        "ert,ero->rto", gates_each, outs_each, preferred_element_type=F32
    ).astype(BF16)
    d_gate_each = jnp.einsum(
        "rto,ero->ert", d_mixed, outs_each, preferred_element_type=F32
    ).astype(BF16)
    d_trunk, back_gate = return_all(d_pre_here, first, d_gate_each.astype(F32))
    d_gate = back_gate.reshape(group, -1).T.astype(BF16)[None]

    columns = lax.dynamic_slice_in_dim(rows_all, rank * depth, depth, 1)
    d_first = lax.dot_general(
        columns, d_pre, (((0,), (0,)), ((), ())), preferred_element_type=F32
    ).astype(BF16)
    some_pre = lax.dynamic_slice_in_dim(pre, rank * units, units, 1)
    some_hidden = jax.nn.silu(some_pre).astype(BF16)
    d_second = lax.dot_general(
        some_hidden, d_output_all, (((0,), (0,)), ((), ())), preferred_element_type=F32
    ).astype(BF16)
    return (mixed, d_trunk, d_gate, d_first[None], d_second[None])


SIDE, LINE, LANES = 2, 4, 128
VMEM_BYTES = 62 * 1024 * 1024


def tiled(count, body, hooks=()):
    @pl.loop(0, count)
    def _(c):
        body(c)
        for at, hook in hooks:
            pl.when(c == at)(hook)


def step_kernel(n_e, n_d, trunk, gates, cot_in, first, second,
                columns_out, d_out_out, d_pre_out, units_out, mixed_out, d_trunk_out, back_out_ref,
                rows, d_out, d_pre, some_hidden, mixed, d_trunk, gate_back, gate_in, gate_piece,
                weights, later, turned, cot, gate_each, mix, piece, tall, hidden, made, outs, d_gate,
                part, near, pair, got,
                load_sem, own_sem, g_send, g_recv, t_send, t_recv, o_send, o_recv, z_send, z_recv,
                m_send, m_recv, n_send, n_recv, p_send, p_recv, b_send, b_recv, out_sem):
    e = lax.axis_index("expert")
    z = lax.axis_index("dp")
    core, seat, pairs = lax.rem(e, 2), e // 2, n_e // 2
    partner = e + 1 - 2 * core
    side, up = lax.rem(seat, SIDE), seat // SIDE
    across = e + 2 - 4 * side
    over = e + 2 * SIDE - 4 * SIDE * up
    corner = across + over - e
    bridge = across * (1 - core) + over * core
    other = across * core + over * (1 - core)
    middle = (z * (n_d - 1 - z)) // 2
    inner = middle == 1
    mate = z + 1 - 2 * lax.rem(z, 2)
    mirror = n_d - 1 - z
    skip = lax.rem(z + 2, n_d)
    order = [z, mate, middle * mirror + (1 - middle) * skip, middle * skip + (1 - middle) * mirror]
    tasks = cot.shape[0] // rows.shape[2]
    share, depth = rows.shape[2], rows.shape[3]
    width = tall.shape[2]
    group = n_e * share
    units = some_hidden.shape[2]
    part_depth = depth // n_d
    depth_here = pl.ds(pl.multiple_of(z * part_depth, part_depth), part_depth)

    def plane(s):
        return lax.rem(e + s, n_e)

    def remote(src, dst, send, recv, where):
        return pltpu.make_async_remote_copy(
            src_ref=src, dst_ref=dst, send_sem=send, recv_sem=recv,
            device_id=where, device_id_type=MESH)

    def load(k):
        src, dst = [(second, later), (cot_in, cot), (first, weights), (gates, gate_in)][k]
        return pltpu.make_async_copy(src, dst, load_sem.at[k])

    def own(k):
        src, dst = [(gate_piece.at[e], gate_each.at[e]), (trunk, rows.at[z, e]),
                    (piece.at[e], d_out.at[z, e]), (made.at[e], outs.at[e]),
                    (d_gate.at[e], gate_back.at[e])][k]
        return pltpu.make_async_copy(src, dst, own_sem.at[k])

    def at_plane(j):
        return {"expert": j}

    def gate_out(s):
        j = plane(s)
        return remote(gate_piece.at[j], gate_each.at[e], g_send.at[s], g_recv.at[e], at_plane(j))

    def trunk_out(g, k):
        zi = order[g]
        j, where = [
            (e, at_plane(across)), (e, at_plane(over)), (e, at_plane(partner)),
            (bridge, at_plane(over * (1 - core) + across * core)),
            (bridge, at_plane(partner)), (other, at_plane(partner)), (corner, at_plane(partner)),
            (e, {"dp": mate}), (e, {"dp": mirror})][k]
        src = trunk if g == 0 and k in (0, 1, 2, 7, 8) else rows.at[zi, j]
        return remote(src, rows.at[zi, j], t_send.at[g, k], t_recv.at[zi, j], where)

    def trunk_in(g, j):
        zi = order[g]
        remote(trunk, rows.at[zi, j], t_send.at[0, 0], t_recv.at[zi, j],
               at_plane(partner)).wait_recv()

    def piece_out(s):
        j = plane(s)
        return remote(piece.at[j], d_out.at[z, e], o_send.at[s], o_recv.at[e], at_plane(j))

    def half(zi, h):
        return d_out.at[zi, h * (n_e // 2):(h + 1) * (n_e // 2)]

    def line_out(g, k, h):
        zi = order[g]
        return remote(half(zi, h), half(zi, h), z_send.at[g, k, h], z_recv.at[zi, h],
                      {"dp": mate if k == 0 else mirror})

    def keep(k):
        src, dst = ([(rows.at[zi, :, :, depth_here], columns_out.at[zi]) for zi in order]
                    + [(d_pre.at[zi], d_pre_out.at[zi]) for zi in order]
                    + [(d_out, d_out_out), (some_hidden, units_out), (mixed, mixed_out),
                       (d_trunk, d_trunk_out), (gate_back, back_out_ref)])[k]
        return pltpu.make_async_copy(src, dst, out_sem.at[k])

    def made_out(s):
        j = plane(s)
        return remote(made.at[j], outs.at[e], m_send.at[s], m_recv.at[e], at_plane(j))

    def back_out(s):
        j = plane(s)
        return remote(d_gate.at[j], gate_back.at[e], b_send.at[s], b_recv.at[e], at_plane(j))

    def near_out(c):
        return remote(part.at[c, :, 1 - core], near.at[c], n_send.at[c], n_recv.at[c],
                      at_plane(partner))

    def part_out(c, s):
        k = lax.rem(seat + s, pairs)
        return remote(pair.at[c, k], got.at[c, seat], p_send.at[c, s], p_recv.at[c, seat],
                      at_plane(2 * k + core))

    def spread(g):
        for k in range(3):
            trunk_out(g, k).start()

    def bridge_on(g):
        trunk_in(g, bridge)
        trunk_out(g, 3).start()
        trunk_out(g, 4).start()
        trunk_in(g, other)
        trunk_out(g, 5).start()

    def corner_on(g):
        trunk_in(g, corner)
        trunk_out(g, 6).start()

    def complete(g):
        for shift in (0, across - e, over - e, corner - e):
            trunk_in(g, partner + shift)

    def arrive(g):
        trunk_in(g, e)
        if g == 1:
            pl.when(inner)(lambda: trunk_out(1, 8).start())
        else:
            pl.when(inner)(lambda: trunk_out(g, 7).start())

    def line_arrive(g, h):
        zi = order[g]
        remote(half(zi, h), half(zi, h), z_send.at[0, 0, h], z_recv.at[zi, h],
               {"dp": mate}).wait_recv()
        pl.when(inner)(lambda: line_out(g, 1 if g == 1 else 0, h).start())

    def in_middle(call, *g):
        pl.when(inner)(lambda: call(*g))

    def at_end(call, *g):
        pl.when(middle == 0)(lambda: call(*g))

    for k in (3, 1, 0, 2):
        load(k).start()
    barrier = pltpu.get_barrier_semaphore()
    for s in range(1, n_e):
        pl.semaphore_signal(barrier, inc=1, device_id=at_plane(plane(s)), device_id_type=MESH)
    for i in range(1, n_d):
        pl.semaphore_signal(barrier, inc=1, device_id={"dp": lax.rem(z + i, n_d)},
                            device_id_type=MESH)
    load(3).wait()
    task_eye = jnp.where(
        lax.broadcasted_iota(jnp.int32, (tasks, LANES), 0)
        == lax.broadcasted_iota(jnp.int32, (tasks, LANES), 1), 1.0, 0.0).astype(BF16)
    gate_piece[...] = lax.dot_general(
        gate_in[...], task_eye, (((0,), (0,)), ((), ())),
        preferred_element_type=F32).reshape(gate_piece.shape)
    own(0).start()
    own(1).start()
    pl.semaphore_wait(barrier, n_e - 1 + n_d - 1)

    for s in range(1, n_e):
        gate_out(s).start()
    trunk_out(0, 7).start()
    pl.when(inner)(lambda: trunk_out(0, 8).start())
    spread(0)

    def turn(low, high):
        @pl.loop(low, high)
        def _(c):
            here = pl.ds(pl.multiple_of(c * 256, 256), 256)
            turned[:, here] = later[here, :].T

    turns = width // 256
    load(0).wait()
    turn(0, turns // 2)

    def task_of():
        shape = (LANES, share * tasks)
        return jnp.where(
            lax.broadcasted_iota(jnp.int32, shape, 0)
            == lax.rem(lax.broadcasted_iota(jnp.int32, shape, 1), tasks), 1.0, 0.0).astype(BF16)

    def same_sample():
        shape = (n_e, share, share * tasks)
        match = (lax.broadcasted_iota(jnp.int32, shape, 1)
                 == lax.div(lax.broadcasted_iota(jnp.int32, shape, 2), tasks))
        return jnp.where(match, 1.0, 0.0).reshape(group, share * tasks)

    for s in range(1, n_e):
        j = plane(s)
        remote(gate_piece.at[j], gate_each.at[j], g_send.at[0], g_recv.at[j],
               at_plane(j)).wait_recv()
    own(0).wait()
    load(1).wait()
    each = gate_each[...].reshape(group, LANES).astype(BF16)
    mix[...] = (jnp.dot(each, task_of(), preferred_element_type=F32)
                * same_sample()).astype(BF16)
    piece[...] = jnp.dot(mix[...], cot[...], preferred_element_type=F32).astype(BF16).reshape(
        piece.shape)
    for s in range(1, n_e):
        piece_out(s).start()
    own(2).start()

    turn(turns // 2, turns)
    bridge_on(0)
    arrive(1)
    in_middle(arrive, 2)
    for s in range(1, n_e):
        j = plane(s)
        remote(piece.at[j], d_out.at[z, j], o_send.at[0], o_recv.at[j], at_plane(j)).wait_recv()
    own(2).wait()
    for h in range(2):
        line_out(0, 0, h).start()
        in_middle(lambda: line_out(0, 1, h).start())

    tile = 512

    def part_of(c):
        return pl.ds(pl.multiple_of(c * tile, tile), tile)

    def back_hidden(g, c):
        left = d_out[order[g]].reshape(group, d_out.shape[3])
        return jnp.dot(left, turned[:, part_of(c)], preferred_element_type=F32)

    def forward_pre(g, c):
        left = rows[order[g]].reshape(group, depth)
        return jnp.dot(left, weights[:, part_of(c)], preferred_element_type=F32)

    def store_d_pre(g, c, d_hidden, value):
        sig = jax.nn.sigmoid(value)
        d_pre[order[g], :, part_of(c)] = (
            d_hidden * sig * (1.0 + value * (1.0 - sig))).astype(BF16)

    def first_hidden(c):
        tall[0, :, part_of(c)] = back_hidden(0, c)

    def first_pre(c):
        value = forward_pre(0, c)
        store_d_pre(0, c, tall[0, :, part_of(c)], value)
        hidden[:, part_of(c)] = (value * jax.nn.sigmoid(value)).astype(BF16)

    def later_pre(g):
        def body(c):
            tall[g, :, part_of(c)] = forward_pre(g, c)
        return body

    def later_hidden(g):
        def body(c):
            store_d_pre(g, c, back_hidden(g, c), tall[g, :, part_of(c)])
        return body

    units_here = pl.ds(pl.multiple_of(z * units, units), units)

    def keep_units(g):
        value = tall[g, :, units_here]
        some_hidden[order[g]] = (value * jax.nn.sigmoid(value)).astype(BF16)

    tiled(width // tile, first_hidden)
    spread(1)
    corner_on(0)
    own(1).wait()
    complete(0)
    load(2).wait()

    def hook_a():
        in_middle(arrive, 3)
        at_end(arrive, 2)
        spread(2)

    tiled(width // tile, first_pre, [(2, hook_a)])
    keep(0).start()
    keep(4).start()
    some_hidden[z] = hidden[:, units_here]

    def first_output(c):
        value = jnp.dot(hidden[...], later[:, part_of(c)], preferred_element_type=F32)
        made[:, :, part_of(c)] = value.astype(BF16).reshape(n_e, share, tile)

    tiled(made.shape[2] // tile, first_output)
    own(3).start()
    bridge_on(1)

    def compute(c):
        value = lax.dot_general(d_pre[z], weights[part_of(c), :], (((1,), (1,)), ((), ())),
                                preferred_element_type=F32)
        part[c] = value.astype(BF16).reshape(pairs, 2, share, tile)

    def combine(c):
        near_out(c).wait_recv()
        pair[c] = (part[c, :, core].astype(F32) + near[c].astype(F32)).astype(BF16)

    def send_parts(low, high):
        @pl.loop(low, high)
        def _(c):
            for s in range(1, pairs):
                part_out(c, s).start()

    count = depth // tile
    compute(0)
    near_out(0).start()
    compute(1)
    combine(0)

    def hook_b():
        at_end(arrive, 3)
        at_end(spread, 3)

    def hook_c():
        for h in range(2):
            line_arrive(1, h)
            in_middle(line_arrive, 2, h)

    hooks = [(2, lambda: in_middle(spread, 3)), (4, hook_b), (5, lambda: bridge_on(2)),
             (6, hook_c), (7, lambda: corner_on(1))]

    @pl.loop(2, count)
    def _(c):
        near_out(c - 1).start()
        compute(c)
        combine(c - 1)
        for at, hook in hooks:
            pl.when(c == at)(hook)

    near_out(count - 1).start()
    complete(1)
    keep(1).start()
    tiled(width // tile, later_pre(1), [(0, lambda: combine(count - 1)),
                                        (2, lambda: bridge_on(3))])
    keep_units(1)
    send_parts(0, count // 2)
    tiled(width // tile, later_hidden(1), [(1, lambda: corner_on(2))])
    send_parts(count // 2, count)
    keep(5).start()
    complete(2)
    keep(2).start()

    def hook_d():
        for h in range(2):
            in_middle(line_arrive, 3, h)

    def hook_e():
        for s in range(1, n_e):
            made_out(s).start()

    tiled(width // tile, later_pre(2), [(0, hook_e), (1, hook_d), (3, lambda: corner_on(3))])
    keep_units(2)
    for h in range(2):
        at_end(line_arrive, 2, h)
    tiled(width // tile, later_hidden(2))
    keep(6).start()
    complete(3)
    keep(3).start()
    tiled(width // tile, later_pre(3))
    keep_units(3)
    keep(9).start()

    own(3).wait()
    for s in range(1, n_e):
        j = plane(s)
        remote(made.at[j], outs.at[j], m_send.at[0], m_recv.at[j], at_plane(j)).wait_recv()
    each_out = outs[...].reshape(group, outs.shape[2])
    product = lax.dot_general(each_out, cot[...], (((1,), (1,)), ((), ())),
                              preferred_element_type=F32)
    product = (product * same_sample()).astype(BF16)
    d_gate[...] = lax.dot_general(product, task_of(), (((1,), (1,)), ((), ())),
                                  preferred_element_type=F32).reshape(d_gate.shape)
    own(4).start()
    for s in range(1, n_e):
        back_out(s).start()
    mixed[...] = lax.dot_general(mix[...], each_out, (((0,), (0,)), ((), ())),
                                 preferred_element_type=F32).astype(BF16)

    @pl.loop(0, count)
    def _(c):
        total = pair[c, seat].astype(F32)
        for s in range(1, pairs):
            k = lax.rem(seat + s, pairs)
            remote(pair.at[c, k], got.at[c, k], p_send.at[c, 0], p_recv.at[c, k],
                   at_plane(2 * k + core)).wait_recv()
            total = total + got[c, k].astype(F32)
        d_trunk[:, part_of(c)] = total.astype(BF16)

    keep(10).start()
    keep(11).start()
    at_end(line_arrive, 3, 0)
    at_end(line_arrive, 3, 1)
    keep(8).start()
    tiled(width // tile, later_hidden(3))
    keep(7).start()

    own(4).wait()
    for s in range(1, n_e):
        j = plane(s)
        remote(d_gate.at[j], gate_back.at[j], b_send.at[0], b_recv.at[j], at_plane(j)).wait_recv()
    for s in range(1, n_e):
        gate_out(s).wait_send()
        piece_out(s).wait_send()
        made_out(s).wait_send()
        back_out(s).wait_send()
    for g in range(n_d):
        for k in range(7):
            trunk_out(g, k).wait_send()
    keep(12).start()
    trunk_out(0, 7).wait_send()
    for h in range(2):
        line_out(0, 0, h).wait_send()

    @pl.when(inner)
    def _():
        trunk_out(0, 8).wait_send()
        trunk_out(1, 8).wait_send()
        for g in range(2, n_d):
            trunk_out(g, 7).wait_send()
        for h in range(2):
            line_out(0, 1, h).wait_send()
            line_out(1, 1, h).wait_send()
            for g in range(2, n_d):
                line_out(g, 0, h).wait_send()

    @pl.loop(0, count)
    def _(c):
        near_out(c).wait_send()
        for s in range(1, pairs):
            part_out(c, s).wait_send()

    for k in range(13):
        keep(k).wait()


def step_all(trunk, gates, cot, first, second):
    n_e, n_d = lax.axis_size("expert"), lax.axis_size("dp")
    share, depth = trunk.shape
    width = first.shape[1]
    out = second.shape[1]
    group = n_e * share
    count, pairs, tile = depth // 512, n_e // 2, 512
    hbm = pl.BlockSpec(memory_space=pltpu.HBM)
    dma = pltpu.SemaphoreType.DMA
    gate_shape = (n_e, share, LANES)
    return pl.pallas_call(
        functools.partial(step_kernel, n_e, n_d),
        out_shape=(
            jax.ShapeDtypeStruct((n_d, n_e, share, depth // n_d), BF16),
            jax.ShapeDtypeStruct((n_d, n_e, share, out), BF16),
            jax.ShapeDtypeStruct((n_d, group, width), BF16),
            jax.ShapeDtypeStruct((n_d, group, width // n_d), BF16),
            jax.ShapeDtypeStruct((cot.shape[0], out), BF16),
            jax.ShapeDtypeStruct((share, depth), BF16),
            jax.ShapeDtypeStruct(gate_shape, F32),
        ),
        in_specs=[hbm] * 5,
        out_specs=(hbm,) * 7,
        scratch_shapes=[
            pltpu.VMEM((n_d, n_e, share, depth), BF16),
            pltpu.VMEM((n_d, n_e, share, out), BF16),
            pltpu.VMEM((n_d, group, width), BF16),
            pltpu.VMEM((n_d, group, width // n_d), BF16),
            pltpu.VMEM((cot.shape[0], out), BF16),
            pltpu.VMEM((share, depth), BF16),
            pltpu.VMEM(gate_shape, F32),
            pltpu.VMEM(gates.shape, BF16),
            pltpu.VMEM(gate_shape, F32),
            pltpu.VMEM(first.shape, BF16),
            pltpu.VMEM(second.shape, BF16),
            pltpu.VMEM(second.shape[::-1], BF16),
            pltpu.VMEM(cot.shape, BF16),
            pltpu.VMEM(gate_shape, F32),
            pltpu.VMEM((group, cot.shape[0]), BF16),
            pltpu.VMEM((n_e, share, out), BF16),
            pltpu.VMEM((n_d, group, width), F32),
            pltpu.VMEM((group, width), BF16),
            pltpu.VMEM((n_e, share, out), BF16),
            pltpu.VMEM((n_e, share, out), BF16),
            pltpu.VMEM(gate_shape, F32),
            pltpu.VMEM((count, pairs, 2, share, tile), BF16),
            pltpu.VMEM((count, pairs, share, tile), BF16),
            pltpu.VMEM((count, pairs, share, tile), BF16),
            pltpu.VMEM((count, pairs, share, tile), BF16),
            dma((4,)), dma((5,)),
            dma((n_e,)), dma((n_e,)),
            dma((n_d, 9)), dma((n_d, n_e)),
            dma((n_e,)), dma((n_e,)),
            dma((n_d, 2, 2)), dma((n_d, 2)),
            dma((n_e,)), dma((n_e,)),
            dma((count,)), dma((count,)),
            dma((count, pairs)), dma((count, pairs)),
            dma((n_e,)), dma((n_e,)), dma((13,)),
        ],
        compiler_params=pltpu.CompilerParams(
            collective_id=2, has_side_effects=True, vmem_limit_bytes=VMEM_BYTES),
    )(trunk, gates, cot, first, second)


def finish_kernel(columns, d_pre, units, d_out, mixed, d_trunk, back,
                  d_first, d_second, mixed_out, d_trunk_out, d_gate,
                  columns_v, d_pre_v, units_v, d_out_v, mixed_v, d_trunk_v, back_v,
                  first_v, second_v, gate_v, in_sem, out_sem, tile_sem, wide_sem):
    pairs = [(units, units_v), (d_out, d_out_v), (columns, columns_v), (mixed, mixed_v),
             (d_trunk, d_trunk_v), (back, back_v)]
    steps = d_pre.shape[0]

    def take(k):
        return pltpu.make_async_copy(*pairs[k], in_sem.at[k])

    def wide(k):
        return pltpu.make_async_copy(d_pre.at[k], d_pre_v.at[k], wide_sem.at[k])

    def give(k):
        src, dst = [(second_v, d_second), (mixed_v, mixed_out), (d_trunk_v, d_trunk_out),
                    (gate_v, d_gate)][k]
        return pltpu.make_async_copy(src, dst, out_sem.at[k])

    for k in range(3):
        take(k).start()
    for k in range(steps):
        wide(k).start()
    for k in range(3, len(pairs)):
        take(k).start()
    take(0).wait()
    take(1).wait()
    second_v[...] = lax.dot_general(
        units_v[...], d_out_v[...], (((0,), (0,)), ((), ())),
        preferred_element_type=F32).astype(BF16)
    give(0).start()
    take(2).wait()
    for k in range(steps):
        wide(k).wait()
    tile = first_v.shape[1]
    count = first_v.shape[0]

    def store(c):
        here = pl.ds(pl.multiple_of(c * tile, tile), tile)
        return pltpu.make_async_copy(first_v.at[c], d_first.at[here], tile_sem.at[c])

    @pl.loop(0, count)
    def _(c):
        here = pl.ds(pl.multiple_of(c * tile, tile), tile)
        right = d_pre_v[...].reshape(-1, d_pre_v.shape[2])
        first_v[c] = lax.dot_general(
            columns_v[:, here], right, (((0,), (0,)), ((), ())),
            preferred_element_type=F32).astype(BF16)
        store(c).start()

        @pl.when(c == 0)
        def _():
            take(3).wait()
            give(1).start()
            take(4).wait()
            give(2).start()
            take(5).wait()
            tasks = d_gate.shape[0]
            eye = jnp.where(
                lax.broadcasted_iota(jnp.int32, (tasks, LANES), 0)
                == lax.broadcasted_iota(jnp.int32, (tasks, LANES), 1), 1.0, 0.0).astype(BF16)
            gate_v[...] = lax.dot_general(
                eye, back_v[...].astype(BF16), (((1,), (1,)), ((), ())),
                preferred_element_type=F32).astype(BF16)
            give(3).start()

    for k in range(4):
        give(k).wait()

    @pl.loop(0, count)
    def _(c):
        store(c).wait()


def finish_all(columns, d_pre, units, d_out, mixed, d_trunk, back, tasks):
    hbm = pl.BlockSpec(memory_space=pltpu.HBM)
    dma = pltpu.SemaphoreType.DMA
    rows, depth = columns.shape
    steps, group, width = d_pre.shape
    unit, out = units.shape[1], d_out.shape[1]
    tile = 256
    ins = (columns, d_pre, units, d_out, mixed, d_trunk, back)
    return pl.pallas_call(
        finish_kernel,
        out_shape=(
            jax.ShapeDtypeStruct((depth, width), BF16),
            jax.ShapeDtypeStruct((unit, out), BF16),
            jax.ShapeDtypeStruct(mixed.shape, BF16),
            jax.ShapeDtypeStruct(d_trunk.shape, BF16),
            jax.ShapeDtypeStruct((tasks, back.shape[0]), BF16),
        ),
        in_specs=[hbm] * 7,
        out_specs=(hbm,) * 5,
        scratch_shapes=[pltpu.VMEM(x.shape, x.dtype) for x in ins] + [
            pltpu.VMEM((depth // tile, tile, width), BF16),
            pltpu.VMEM((unit, out), BF16),
            pltpu.VMEM((tasks, back.shape[0]), BF16),
            dma((6,)), dma((4,)), dma((depth // tile,)), dma((steps,)),
        ],
        compiler_params=pltpu.CompilerParams(vmem_limit_bytes=VMEM_BYTES),
    )(*ins)


def on_square(trunk, w_first, w_second, gates, d_mixed):
    first, second, gate_here = w_first[0], w_second[0], gates[0]
    tasks, group = gate_here.shape
    columns, d_out, d_pre, units, mixed, d_trunk, back = step_all(
        trunk, gate_here, d_mixed.reshape(-1, d_mixed.shape[2]), first, second)
    d_first, d_second, mixed, d_trunk, d_gate = finish_all(
        columns.reshape(-1, columns.shape[3]), d_pre, units.reshape(-1, units.shape[2]),
        d_out.reshape(-1, d_out.shape[3]), mixed, d_trunk, back.reshape(group, -1), tasks)
    return (mixed.reshape(d_mixed.shape), d_trunk, d_gate[None], d_first[None], d_second[None])


def solution(mesh):
    in_specs = (
        P(("dp", "expert"), None),
        P("expert", None, None),
        P("expert", None, None),
        P("expert", None, "dp"),
        P(("dp", "expert"), None, None),
    )
    out_specs = (
        P(("dp", "expert"), None, None),
        P(("dp", "expert"), None),
        P("expert", None, "dp"),
        P("expert", "dp", None),
        P("expert", "dp", None),
    )
    fits = mesh.shape["expert"] == 2 * SIDE * SIDE and mesh.shape["dp"] == LINE
    return jax.shard_map(
        on_square if fits else on_device, mesh=mesh, in_specs=in_specs, out_specs=out_specs, check_vma=False
    )
```

```python
import functools

import jax
import jax.numpy as jnp
from jax import lax
from jax.experimental import pallas as pl
from jax.experimental.pallas import tpu as pltpu
from jax.sharding import PartitionSpec as P

F32 = jnp.float32
BF16 = jnp.bfloat16


MESH = pl.DeviceIdType.MESH


def gather_kernel(n_e, n_d, trunk, gates, cot, first, second, rows, d_out, pre, gate_each,
                  outs, weights, later, hidden, made, m_send, m_recv, later_sem, piece, block, tall, w_sem, load_sem, store_sem,
                  g_send, g_recv, t_send, t_recv, o_send, o_recv, z_send, z_recv,
                  own_sem):
    e = lax.axis_index("expert")
    z = lax.axis_index("dp")
    partner = e + 1 - 2 * lax.rem(e, 2)
    pairs = n_e // 2

    def plane(s):
        return lax.rem(e + s, n_e)

    def along(i):
        return lax.rem(z + i, n_d)

    def remote(src, dst, send, recv, where):
        return pltpu.make_async_remote_copy(
            src_ref=src, dst_ref=dst, send_sem=send, recv_sem=recv,
            device_id=where, device_id_type=MESH)

    load_weights = pltpu.make_async_copy(first, weights, w_sem)
    load_weights.start()
    load_later = pltpu.make_async_copy(second, later, later_sem)
    load_later.start()

    barrier = pltpu.get_barrier_semaphore()
    for s in range(1, n_e):
        pl.semaphore_signal(barrier, inc=1, device_id={"expert": plane(s)}, device_id_type=MESH)
    for i in range(1, n_d):
        pl.semaphore_signal(barrier, inc=1, device_id={"dp": along(i)}, device_id_type=MESH)
    pl.semaphore_wait(barrier, n_e - 1 + n_d - 1)

    sent = []

    def go(copy):
        copy.start()
        sent.append(copy)

    for s in range(1, n_e):
        j = plane(s)
        go(remote(gates.at[j], gate_each.at[e], g_send.at[s], g_recv.at[e], {"expert": j}))
    own_gate = pltpu.make_async_copy(gates.at[e], gate_each.at[e], own_sem.at[0])
    own_gate.start()
    own_rows = pltpu.make_async_copy(trunk, rows.at[z, e], own_sem.at[1])
    own_rows.start()

    def spread(i):
        zi = along(i)
        src = trunk if i == 0 else rows.at[zi, e]
        for s in range(1, pairs):
            go(remote(src, rows.at[zi, e], t_send.at[i, s], t_recv.at[zi, e],
                      {"expert": plane(2 * s)}))
        go(remote(src, rows.at[zi, e], t_send.at[i, 0], t_recv.at[zi, e], {"expert": partner}))

    def arrived(zi, j):
        remote(trunk, rows.at[zi, j], t_send.at[0, 0], t_recv.at[zi, j],
               {"expert": partner}).wait_recv()

    for i in range(1, n_d):
        go(remote(trunk, rows.at[z, e], t_send.at[i, n_e - 1], t_recv.at[z, e], {"dp": along(i)}))
    spread(0)

    for s in range(1, n_e):
        j = plane(s)
        remote(gates.at[j], gate_each.at[j], g_send.at[0], g_recv.at[j], {"expert": j}).wait_recv()
    own_gate.wait()
    tasks = cot.shape[0]

    @pl.loop(0, n_e)
    def _(j):
        weight = gate_each[j]
        total = weight[:, 0:1] * cot[0].astype(F32)
        for t in range(1, tasks):
            total = total + weight[:, t:t + 1] * cot[t].astype(F32)
        piece[j] = total.astype(BF16)

    own_piece = pltpu.make_async_copy(piece.at[e], d_out.at[z, e], own_sem.at[2])
    own_piece.start()
    for s in range(1, n_e):
        j = plane(s)
        go(remote(piece.at[j], d_out.at[z, e], o_send.at[s], o_recv.at[e], {"expert": j}))

    def send_outputs():
        own_made.start()
        for s in range(1, n_e):
            j = plane(s)
            go(remote(made.at[j], outs.at[e], m_send.at[s], m_recv.at[e], {"expert": j}))

    own_made = pltpu.make_async_copy(made.at[e], outs.at[e], own_sem.at[3])
    stores = []
    for i in range(n_d):
        zi = along(i)
        if i + 1 < n_d:
            arrived(along(i + 1), e)
            spread(i + 1)
        if i == 1:
            send_outputs()
        if i == 0:
            for s in range(1, n_e):
                j = plane(s)
                remote(piece.at[j], d_out.at[z, j], o_send.at[0], o_recv.at[j],
                       {"expert": j}).wait_recv()
            own_piece.wait()
            for k in range(1, n_d):
                go(remote(d_out.at[z], d_out.at[z], z_send.at[k], z_recv.at[z], {"dp": along(k)}))
            own_rows.wait()
        for s in range(1, pairs):
            j = plane(2 * s)
            arrived(zi, j)
            go(remote(rows.at[zi, j], rows.at[zi, j], t_send.at[i, pairs - 1 + s],
                      t_recv.at[zi, j], {"expert": partner}))
        for s in range(pairs):
            arrived(zi, lax.rem(partner + 2 * s, n_e))
        load = pltpu.make_async_copy(rows.at[zi], block, load_sem)
        load.start()
        if i == 0:
            load_weights.wait()
        else:
            stores[-1].wait()
        load.wait()
        height = block.shape[0] * block.shape[1]
        tile = 256
        left = block[...].reshape(height, block.shape[2])

        @pl.loop(0, tall.shape[1] // tile)
        def _(c):
            here = pl.ds(pl.multiple_of(c * tile, tile), tile)
            value = jnp.dot(left, weights[:, here], preferred_element_type=F32)
            tall[:, here] = value
            if i == 0:
                hidden[:, here] = (value * jax.nn.sigmoid(value)).astype(BF16)

        store = pltpu.make_async_copy(tall, pre.at[zi], store_sem)
        store.start()
        stores.append(store)
        if i == 0:
            load_later.wait()

            @pl.loop(0, made.shape[2] // tile)
            def _(c):
                here = pl.ds(pl.multiple_of(c * tile, tile), tile)
                value = jnp.dot(hidden[...], later[:, here], preferred_element_type=F32)
                made[:, :, here] = value.astype(BF16).reshape(n_e, -1, tile)

    stores[-1].wait()
    if n_d == 1:
        send_outputs()
    own_made.wait()
    for s in range(1, n_e):
        j = plane(s)
        remote(made.at[j], outs.at[j], m_send.at[0], m_recv.at[j], {"expert": j}).wait_recv()
    for i in range(1, n_d):
        zi = along(i)
        remote(d_out.at[zi], d_out.at[zi], z_send.at[0], z_recv.at[zi], {"dp": zi}).wait_recv()
    for copy in sent:
        copy.wait_send()


def gather_all(trunk, gates, cot, first, second):
    n_e, n_d = lax.axis_size("expert"), lax.axis_size("dp")
    share, depth = trunk.shape
    width = first.shape[1]
    out = cot.shape[2]
    anywhere = pl.BlockSpec(memory_space=pl.ANY)
    hbm = pl.BlockSpec(memory_space=pltpu.HBM)
    vmem = pl.BlockSpec(memory_space=pltpu.VMEM)
    dma = pltpu.SemaphoreType.DMA
    return pl.pallas_call(
        functools.partial(gather_kernel, n_e, n_d),
        out_shape=(
            jax.ShapeDtypeStruct((n_d, n_e, share, depth), BF16),
            jax.ShapeDtypeStruct((n_d, n_e, share, out), BF16),
            jax.ShapeDtypeStruct((n_d, n_e * share, width), F32),
            jax.ShapeDtypeStruct(gates.shape, F32),
            jax.ShapeDtypeStruct((n_e, share, out), BF16),
        ),
        in_specs=[vmem, vmem, vmem, hbm, hbm],
        out_specs=(hbm, hbm, hbm, vmem, hbm),
        scratch_shapes=[
            pltpu.VMEM(first.shape, BF16),
            pltpu.VMEM(second.shape, BF16),
            pltpu.VMEM((n_e * share, width), BF16),
            pltpu.VMEM((n_e, share, out), BF16),
            dma((n_e,)), dma((n_e,)), dma,
            pltpu.VMEM((n_e, share, out), BF16),
            pltpu.VMEM((n_e, share, depth), BF16),
            pltpu.VMEM((n_e * share, width), F32),
            dma, dma, dma,
            dma((n_e,)), dma((n_e,)),
            dma((n_d, n_e)), dma((n_d, n_e)),
            dma((n_e,)), dma((n_e,)),
            dma((n_d,)), dma((n_d,)),
            dma((4,)),
        ],
        compiler_params=pltpu.CompilerParams(
            collective_id=0, has_side_effects=True, vmem_limit_bytes=48 * 1024 * 1024),
    )(trunk, gates, cot, first, second)


def return_kernel(n_e, d_pre, first, d_gate, d_trunk, gate_back, weights, part, near, pair, got,
                  w_sem, n_send, n_recv, p_send, p_recv, g_send, g_recv, own_sem):
    e = lax.axis_index("expert")
    core, seat, pairs = lax.rem(e, 2), e // 2, n_e // 2
    partner = e + 1 - 2 * core
    tiles, tile, _ = weights.shape

    def plane(s):
        return lax.rem(e + s, n_e)

    def remote(src, dst, send, recv, j):
        return pltpu.make_async_remote_copy(
            src_ref=src, dst_ref=dst, send_sem=send, recv_sem=recv,
            device_id={"expert": j}, device_id_type=MESH)

    def load(c):
        return pltpu.make_async_copy(first.at[c], weights.at[c], w_sem.at[c])

    for c in range(tiles):
        load(c).start()
    barrier = pltpu.get_barrier_semaphore()
    for s in range(1, n_e):
        pl.semaphore_signal(barrier, inc=1, device_id={"expert": plane(s)}, device_id_type=MESH)
    pl.semaphore_wait(barrier, n_e - 1)

    own = pltpu.make_async_copy(d_gate.at[e], gate_back.at[e], own_sem)
    own.start()

    def gate_out(s):
        j = plane(s)
        return remote(d_gate.at[j], gate_back.at[e], g_send.at[s], g_recv.at[e], j)

    def near_out(c):
        return remote(part.at[c, :, 1 - core], near.at[c], n_send.at[c], n_recv.at[c], partner)

    def part_out(c, s):
        k = lax.rem(seat + s, pairs)
        return remote(pair.at[c, k], got.at[c, seat], p_send.at[c, s], p_recv.at[c, seat],
                      2 * k + core)

    for s in range(1, n_e):
        gate_out(s).start()

    def compute(c):
        load(c).wait()
        value = lax.dot_general(
            d_pre[...], weights[c], (((1,), (1,)), ((), ())), preferred_element_type=F32)
        part[c] = value.astype(BF16).reshape(pairs, 2, -1, tile)

    def combine(c):
        near_out(c).wait_recv()
        pair[c] = (part[c, :, core].astype(F32) + near[c].astype(F32)).astype(BF16)

    def send(c):
        for s in range(1, pairs):
            part_out(c, s).start()

    compute(0)
    near_out(0).start()
    compute(1)
    combine(0)

    @pl.loop(2, tiles)
    def _(c):
        near_out(c - 1).start()
        send(c - 2)
        compute(c)
        combine(c - 1)

    near_out(tiles - 1).start()
    send(tiles - 2)
    combine(tiles - 1)
    send(tiles - 1)

    @pl.loop(0, tiles)
    def _(c):
        total = pair[c, seat].astype(F32)
        for s in range(1, pairs):
            k = lax.rem(seat + s, pairs)
            remote(pair.at[c, k], got.at[c, k], p_send.at[c, 0], p_recv.at[c, k],
                   2 * k + core).wait_recv()
            total = total + got[c, k].astype(F32)
        d_trunk[:, pl.ds(pl.multiple_of(c * tile, tile), tile)] = total.astype(BF16)

    own.wait()
    for s in range(1, n_e):
        j = plane(s)
        remote(d_gate.at[j], gate_back.at[j], g_send.at[0], g_recv.at[j], j).wait_recv()
    for s in range(1, n_e):
        gate_out(s).wait_send()

    @pl.loop(0, tiles)
    def _(c):
        near_out(c).wait_send()
        for s in range(1, pairs):
            part_out(c, s).wait_send()


def return_all(d_pre, first, d_gate):
    n_e = lax.axis_size("expert")
    tile = 512
    depth, width = first.shape
    tiles = depth // tile
    share = d_pre.shape[0] // n_e
    hbm = pl.BlockSpec(memory_space=pltpu.HBM)
    vmem = pl.BlockSpec(memory_space=pltpu.VMEM)
    dma = pltpu.SemaphoreType.DMA
    return pl.pallas_call(
        functools.partial(return_kernel, n_e),
        out_shape=(
            jax.ShapeDtypeStruct((share, depth), BF16),
            jax.ShapeDtypeStruct(d_gate.shape, F32),
        ),
        in_specs=[vmem, hbm, vmem],
        out_specs=(vmem, vmem),
        scratch_shapes=[
            pltpu.VMEM((tiles, tile, width), BF16),
            pltpu.VMEM((tiles, n_e // 2, 2, share, tile), BF16),
            pltpu.VMEM((tiles, n_e // 2, share, tile), BF16),
            pltpu.VMEM((tiles, n_e // 2, share, tile), BF16),
            pltpu.VMEM((tiles, n_e // 2, share, tile), BF16),
            dma((tiles,)), dma((tiles,)), dma((tiles,)),
            dma((tiles, n_e // 2)), dma((tiles, n_e // 2)),
            dma((n_e,)), dma((n_e,)), dma,
        ],
        compiler_params=pltpu.CompilerParams(
            collective_id=1, has_side_effects=True, vmem_limit_bytes=48 * 1024 * 1024),
    )(d_pre, first.reshape(tiles, tile, width), d_gate)


def on_device(trunk, w_first, w_second, gates, d_mixed):
    rank = lax.axis_index("dp")
    first = w_first[0]
    second = w_second[0]
    gate_here = gates[0]
    n_dp = lax.axis_size("dp")
    depth = first.shape[0] // n_dp
    units = second.shape[0] // n_dp
    group = gate_here.shape[1]

    n_e = lax.axis_size("expert")
    gate_parts = gate_here.T.astype(F32).reshape(n_e, -1, gate_here.shape[0])
    rows_all, d_output_all, pre, gates_each, outs_each = gather_all(
        trunk, gate_parts, jnp.transpose(d_mixed, (1, 0, 2)), first, second)
    rows_all = rows_all.reshape(-1, trunk.shape[1])
    d_output_all = d_output_all.reshape(-1, second.shape[1])
    pre = pre.reshape(-1, first.shape[1])
    gates_each = gates_each.astype(BF16)
    d_hidden = lax.dot_general(
        d_output_all, second, (((1,), (1,)), ((), ())), preferred_element_type=F32
    )
    sig = jax.nn.sigmoid(pre)
    d_pre = (d_hidden * sig * (1.0 + pre * (1.0 - sig))).astype(BF16)
    d_pre_here = lax.dynamic_slice_in_dim(d_pre, rank * group, group, 0)
    mixed = jnp.einsum(
        "ert,ero->rto", gates_each, outs_each, preferred_element_type=F32
    ).astype(BF16)
    d_gate_each = jnp.einsum(
        "rto,ero->ert", d_mixed, outs_each, preferred_element_type=F32
    ).astype(BF16)
    d_trunk, back_gate = return_all(d_pre_here, first, d_gate_each.astype(F32))
    d_gate = back_gate.reshape(group, -1).T.astype(BF16)[None]

    columns = lax.dynamic_slice_in_dim(rows_all, rank * depth, depth, 1)
    d_first = lax.dot_general(
        columns, d_pre, (((0,), (0,)), ((), ())), preferred_element_type=F32
    ).astype(BF16)
    some_pre = lax.dynamic_slice_in_dim(pre, rank * units, units, 1)
    some_hidden = jax.nn.silu(some_pre).astype(BF16)
    d_second = lax.dot_general(
        some_hidden, d_output_all, (((0,), (0,)), ((), ())), preferred_element_type=F32
    ).astype(BF16)
    return (mixed, d_trunk, d_gate, d_first[None], d_second[None])


SIDE, LINE, LANES = 2, 4, 128
VMEM_BYTES = 62 * 1024 * 1024


def tiled(count, body, hooks=()):
    @pl.loop(0, count)
    def _(c):
        body(c)
        for at, hook in hooks:
            pl.when(c == at)(hook)


def step_kernel(n_e, n_d, trunk, gates, cot_in, first, second,
                columns_out, d_out_out, d_pre_out, units_out, mixed_out, d_trunk_out, back_out_ref,
                rows, d_out, d_pre, some_hidden, mixed, d_trunk, gate_back, gate_in, gate_piece,
                weights, later, turned, cot, gate_each, mix, piece, tall, hidden, made, outs, d_gate,
                part, near, pair, got,
                load_sem, own_sem, g_send, g_recv, t_send, t_recv, o_send, o_recv, z_send, z_recv,
                m_send, m_recv, n_send, n_recv, p_send, p_recv, b_send, b_recv, out_sem):
    e = lax.axis_index("expert")
    z = lax.axis_index("dp")
    core, seat, pairs = lax.rem(e, 2), e // 2, n_e // 2
    partner = e + 1 - 2 * core
    side, up = lax.rem(seat, SIDE), seat // SIDE
    across = e + 2 - 4 * side
    over = e + 2 * SIDE - 4 * SIDE * up
    corner = across + over - e
    bridge = across * (1 - core) + over * core
    other = across * core + over * (1 - core)
    middle = (z * (n_d - 1 - z)) // 2
    inner = middle == 1
    mate = z + 1 - 2 * lax.rem(z, 2)
    mirror = n_d - 1 - z
    skip = lax.rem(z + 2, n_d)
    order = [z, mate, middle * mirror + (1 - middle) * skip, middle * skip + (1 - middle) * mirror]
    tasks = cot.shape[0] // rows.shape[2]
    share, depth = rows.shape[2], rows.shape[3]
    width = tall.shape[2]
    group = n_e * share
    units = some_hidden.shape[2]
    part_depth = depth // n_d
    depth_here = pl.ds(pl.multiple_of(z * part_depth, part_depth), part_depth)

    def plane(s):
        return lax.rem(e + s, n_e)

    def remote(src, dst, send, recv, where):
        return pltpu.make_async_remote_copy(
            src_ref=src, dst_ref=dst, send_sem=send, recv_sem=recv,
            device_id=where, device_id_type=MESH)

    def load(k):
        src, dst = [(second, later), (cot_in, cot), (first, weights), (gates, gate_in)][k]
        return pltpu.make_async_copy(src, dst, load_sem.at[k])

    def own(k):
        src, dst = [(gate_piece.at[e], gate_each.at[e]), (trunk, rows.at[z, e]),
                    (piece.at[e], d_out.at[z, e]), (made.at[e], outs.at[e]),
                    (d_gate.at[e], gate_back.at[e])][k]
        return pltpu.make_async_copy(src, dst, own_sem.at[k])

    def at_plane(j):
        return {"expert": j}

    def gate_out(s):
        j = plane(s)
        return remote(gate_piece.at[j], gate_each.at[e], g_send.at[s], g_recv.at[e], at_plane(j))

    def trunk_out(g, k):
        zi = order[g]
        j, where = [
            (e, at_plane(across)), (e, at_plane(over)), (e, at_plane(partner)),
            (bridge, at_plane(over * (1 - core) + across * core)),
            (bridge, at_plane(partner)), (other, at_plane(partner)), (corner, at_plane(partner)),
            (e, {"dp": mate}), (e, {"dp": mirror})][k]
        src = trunk if g == 0 and k in (0, 1, 2, 7, 8) else rows.at[zi, j]
        return remote(src, rows.at[zi, j], t_send.at[g, k], t_recv.at[zi, j], where)

    def trunk_in(g, j):
        zi = order[g]
        remote(trunk, rows.at[zi, j], t_send.at[0, 0], t_recv.at[zi, j],
               at_plane(partner)).wait_recv()

    def piece_out(s):
        j = plane(s)
        return remote(piece.at[j], d_out.at[z, e], o_send.at[s], o_recv.at[e], at_plane(j))

    def half(zi, h):
        return d_out.at[zi, h * (n_e // 2):(h + 1) * (n_e // 2)]

    def line_out(g, k, h):
        zi = order[g]
        return remote(half(zi, h), half(zi, h), z_send.at[g, k, h], z_recv.at[zi, h],
                      {"dp": mate if k == 0 else mirror})

    def keep(k):
        src, dst = ([(rows.at[zi, :, :, depth_here], columns_out.at[zi]) for zi in order]
                    + [(d_pre.at[zi], d_pre_out.at[zi]) for zi in order]
                    + [(d_out, d_out_out), (some_hidden, units_out), (mixed, mixed_out),
                       (d_trunk, d_trunk_out), (gate_back, back_out_ref)])[k]
        return pltpu.make_async_copy(src, dst, out_sem.at[k])

    def made_out(s):
        j = plane(s)
        return remote(made.at[j], outs.at[e], m_send.at[s], m_recv.at[e], at_plane(j))

    def back_out(s):
        j = plane(s)
        return remote(d_gate.at[j], gate_back.at[e], b_send.at[s], b_recv.at[e], at_plane(j))

    def near_out(c):
        return remote(part.at[c, :, 1 - core], near.at[c], n_send.at[c], n_recv.at[c],
                      at_plane(partner))

    def part_out(c, s):
        k = lax.rem(seat + s, pairs)
        return remote(pair.at[c, k], got.at[c, seat], p_send.at[c, s], p_recv.at[c, seat],
                      at_plane(2 * k + core))

    def spread(g):
        for k in range(3):
            trunk_out(g, k).start()

    def bridge_on(g):
        trunk_in(g, bridge)
        trunk_out(g, 3).start()
        trunk_out(g, 4).start()
        trunk_in(g, other)
        trunk_out(g, 5).start()

    def corner_on(g):
        trunk_in(g, corner)
        trunk_out(g, 6).start()

    def complete(g):
        for shift in (0, across - e, over - e, corner - e):
            trunk_in(g, partner + shift)

    def arrive(g):
        trunk_in(g, e)
        if g == 1:
            pl.when(inner)(lambda: trunk_out(1, 8).start())
        else:
            pl.when(inner)(lambda: trunk_out(g, 7).start())

    def line_arrive(g, h):
        zi = order[g]
        remote(half(zi, h), half(zi, h), z_send.at[0, 0, h], z_recv.at[zi, h],
               {"dp": mate}).wait_recv()
        pl.when(inner)(lambda: line_out(g, 1 if g == 1 else 0, h).start())

    def in_middle(call, *g):
        pl.when(inner)(lambda: call(*g))

    def at_end(call, *g):
        pl.when(middle == 0)(lambda: call(*g))

    for k in (3, 1, 0, 2):
        load(k).start()
    barrier = pltpu.get_barrier_semaphore()
    for s in range(1, n_e):
        pl.semaphore_signal(barrier, inc=1, device_id=at_plane(plane(s)), device_id_type=MESH)
    for i in range(1, n_d):
        pl.semaphore_signal(barrier, inc=1, device_id={"dp": lax.rem(z + i, n_d)},
                            device_id_type=MESH)
    load(3).wait()
    task_eye = jnp.where(
        lax.broadcasted_iota(jnp.int32, (tasks, LANES), 0)
        == lax.broadcasted_iota(jnp.int32, (tasks, LANES), 1), 1.0, 0.0).astype(BF16)
    gate_piece[...] = lax.dot_general(
        gate_in[...], task_eye, (((0,), (0,)), ((), ())),
        preferred_element_type=F32).reshape(gate_piece.shape)
    own(0).start()
    own(1).start()
    pl.semaphore_wait(barrier, n_e - 1 + n_d - 1)

    for s in range(1, n_e):
        gate_out(s).start()
    trunk_out(0, 7).start()
    pl.when(inner)(lambda: trunk_out(0, 8).start())
    spread(0)

    def turn(low, high):
        @pl.loop(low, high)
        def _(c):
            here = pl.ds(pl.multiple_of(c * 256, 256), 256)
            turned[:, here] = later[here, :].T

    turns = width // 256
    load(0).wait()
    turn(0, turns // 2)

    def task_of():
        shape = (LANES, share * tasks)
        return jnp.where(
            lax.broadcasted_iota(jnp.int32, shape, 0)
            == lax.rem(lax.broadcasted_iota(jnp.int32, shape, 1), tasks), 1.0, 0.0).astype(BF16)

    def same_sample():
        shape = (n_e, share, share * tasks)
        match = (lax.broadcasted_iota(jnp.int32, shape, 1)
                 == lax.div(lax.broadcasted_iota(jnp.int32, shape, 2), tasks))
        return jnp.where(match, 1.0, 0.0).reshape(group, share * tasks)

    for s in range(1, n_e):
        j = plane(s)
        remote(gate_piece.at[j], gate_each.at[j], g_send.at[0], g_recv.at[j],
               at_plane(j)).wait_recv()
    own(0).wait()
    load(1).wait()
    each = gate_each[...].reshape(group, LANES).astype(BF16)
    mix[...] = (jnp.dot(each, task_of(), preferred_element_type=F32)
                * same_sample()).astype(BF16)
    piece[...] = jnp.dot(mix[...], cot[...], preferred_element_type=F32).astype(BF16).reshape(
        piece.shape)
    for s in range(1, n_e):
        piece_out(s).start()
    own(2).start()

    turn(turns // 2, turns)
    bridge_on(0)
    arrive(1)
    in_middle(arrive, 2)
    for s in range(1, n_e):
        j = plane(s)
        remote(piece.at[j], d_out.at[z, j], o_send.at[0], o_recv.at[j], at_plane(j)).wait_recv()
    own(2).wait()
    for h in range(2):
        line_out(0, 0, h).start()
        in_middle(lambda: line_out(0, 1, h).start())

    tile = 512

    broad = 2 * tile

    def part_of(c, span=tile):
        return pl.ds(pl.multiple_of(c * span, span), span)

    def back_hidden(g, c, span=tile):
        left = d_out[order[g]].reshape(group, d_out.shape[3])
        return jnp.dot(left, turned[:, part_of(c, span)], preferred_element_type=F32)

    def forward_pre(g, c, span=tile):
        left = rows[order[g]].reshape(group, depth)
        return jnp.dot(left, weights[:, part_of(c, span)], preferred_element_type=F32)

    def store_d_pre(g, c, d_hidden, value, span=tile):
        sig = jax.nn.sigmoid(value)
        d_pre[order[g], :, part_of(c, span)] = (
            d_hidden * sig * (1.0 + value * (1.0 - sig))).astype(BF16)

    def first_hidden(c):
        tall[0, :, part_of(c, broad)] = back_hidden(0, c, broad)

    def first_pre(c):
        value = forward_pre(0, c)
        store_d_pre(0, c, tall[0, :, part_of(c)], value)
        hidden[:, part_of(c)] = (value * jax.nn.sigmoid(value)).astype(BF16)

    def later_pre(g, span=tile):
        def body(c):
            tall[g, :, part_of(c, span)] = forward_pre(g, c, span)
        return body

    def later_hidden(g):
        def body(c):
            store_d_pre(g, c, back_hidden(g, c), tall[g, :, part_of(c)])
        return body

    units_here = pl.ds(pl.multiple_of(z * units, units), units)

    def keep_units(g):
        value = tall[g, :, units_here]
        some_hidden[order[g]] = (value * jax.nn.sigmoid(value)).astype(BF16)

    tiled(width // broad, first_hidden)
    spread(1)
    corner_on(0)
    in_middle(arrive, 3)
    own(1).wait()
    complete(0)
    load(2).wait()

    def hook_a():
        at_end(arrive, 2)
        spread(2)

    tiled(width // tile, first_pre, [(2, hook_a)])
    keep(0).start()
    keep(4).start()
    some_hidden[z] = hidden[:, units_here]


    def compute(c):
        value = lax.dot_general(d_pre[z], weights[part_of(c), :], (((1,), (1,)), ((), ())),
                                preferred_element_type=F32)
        part[c] = value.astype(BF16).reshape(pairs, 2, share, tile)

    def combine(c):
        near_out(c).wait_recv()
        pair[c] = (part[c, :, core].astype(F32) + near[c].astype(F32)).astype(BF16)

    def send_parts(low, high):
        @pl.loop(low, high)
        def _(c):
            for s in range(1, pairs):
                part_out(c, s).start()

    count = depth // tile
    compute(0)
    near_out(0).start()
    bridge_on(1)
    compute(1)
    combine(0)

    def hook_b():
        at_end(arrive, 3)
        at_end(spread, 3)

    def hook_c():
        for h in range(2):
            line_arrive(1, h)
            in_middle(line_arrive, 2, h)

    hooks = [(2, lambda: in_middle(spread, 3)), (4, hook_b), (6, lambda: bridge_on(2)),
             (7, lambda: corner_on(1))]

    @pl.loop(2, count)
    def _(c):
        near_out(c - 1).start()
        compute(c)
        combine(c - 1)
        for at, hook in hooks:
            pl.when(c == at)(hook)

    near_out(count - 1).start()

    def first_output(c):
        value = jnp.dot(hidden[...], later[:, part_of(c)], preferred_element_type=F32)
        made[:, :, part_of(c)] = value.astype(BF16).reshape(n_e, share, tile)

    tiled(made.shape[2] // tile, first_output)
    own(3).start()
    complete(1)
    keep(1).start()
    tiled(width // tile, later_pre(1), [(0, lambda: combine(count - 1)), (1, hook_c),
                                        (2, lambda: bridge_on(3))])
    keep_units(1)
    tiled(width // tile, later_hidden(1), [(1, lambda: corner_on(2))])
    send_parts(0, count // 2)
    keep(5).start()
    complete(2)
    keep(2).start()

    def hook_d():
        for h in range(2):
            in_middle(line_arrive, 3, h)

    def hook_e():
        for s in range(1, n_e):
            made_out(s).start()

    tiled(width // tile, later_pre(2), [(2, hook_e)])
    hook_d()
    keep_units(2)
    send_parts(count // 2, count)
    for h in range(2):
        at_end(line_arrive, 2, h)
    tiled(width // tile, later_hidden(2), [(1, lambda: corner_on(3))])
    keep(6).start()
    complete(3)
    keep(3).start()
    tiled(width // broad, later_pre(3, broad))
    keep_units(3)
    keep(9).start()

    own(3).wait()
    for s in range(1, n_e):
        j = plane(s)
        remote(made.at[j], outs.at[j], m_send.at[0], m_recv.at[j], at_plane(j)).wait_recv()
    each_out = outs[...].reshape(group, outs.shape[2])
    product = lax.dot_general(each_out, cot[...], (((1,), (1,)), ((), ())),
                              preferred_element_type=F32)
    product = (product * same_sample()).astype(BF16)
    d_gate[...] = lax.dot_general(product, task_of(), (((1,), (1,)), ((), ())),
                                  preferred_element_type=F32).reshape(d_gate.shape)
    own(4).start()
    for s in range(1, n_e):
        back_out(s).start()
    mixed[...] = lax.dot_general(mix[...], each_out, (((0,), (0,)), ((), ())),
                                 preferred_element_type=F32).astype(BF16)

    keep(10).start()
    at_end(line_arrive, 3, 0)
    at_end(line_arrive, 3, 1)
    keep(8).start()
    tiled(width // tile, later_hidden(3))
    keep(7).start()

    @pl.loop(0, count)
    def _(c):
        total = pair[c, seat].astype(F32)
        for s in range(1, pairs):
            k = lax.rem(seat + s, pairs)
            remote(pair.at[c, k], got.at[c, k], p_send.at[c, 0], p_recv.at[c, k],
                   at_plane(2 * k + core)).wait_recv()
            total = total + got[c, k].astype(F32)
        d_trunk[:, part_of(c)] = total.astype(BF16)

    keep(11).start()

    own(4).wait()
    for s in range(1, n_e):
        j = plane(s)
        remote(d_gate.at[j], gate_back.at[j], b_send.at[0], b_recv.at[j], at_plane(j)).wait_recv()
    for s in range(1, n_e):
        gate_out(s).wait_send()
        piece_out(s).wait_send()
        made_out(s).wait_send()
        back_out(s).wait_send()
    for g in range(n_d):
        for k in range(7):
            trunk_out(g, k).wait_send()
    keep(12).start()
    trunk_out(0, 7).wait_send()
    for h in range(2):
        line_out(0, 0, h).wait_send()

    @pl.when(inner)
    def _():
        trunk_out(0, 8).wait_send()
        trunk_out(1, 8).wait_send()
        for g in range(2, n_d):
            trunk_out(g, 7).wait_send()
        for h in range(2):
            line_out(0, 1, h).wait_send()
            line_out(1, 1, h).wait_send()
            for g in range(2, n_d):
                line_out(g, 0, h).wait_send()

    @pl.loop(0, count)
    def _(c):
        near_out(c).wait_send()
        for s in range(1, pairs):
            part_out(c, s).wait_send()

    for k in range(13):
        keep(k).wait()


def step_all(trunk, gates, cot, first, second):
    n_e, n_d = lax.axis_size("expert"), lax.axis_size("dp")
    share, depth = trunk.shape
    width = first.shape[1]
    out = second.shape[1]
    group = n_e * share
    count, pairs, tile = depth // 512, n_e // 2, 512
    hbm = pl.BlockSpec(memory_space=pltpu.HBM)
    dma = pltpu.SemaphoreType.DMA
    gate_shape = (n_e, share, LANES)
    return pl.pallas_call(
        functools.partial(step_kernel, n_e, n_d),
        out_shape=(
            jax.ShapeDtypeStruct((n_d, n_e, share, depth // n_d), BF16),
            jax.ShapeDtypeStruct((n_d, n_e, share, out), BF16),
            jax.ShapeDtypeStruct((n_d, group, width), BF16),
            jax.ShapeDtypeStruct((n_d, group, width // n_d), BF16),
            jax.ShapeDtypeStruct((cot.shape[0], out), BF16),
            jax.ShapeDtypeStruct((share, depth), BF16),
            jax.ShapeDtypeStruct(gate_shape, F32),
        ),
        in_specs=[hbm] * 5,
        out_specs=(hbm,) * 7,
        scratch_shapes=[
            pltpu.VMEM((n_d, n_e, share, depth), BF16),
            pltpu.VMEM((n_d, n_e, share, out), BF16),
            pltpu.VMEM((n_d, group, width), BF16),
            pltpu.VMEM((n_d, group, width // n_d), BF16),
            pltpu.VMEM((cot.shape[0], out), BF16),
            pltpu.VMEM((share, depth), BF16),
            pltpu.VMEM(gate_shape, F32),
            pltpu.VMEM(gates.shape, BF16),
            pltpu.VMEM(gate_shape, F32),
            pltpu.VMEM(first.shape, BF16),
            pltpu.VMEM(second.shape, BF16),
            pltpu.VMEM(second.shape[::-1], BF16),
            pltpu.VMEM(cot.shape, BF16),
            pltpu.VMEM(gate_shape, F32),
            pltpu.VMEM((group, cot.shape[0]), BF16),
            pltpu.VMEM((n_e, share, out), BF16),
            pltpu.VMEM((n_d, group, width), F32),
            pltpu.VMEM((group, width), BF16),
            pltpu.VMEM((n_e, share, out), BF16),
            pltpu.VMEM((n_e, share, out), BF16),
            pltpu.VMEM(gate_shape, F32),
            pltpu.VMEM((count, pairs, 2, share, tile), BF16),
            pltpu.VMEM((count, pairs, share, tile), BF16),
            pltpu.VMEM((count, pairs, share, tile), BF16),
            pltpu.VMEM((count, pairs, share, tile), BF16),
            dma((4,)), dma((5,)),
            dma((n_e,)), dma((n_e,)),
            dma((n_d, 9)), dma((n_d, n_e)),
            dma((n_e,)), dma((n_e,)),
            dma((n_d, 2, 2)), dma((n_d, 2)),
            dma((n_e,)), dma((n_e,)),
            dma((count,)), dma((count,)),
            dma((count, pairs)), dma((count, pairs)),
            dma((n_e,)), dma((n_e,)), dma((13,)),
        ],
        compiler_params=pltpu.CompilerParams(
            collective_id=2, has_side_effects=True, vmem_limit_bytes=VMEM_BYTES),
    )(trunk, gates, cot, first, second)


def finish_kernel(columns, d_pre, units, d_out, mixed, d_trunk, back,
                  d_first, d_second, mixed_out, d_trunk_out, d_gate,
                  columns_v, d_pre_v, units_v, d_out_v, mixed_v, d_trunk_v, back_v,
                  first_v, second_v, gate_v, in_sem, out_sem, tile_sem, wide_sem):
    pairs = [(units, units_v), (d_out, d_out_v), (columns, columns_v), (mixed, mixed_v),
             (d_trunk, d_trunk_v), (back, back_v)]
    steps = d_pre.shape[0]

    def take(k):
        return pltpu.make_async_copy(*pairs[k], in_sem.at[k])

    def wide(k):
        return pltpu.make_async_copy(d_pre.at[k], d_pre_v.at[k], wide_sem.at[k])

    def give(k):
        src, dst = [(second_v, d_second), (mixed_v, mixed_out), (d_trunk_v, d_trunk_out),
                    (gate_v, d_gate)][k]
        return pltpu.make_async_copy(src, dst, out_sem.at[k])

    for k in range(3):
        take(k).start()
    for k in range(steps):
        wide(k).start()
    for k in range(3, len(pairs)):
        take(k).start()
    take(0).wait()
    take(1).wait()
    second_v[...] = lax.dot_general(
        units_v[...], d_out_v[...], (((0,), (0,)), ((), ())),
        preferred_element_type=F32).astype(BF16)
    give(0).start()
    take(2).wait()
    for k in range(steps):
        wide(k).wait()
    tile = first_v.shape[1]
    count = first_v.shape[0]

    def store(c):
        here = pl.ds(pl.multiple_of(c * tile, tile), tile)
        return pltpu.make_async_copy(first_v.at[c], d_first.at[here], tile_sem.at[c])

    @pl.loop(0, count)
    def _(c):
        here = pl.ds(pl.multiple_of(c * tile, tile), tile)
        right = d_pre_v[...].reshape(-1, d_pre_v.shape[2])
        first_v[c] = lax.dot_general(
            columns_v[:, here], right, (((0,), (0,)), ((), ())),
            preferred_element_type=F32).astype(BF16)
        store(c).start()

        @pl.when(c == 0)
        def _():
            take(3).wait()
            give(1).start()
            take(4).wait()
            give(2).start()
            take(5).wait()
            tasks = d_gate.shape[0]
            eye = jnp.where(
                lax.broadcasted_iota(jnp.int32, (tasks, LANES), 0)
                == lax.broadcasted_iota(jnp.int32, (tasks, LANES), 1), 1.0, 0.0).astype(BF16)
            gate_v[...] = lax.dot_general(
                eye, back_v[...].astype(BF16), (((1,), (1,)), ((), ())),
                preferred_element_type=F32).astype(BF16)
            give(3).start()

    for k in range(4):
        give(k).wait()

    @pl.loop(0, count)
    def _(c):
        store(c).wait()


def finish_all(columns, d_pre, units, d_out, mixed, d_trunk, back, tasks):
    hbm = pl.BlockSpec(memory_space=pltpu.HBM)
    dma = pltpu.SemaphoreType.DMA
    rows, depth = columns.shape
    steps, group, width = d_pre.shape
    unit, out = units.shape[1], d_out.shape[1]
    tile = 256
    ins = (columns, d_pre, units, d_out, mixed, d_trunk, back)
    return pl.pallas_call(
        finish_kernel,
        out_shape=(
            jax.ShapeDtypeStruct((depth, width), BF16),
            jax.ShapeDtypeStruct((unit, out), BF16),
            jax.ShapeDtypeStruct(mixed.shape, BF16),
            jax.ShapeDtypeStruct(d_trunk.shape, BF16),
            jax.ShapeDtypeStruct((tasks, back.shape[0]), BF16),
        ),
        in_specs=[hbm] * 7,
        out_specs=(hbm,) * 5,
        scratch_shapes=[pltpu.VMEM(x.shape, x.dtype) for x in ins] + [
            pltpu.VMEM((depth // tile, tile, width), BF16),
            pltpu.VMEM((unit, out), BF16),
            pltpu.VMEM((tasks, back.shape[0]), BF16),
            dma((6,)), dma((4,)), dma((depth // tile,)), dma((steps,)),
        ],
        compiler_params=pltpu.CompilerParams(vmem_limit_bytes=VMEM_BYTES),
    )(*ins)


def on_square(trunk, w_first, w_second, gates, d_mixed):
    first, second, gate_here = w_first[0], w_second[0], gates[0]
    tasks, group = gate_here.shape
    columns, d_out, d_pre, units, mixed, d_trunk, back = step_all(
        trunk, gate_here, d_mixed.reshape(-1, d_mixed.shape[2]), first, second)
    d_first, d_second, mixed, d_trunk, d_gate = finish_all(
        columns.reshape(-1, columns.shape[3]), d_pre, units.reshape(-1, units.shape[2]),
        d_out.reshape(-1, d_out.shape[3]), mixed, d_trunk, back.reshape(group, -1), tasks)
    return (mixed.reshape(d_mixed.shape), d_trunk, d_gate[None], d_first[None], d_second[None])


def solution(mesh):
    in_specs = (
        P(("dp", "expert"), None),
        P("expert", None, None),
        P("expert", None, None),
        P("expert", None, "dp"),
        P(("dp", "expert"), None, None),
    )
    out_specs = (
        P(("dp", "expert"), None, None),
        P(("dp", "expert"), None),
        P("expert", None, "dp"),
        P("expert", "dp", None),
        P("expert", "dp", None),
    )
    fits = mesh.shape["expert"] == 2 * SIDE * SIDE and mesh.shape["dp"] == LINE
    return jax.shard_map(
        on_square if fits else on_device, mesh=mesh, in_specs=in_specs, out_specs=out_specs, check_vma=False
    )
```

```python
import functools

import jax
import jax.numpy as jnp
from jax import lax
from jax.experimental import pallas as pl
from jax.experimental.pallas import tpu as pltpu
from jax.sharding import PartitionSpec as P

F32 = jnp.float32
BF16 = jnp.bfloat16


MESH = pl.DeviceIdType.MESH


def gather_kernel(n_e, n_d, trunk, gates, cot, first, second, rows, d_out, pre, gate_each,
                  outs, weights, later, hidden, made, m_send, m_recv, later_sem, piece, block, tall, w_sem, load_sem, store_sem,
                  g_send, g_recv, t_send, t_recv, o_send, o_recv, z_send, z_recv,
                  own_sem):
    e = lax.axis_index("expert")
    z = lax.axis_index("dp")
    partner = e + 1 - 2 * lax.rem(e, 2)
    pairs = n_e // 2

    def plane(s):
        return lax.rem(e + s, n_e)

    def along(i):
        return lax.rem(z + i, n_d)

    def remote(src, dst, send, recv, where):
        return pltpu.make_async_remote_copy(
            src_ref=src, dst_ref=dst, send_sem=send, recv_sem=recv,
            device_id=where, device_id_type=MESH)

    load_weights = pltpu.make_async_copy(first, weights, w_sem)
    load_weights.start()
    load_later = pltpu.make_async_copy(second, later, later_sem)
    load_later.start()

    barrier = pltpu.get_barrier_semaphore()
    for s in range(1, n_e):
        pl.semaphore_signal(barrier, inc=1, device_id={"expert": plane(s)}, device_id_type=MESH)
    for i in range(1, n_d):
        pl.semaphore_signal(barrier, inc=1, device_id={"dp": along(i)}, device_id_type=MESH)
    pl.semaphore_wait(barrier, n_e - 1 + n_d - 1)

    sent = []

    def go(copy):
        copy.start()
        sent.append(copy)

    for s in range(1, n_e):
        j = plane(s)
        go(remote(gates.at[j], gate_each.at[e], g_send.at[s], g_recv.at[e], {"expert": j}))
    own_gate = pltpu.make_async_copy(gates.at[e], gate_each.at[e], own_sem.at[0])
    own_gate.start()
    own_rows = pltpu.make_async_copy(trunk, rows.at[z, e], own_sem.at[1])
    own_rows.start()

    def spread(i):
        zi = along(i)
        src = trunk if i == 0 else rows.at[zi, e]
        for s in range(1, pairs):
            go(remote(src, rows.at[zi, e], t_send.at[i, s], t_recv.at[zi, e],
                      {"expert": plane(2 * s)}))
        go(remote(src, rows.at[zi, e], t_send.at[i, 0], t_recv.at[zi, e], {"expert": partner}))

    def arrived(zi, j):
        remote(trunk, rows.at[zi, j], t_send.at[0, 0], t_recv.at[zi, j],
               {"expert": partner}).wait_recv()

    for i in range(1, n_d):
        go(remote(trunk, rows.at[z, e], t_send.at[i, n_e - 1], t_recv.at[z, e], {"dp": along(i)}))
    spread(0)

    for s in range(1, n_e):
        j = plane(s)
        remote(gates.at[j], gate_each.at[j], g_send.at[0], g_recv.at[j], {"expert": j}).wait_recv()
    own_gate.wait()
    tasks = cot.shape[0]

    @pl.loop(0, n_e)
    def _(j):
        weight = gate_each[j]
        total = weight[:, 0:1] * cot[0].astype(F32)
        for t in range(1, tasks):
            total = total + weight[:, t:t + 1] * cot[t].astype(F32)
        piece[j] = total.astype(BF16)

    own_piece = pltpu.make_async_copy(piece.at[e], d_out.at[z, e], own_sem.at[2])
    own_piece.start()
    for s in range(1, n_e):
        j = plane(s)
        go(remote(piece.at[j], d_out.at[z, e], o_send.at[s], o_recv.at[e], {"expert": j}))

    def send_outputs():
        own_made.start()
        for s in range(1, n_e):
            j = plane(s)
            go(remote(made.at[j], outs.at[e], m_send.at[s], m_recv.at[e], {"expert": j}))

    own_made = pltpu.make_async_copy(made.at[e], outs.at[e], own_sem.at[3])
    stores = []
    for i in range(n_d):
        zi = along(i)
        if i + 1 < n_d:
            arrived(along(i + 1), e)
            spread(i + 1)
        if i == 1:
            send_outputs()
        if i == 0:
            for s in range(1, n_e):
                j = plane(s)
                remote(piece.at[j], d_out.at[z, j], o_send.at[0], o_recv.at[j],
                       {"expert": j}).wait_recv()
            own_piece.wait()
            for k in range(1, n_d):
                go(remote(d_out.at[z], d_out.at[z], z_send.at[k], z_recv.at[z], {"dp": along(k)}))
            own_rows.wait()
        for s in range(1, pairs):
            j = plane(2 * s)
            arrived(zi, j)
            go(remote(rows.at[zi, j], rows.at[zi, j], t_send.at[i, pairs - 1 + s],
                      t_recv.at[zi, j], {"expert": partner}))
        for s in range(pairs):
            arrived(zi, lax.rem(partner + 2 * s, n_e))
        load = pltpu.make_async_copy(rows.at[zi], block, load_sem)
        load.start()
        if i == 0:
            load_weights.wait()
        else:
            stores[-1].wait()
        load.wait()
        height = block.shape[0] * block.shape[1]
        tile = 256
        left = block[...].reshape(height, block.shape[2])

        @pl.loop(0, tall.shape[1] // tile)
        def _(c):
            here = pl.ds(pl.multiple_of(c * tile, tile), tile)
            value = jnp.dot(left, weights[:, here], preferred_element_type=F32)
            tall[:, here] = value
            if i == 0:
                hidden[:, here] = (value * jax.nn.sigmoid(value)).astype(BF16)

        store = pltpu.make_async_copy(tall, pre.at[zi], store_sem)
        store.start()
        stores.append(store)
        if i == 0:
            load_later.wait()

            @pl.loop(0, made.shape[2] // tile)
            def _(c):
                here = pl.ds(pl.multiple_of(c * tile, tile), tile)
                value = jnp.dot(hidden[...], later[:, here], preferred_element_type=F32)
                made[:, :, here] = value.astype(BF16).reshape(n_e, -1, tile)

    stores[-1].wait()
    if n_d == 1:
        send_outputs()
    own_made.wait()
    for s in range(1, n_e):
        j = plane(s)
        remote(made.at[j], outs.at[j], m_send.at[0], m_recv.at[j], {"expert": j}).wait_recv()
    for i in range(1, n_d):
        zi = along(i)
        remote(d_out.at[zi], d_out.at[zi], z_send.at[0], z_recv.at[zi], {"dp": zi}).wait_recv()
    for copy in sent:
        copy.wait_send()


def gather_all(trunk, gates, cot, first, second):
    n_e, n_d = lax.axis_size("expert"), lax.axis_size("dp")
    share, depth = trunk.shape
    width = first.shape[1]
    out = cot.shape[2]
    anywhere = pl.BlockSpec(memory_space=pl.ANY)
    hbm = pl.BlockSpec(memory_space=pltpu.HBM)
    vmem = pl.BlockSpec(memory_space=pltpu.VMEM)
    dma = pltpu.SemaphoreType.DMA
    return pl.pallas_call(
        functools.partial(gather_kernel, n_e, n_d),
        out_shape=(
            jax.ShapeDtypeStruct((n_d, n_e, share, depth), BF16),
            jax.ShapeDtypeStruct((n_d, n_e, share, out), BF16),
            jax.ShapeDtypeStruct((n_d, n_e * share, width), F32),
            jax.ShapeDtypeStruct(gates.shape, F32),
            jax.ShapeDtypeStruct((n_e, share, out), BF16),
        ),
        in_specs=[vmem, vmem, vmem, hbm, hbm],
        out_specs=(hbm, hbm, hbm, vmem, hbm),
        scratch_shapes=[
            pltpu.VMEM(first.shape, BF16),
            pltpu.VMEM(second.shape, BF16),
            pltpu.VMEM((n_e * share, width), BF16),
            pltpu.VMEM((n_e, share, out), BF16),
            dma((n_e,)), dma((n_e,)), dma,
            pltpu.VMEM((n_e, share, out), BF16),
            pltpu.VMEM((n_e, share, depth), BF16),
            pltpu.VMEM((n_e * share, width), F32),
            dma, dma, dma,
            dma((n_e,)), dma((n_e,)),
            dma((n_d, n_e)), dma((n_d, n_e)),
            dma((n_e,)), dma((n_e,)),
            dma((n_d,)), dma((n_d,)),
            dma((4,)),
        ],
        compiler_params=pltpu.CompilerParams(
            collective_id=0, has_side_effects=True, vmem_limit_bytes=48 * 1024 * 1024),
    )(trunk, gates, cot, first, second)


def return_kernel(n_e, d_pre, first, d_gate, d_trunk, gate_back, weights, part, near, pair, got,
                  w_sem, n_send, n_recv, p_send, p_recv, g_send, g_recv, own_sem):
    e = lax.axis_index("expert")
    core, seat, pairs = lax.rem(e, 2), e // 2, n_e // 2
    partner = e + 1 - 2 * core
    tiles, tile, _ = weights.shape

    def plane(s):
        return lax.rem(e + s, n_e)

    def remote(src, dst, send, recv, j):
        return pltpu.make_async_remote_copy(
            src_ref=src, dst_ref=dst, send_sem=send, recv_sem=recv,
            device_id={"expert": j}, device_id_type=MESH)

    def load(c):
        return pltpu.make_async_copy(first.at[c], weights.at[c], w_sem.at[c])

    for c in range(tiles):
        load(c).start()
    barrier = pltpu.get_barrier_semaphore()
    for s in range(1, n_e):
        pl.semaphore_signal(barrier, inc=1, device_id={"expert": plane(s)}, device_id_type=MESH)
    pl.semaphore_wait(barrier, n_e - 1)

    own = pltpu.make_async_copy(d_gate.at[e], gate_back.at[e], own_sem)
    own.start()

    def gate_out(s):
        j = plane(s)
        return remote(d_gate.at[j], gate_back.at[e], g_send.at[s], g_recv.at[e], j)

    def near_out(c):
        return remote(part.at[c, :, 1 - core], near.at[c], n_send.at[c], n_recv.at[c], partner)

    def part_out(c, s):
        k = lax.rem(seat + s, pairs)
        return remote(pair.at[c, k], got.at[c, seat], p_send.at[c, s], p_recv.at[c, seat],
                      2 * k + core)

    for s in range(1, n_e):
        gate_out(s).start()

    def compute(c):
        load(c).wait()
        value = lax.dot_general(
            d_pre[...], weights[c], (((1,), (1,)), ((), ())), preferred_element_type=F32)
        part[c] = value.astype(BF16).reshape(pairs, 2, -1, tile)

    def combine(c):
        near_out(c).wait_recv()
        pair[c] = (part[c, :, core].astype(F32) + near[c].astype(F32)).astype(BF16)

    def send(c):
        for s in range(1, pairs):
            part_out(c, s).start()

    compute(0)
    near_out(0).start()
    compute(1)
    combine(0)

    @pl.loop(2, tiles)
    def _(c):
        near_out(c - 1).start()
        send(c - 2)
        compute(c)
        combine(c - 1)

    near_out(tiles - 1).start()
    send(tiles - 2)
    combine(tiles - 1)
    send(tiles - 1)

    @pl.loop(0, tiles)
    def _(c):
        total = pair[c, seat].astype(F32)
        for s in range(1, pairs):
            k = lax.rem(seat + s, pairs)
            remote(pair.at[c, k], got.at[c, k], p_send.at[c, 0], p_recv.at[c, k],
                   2 * k + core).wait_recv()
            total = total + got[c, k].astype(F32)
        d_trunk[:, pl.ds(pl.multiple_of(c * tile, tile), tile)] = total.astype(BF16)

    own.wait()
    for s in range(1, n_e):
        j = plane(s)
        remote(d_gate.at[j], gate_back.at[j], g_send.at[0], g_recv.at[j], j).wait_recv()
    for s in range(1, n_e):
        gate_out(s).wait_send()

    @pl.loop(0, tiles)
    def _(c):
        near_out(c).wait_send()
        for s in range(1, pairs):
            part_out(c, s).wait_send()


def return_all(d_pre, first, d_gate):
    n_e = lax.axis_size("expert")
    tile = 512
    depth, width = first.shape
    tiles = depth // tile
    share = d_pre.shape[0] // n_e
    hbm = pl.BlockSpec(memory_space=pltpu.HBM)
    vmem = pl.BlockSpec(memory_space=pltpu.VMEM)
    dma = pltpu.SemaphoreType.DMA
    return pl.pallas_call(
        functools.partial(return_kernel, n_e),
        out_shape=(
            jax.ShapeDtypeStruct((share, depth), BF16),
            jax.ShapeDtypeStruct(d_gate.shape, F32),
        ),
        in_specs=[vmem, hbm, vmem],
        out_specs=(vmem, vmem),
        scratch_shapes=[
            pltpu.VMEM((tiles, tile, width), BF16),
            pltpu.VMEM((tiles, n_e // 2, 2, share, tile), BF16),
            pltpu.VMEM((tiles, n_e // 2, share, tile), BF16),
            pltpu.VMEM((tiles, n_e // 2, share, tile), BF16),
            pltpu.VMEM((tiles, n_e // 2, share, tile), BF16),
            dma((tiles,)), dma((tiles,)), dma((tiles,)),
            dma((tiles, n_e // 2)), dma((tiles, n_e // 2)),
            dma((n_e,)), dma((n_e,)), dma,
        ],
        compiler_params=pltpu.CompilerParams(
            collective_id=1, has_side_effects=True, vmem_limit_bytes=48 * 1024 * 1024),
    )(d_pre, first.reshape(tiles, tile, width), d_gate)


def on_device(trunk, w_first, w_second, gates, d_mixed):
    rank = lax.axis_index("dp")
    first = w_first[0]
    second = w_second[0]
    gate_here = gates[0]
    n_dp = lax.axis_size("dp")
    depth = first.shape[0] // n_dp
    units = second.shape[0] // n_dp
    group = gate_here.shape[1]

    n_e = lax.axis_size("expert")
    gate_parts = gate_here.T.astype(F32).reshape(n_e, -1, gate_here.shape[0])
    rows_all, d_output_all, pre, gates_each, outs_each = gather_all(
        trunk, gate_parts, jnp.transpose(d_mixed, (1, 0, 2)), first, second)
    rows_all = rows_all.reshape(-1, trunk.shape[1])
    d_output_all = d_output_all.reshape(-1, second.shape[1])
    pre = pre.reshape(-1, first.shape[1])
    gates_each = gates_each.astype(BF16)
    d_hidden = lax.dot_general(
        d_output_all, second, (((1,), (1,)), ((), ())), preferred_element_type=F32
    )
    sig = jax.nn.sigmoid(pre)
    d_pre = (d_hidden * sig * (1.0 + pre * (1.0 - sig))).astype(BF16)
    d_pre_here = lax.dynamic_slice_in_dim(d_pre, rank * group, group, 0)
    mixed = jnp.einsum(
        "ert,ero->rto", gates_each, outs_each, preferred_element_type=F32
    ).astype(BF16)
    d_gate_each = jnp.einsum(
        "rto,ero->ert", d_mixed, outs_each, preferred_element_type=F32
    ).astype(BF16)
    d_trunk, back_gate = return_all(d_pre_here, first, d_gate_each.astype(F32))
    d_gate = back_gate.reshape(group, -1).T.astype(BF16)[None]

    columns = lax.dynamic_slice_in_dim(rows_all, rank * depth, depth, 1)
    d_first = lax.dot_general(
        columns, d_pre, (((0,), (0,)), ((), ())), preferred_element_type=F32
    ).astype(BF16)
    some_pre = lax.dynamic_slice_in_dim(pre, rank * units, units, 1)
    some_hidden = jax.nn.silu(some_pre).astype(BF16)
    d_second = lax.dot_general(
        some_hidden, d_output_all, (((0,), (0,)), ((), ())), preferred_element_type=F32
    ).astype(BF16)
    return (mixed, d_trunk, d_gate, d_first[None], d_second[None])


SIDE, LINE, LANES = 2, 4, 128
VMEM_BYTES = 62 * 1024 * 1024


def tiled(count, body, hooks=()):
    @pl.loop(0, count)
    def _(c):
        body(c)
        for at, hook in hooks:
            pl.when(c == at)(hook)


def step_kernel(n_e, n_d, trunk, gates, cot_in, first, second,
                columns_out, d_out_out, d_pre_out, units_out, mixed_out, d_trunk_out, back_out_ref,
                rows, d_out, d_pre, some_hidden, mixed, d_trunk, gate_back, gate_in, gate_piece,
                weights, later, turned, cot, gate_each, mix, piece, tall, hidden, made, outs, d_gate,
                part, near, pair, got,
                load_sem, own_sem, g_send, g_recv, t_send, t_recv, o_send, o_recv, z_send, z_recv,
                m_send, m_recv, n_send, n_recv, p_send, p_recv, b_send, b_recv, out_sem):
    e = lax.axis_index("expert")
    z = lax.axis_index("dp")
    core, seat, pairs = lax.rem(e, 2), e // 2, n_e // 2
    partner = e + 1 - 2 * core
    side, up = lax.rem(seat, SIDE), seat // SIDE
    across = e + 2 - 4 * side
    over = e + 2 * SIDE - 4 * SIDE * up
    corner = across + over - e
    bridge = across * (1 - core) + over * core
    other = across * core + over * (1 - core)
    middle = (z * (n_d - 1 - z)) // 2
    inner = middle == 1
    mate = z + 1 - 2 * lax.rem(z, 2)
    mirror = n_d - 1 - z
    skip = lax.rem(z + 2, n_d)
    order = [z, mate, middle * mirror + (1 - middle) * skip, middle * skip + (1 - middle) * mirror]
    tasks = cot.shape[0] // rows.shape[2]
    share, depth = rows.shape[2], rows.shape[3]
    width = tall.shape[2]
    group = n_e * share
    units = some_hidden.shape[2]
    part_depth = depth // n_d
    depth_here = pl.ds(pl.multiple_of(z * part_depth, part_depth), part_depth)

    def plane(s):
        return lax.rem(e + s, n_e)

    def remote(src, dst, send, recv, where):
        return pltpu.make_async_remote_copy(
            src_ref=src, dst_ref=dst, send_sem=send, recv_sem=recv,
            device_id=where, device_id_type=MESH)

    def load(k):
        src, dst = [(second, later), (cot_in, cot), (first, weights), (gates, gate_in)][k]
        return pltpu.make_async_copy(src, dst, load_sem.at[k])

    def own(k):
        src, dst = [(gate_piece.at[e], gate_each.at[e]), (trunk, rows.at[z, e]),
                    (piece.at[e], d_out.at[z, e]), (made.at[e], outs.at[e]),
                    (d_gate.at[e], gate_back.at[e])][k]
        return pltpu.make_async_copy(src, dst, own_sem.at[k])

    def at_plane(j):
        return {"expert": j}

    def gate_out(s):
        j = plane(s)
        return remote(gate_piece.at[j], gate_each.at[e], g_send.at[s], g_recv.at[e], at_plane(j))

    def trunk_out(g, k):
        zi = order[g]
        j, where = [
            (e, at_plane(across)), (e, at_plane(over)), (e, at_plane(partner)),
            (bridge, at_plane(over * (1 - core) + across * core)),
            (bridge, at_plane(partner)), (other, at_plane(partner)), (corner, at_plane(partner)),
            (e, {"dp": mate}), (e, {"dp": mirror})][k]
        src = trunk if g == 0 and k in (0, 1, 2, 7, 8) else rows.at[zi, j]
        return remote(src, rows.at[zi, j], t_send.at[g, k], t_recv.at[zi, j], where)

    def trunk_in(g, j):
        zi = order[g]
        remote(trunk, rows.at[zi, j], t_send.at[0, 0], t_recv.at[zi, j],
               at_plane(partner)).wait_recv()

    def piece_out(s):
        j = plane(s)
        return remote(piece.at[j], d_out.at[z, e], o_send.at[s], o_recv.at[e], at_plane(j))

    def half(zi, h):
        return d_out.at[zi, h * (n_e // 2):(h + 1) * (n_e // 2)]

    def line_out(g, k, h):
        zi = order[g]
        return remote(half(zi, h), half(zi, h), z_send.at[g, k, h], z_recv.at[zi, h],
                      {"dp": mate if k == 0 else mirror})

    def keep(k):
        src, dst = ([(rows.at[zi, :, :, depth_here], columns_out.at[zi]) for zi in order]
                    + [(d_pre.at[zi], d_pre_out.at[zi]) for zi in order]
                    + [(d_out, d_out_out), (some_hidden, units_out), (mixed, mixed_out),
                       (d_trunk, d_trunk_out), (gate_back, back_out_ref)])[k]
        return pltpu.make_async_copy(src, dst, out_sem.at[k])

    def made_out(s):
        j = plane(s)
        return remote(made.at[j], outs.at[e], m_send.at[s], m_recv.at[e], at_plane(j))

    def back_out(s):
        j = plane(s)
        return remote(d_gate.at[j], gate_back.at[e], b_send.at[s], b_recv.at[e], at_plane(j))

    def near_out(c):
        return remote(part.at[c, :, 1 - core], near.at[c], n_send.at[c], n_recv.at[c],
                      at_plane(partner))

    def part_out(c, s):
        k = lax.rem(seat + s, pairs)
        return remote(pair.at[c, k], got.at[c, seat], p_send.at[c, s], p_recv.at[c, seat],
                      at_plane(2 * k + core))

    def spread(g):
        for k in range(3):
            trunk_out(g, k).start()

    def bridge_on(g):
        trunk_in(g, bridge)
        trunk_out(g, 3).start()
        trunk_out(g, 4).start()
        trunk_in(g, other)
        trunk_out(g, 5).start()

    def corner_on(g):
        trunk_in(g, corner)
        trunk_out(g, 6).start()

    def complete(g):
        for shift in (0, across - e, over - e, corner - e):
            trunk_in(g, partner + shift)

    def arrive(g):
        trunk_in(g, e)
        if g == 1:
            pl.when(inner)(lambda: trunk_out(1, 8).start())
        else:
            pl.when(inner)(lambda: trunk_out(g, 7).start())

    def line_arrive(g, h):
        zi = order[g]
        remote(half(zi, h), half(zi, h), z_send.at[0, 0, h], z_recv.at[zi, h],
               {"dp": mate}).wait_recv()
        pl.when(inner)(lambda: line_out(g, 1 if g == 1 else 0, h).start())

    def in_middle(call, *g):
        pl.when(inner)(lambda: call(*g))

    def at_end(call, *g):
        pl.when(middle == 0)(lambda: call(*g))

    for k in (3, 1, 0, 2):
        load(k).start()
    barrier = pltpu.get_barrier_semaphore()
    for s in range(1, n_e):
        pl.semaphore_signal(barrier, inc=1, device_id=at_plane(plane(s)), device_id_type=MESH)
    for i in range(1, n_d):
        pl.semaphore_signal(barrier, inc=1, device_id={"dp": lax.rem(z + i, n_d)},
                            device_id_type=MESH)
    load(3).wait()
    task_eye = jnp.where(
        lax.broadcasted_iota(jnp.int32, (tasks, LANES), 0)
        == lax.broadcasted_iota(jnp.int32, (tasks, LANES), 1), 1.0, 0.0).astype(BF16)
    gate_piece[...] = lax.dot_general(
        gate_in[...], task_eye, (((0,), (0,)), ((), ())),
        preferred_element_type=F32).reshape(gate_piece.shape)
    own(0).start()
    own(1).start()
    pl.semaphore_wait(barrier, n_e - 1 + n_d - 1)

    for s in range(1, n_e):
        gate_out(s).start()
    trunk_out(0, 7).start()
    pl.when(inner)(lambda: trunk_out(0, 8).start())
    spread(0)

    def turn(low, high):
        @pl.loop(low, high)
        def _(c):
            here = pl.ds(pl.multiple_of(c * 256, 256), 256)
            turned[:, here] = later[here, :].T

    turns = width // 256
    load(0).wait()
    turn(0, turns // 2)

    def task_of():
        shape = (LANES, share * tasks)
        return jnp.where(
            lax.broadcasted_iota(jnp.int32, shape, 0)
            == lax.rem(lax.broadcasted_iota(jnp.int32, shape, 1), tasks), 1.0, 0.0).astype(BF16)

    def same_sample():
        shape = (n_e, share, share * tasks)
        match = (lax.broadcasted_iota(jnp.int32, shape, 1)
                 == lax.div(lax.broadcasted_iota(jnp.int32, shape, 2), tasks))
        return jnp.where(match, 1.0, 0.0).reshape(group, share * tasks)

    for s in range(1, n_e):
        j = plane(s)
        remote(gate_piece.at[j], gate_each.at[j], g_send.at[0], g_recv.at[j],
               at_plane(j)).wait_recv()
    own(0).wait()
    load(1).wait()
    each = gate_each[...].reshape(group, LANES).astype(BF16)
    mix[...] = (jnp.dot(each, task_of(), preferred_element_type=F32)
                * same_sample()).astype(BF16)
    piece[...] = jnp.dot(mix[...], cot[...], preferred_element_type=F32).astype(BF16).reshape(
        piece.shape)
    for s in range(1, n_e):
        piece_out(s).start()
    own(2).start()

    turn(turns // 2, turns)
    bridge_on(0)
    arrive(1)
    in_middle(arrive, 2)
    for s in range(1, n_e):
        j = plane(s)
        remote(piece.at[j], d_out.at[z, j], o_send.at[0], o_recv.at[j], at_plane(j)).wait_recv()
    own(2).wait()
    for h in range(2):
        line_out(0, 0, h).start()
        in_middle(lambda: line_out(0, 1, h).start())

    tile = 512

    broad = 2 * tile

    def part_of(c, span=tile):
        return pl.ds(pl.multiple_of(c * span, span), span)

    def back_hidden(g, c, span=tile):
        left = d_out[order[g]].reshape(group, d_out.shape[3])
        return jnp.dot(left, turned[:, part_of(c, span)], preferred_element_type=F32)

    def forward_pre(g, c, span=tile):
        left = rows[order[g]].reshape(group, depth)
        return jnp.dot(left, weights[:, part_of(c, span)], preferred_element_type=F32)

    def store_d_pre(g, c, d_hidden, value, span=tile):
        sig = jax.nn.sigmoid(value)
        d_pre[order[g], :, part_of(c, span)] = (
            d_hidden * sig * (1.0 + value * (1.0 - sig))).astype(BF16)

    def first_hidden(c):
        tall[0, :, part_of(c, broad)] = back_hidden(0, c, broad)

    def first_pre(c):
        value = forward_pre(0, c)
        store_d_pre(0, c, tall[0, :, part_of(c)], value)
        hidden[:, part_of(c)] = (value * jax.nn.sigmoid(value)).astype(BF16)

    def later_pre(g, span=tile):
        def body(c):
            tall[g, :, part_of(c, span)] = forward_pre(g, c, span)
        return body

    def later_hidden(g):
        def body(c):
            store_d_pre(g, c, back_hidden(g, c), tall[g, :, part_of(c)])
        return body

    units_here = pl.ds(pl.multiple_of(z * units, units), units)

    def keep_units(g):
        value = tall[g, :, units_here]
        some_hidden[order[g]] = (value * jax.nn.sigmoid(value)).astype(BF16)

    tiled(width // broad, first_hidden)
    spread(1)
    corner_on(0)
    in_middle(arrive, 3)
    own(1).wait()
    complete(0)
    load(2).wait()

    def hook_a():
        at_end(arrive, 2)
        spread(2)

    tiled(width // tile, first_pre, [(2, hook_a)])
    keep(0).start()
    keep(4).start()
    some_hidden[z] = hidden[:, units_here]


    def compute(c):
        value = lax.dot_general(d_pre[z], weights[part_of(c), :], (((1,), (1,)), ((), ())),
                                preferred_element_type=F32)
        part[c] = value.astype(BF16).reshape(pairs, 2, share, tile)

    def combine(c):
        near_out(c).wait_recv()
        pair[c] = (part[c, :, core].astype(F32) + near[c].astype(F32)).astype(BF16)

    def send_parts(low, high):
        @pl.loop(low, high)
        def _(c):
            for s in range(1, pairs):
                part_out(c, s).start()

    count = depth // tile
    compute(0)
    near_out(0).start()
    bridge_on(1)
    compute(1)

    def hook_b():
        at_end(arrive, 3)
        at_end(spread, 3)

    def hook_c():
        for h in range(2):
            in_middle(line_arrive, 1, h)
            in_middle(line_arrive, 2, h)

    hooks = [(2, lambda: in_middle(spread, 3)), (4, hook_b), (5, hook_c), (6, lambda: bridge_on(2)),
             (7, lambda: corner_on(1))]

    @pl.loop(2, count)
    def _(c):
        near_out(c - 1).start()
        compute(c)
        combine(c - 2)
        for at, hook in hooks:
            pl.when(c == at)(hook)

    near_out(count - 1).start()

    def first_output(c):
        value = jnp.dot(hidden[...], later[:, part_of(c)], preferred_element_type=F32)
        made[:, :, part_of(c)] = value.astype(BF16).reshape(n_e, share, tile)

    tiled(made.shape[2] // tile, first_output)
    own(3).start()
    complete(1)
    keep(1).start()

    def hook_f():
        combine(count - 2)
        combine(count - 1)
        bridge_on(3)

    tiled(width // broad, later_pre(1, broad), [(0, hook_f)])
    keep_units(1)
    for h in range(2):
        at_end(line_arrive, 1, h)
    tiled(width // tile, later_hidden(1), [(1, lambda: corner_on(2))])
    send_parts(0, count // 2)
    keep(5).start()
    complete(2)
    keep(2).start()

    def hook_d():
        for h in range(2):
            in_middle(line_arrive, 3, h)

    def hook_e():
        for s in range(1, n_e):
            made_out(s).start()

    tiled(width // broad, later_pre(2, broad), [(0, hook_d), (1, hook_e)])
    keep_units(2)
    send_parts(count // 2, count)
    for h in range(2):
        at_end(line_arrive, 2, h)
    tiled(width // tile, later_hidden(2), [(1, lambda: corner_on(3))])
    keep(6).start()
    complete(3)
    keep(3).start()
    tiled(width // broad, later_pre(3, broad))
    keep_units(3)
    keep(9).start()

    own(3).wait()
    for s in range(1, n_e):
        j = plane(s)
        remote(made.at[j], outs.at[j], m_send.at[0], m_recv.at[j], at_plane(j)).wait_recv()
    each_out = outs[...].reshape(group, outs.shape[2])
    product = lax.dot_general(each_out, cot[...], (((1,), (1,)), ((), ())),
                              preferred_element_type=F32)
    product = (product * same_sample()).astype(BF16)
    d_gate[...] = lax.dot_general(product, task_of(), (((1,), (1,)), ((), ())),
                                  preferred_element_type=F32).reshape(d_gate.shape)
    own(4).start()
    for s in range(1, n_e):
        back_out(s).start()
    mixed[...] = lax.dot_general(mix[...], each_out, (((0,), (0,)), ((), ())),
                                 preferred_element_type=F32).astype(BF16)

    keep(10).start()
    at_end(line_arrive, 3, 0)
    at_end(line_arrive, 3, 1)
    keep(8).start()
    tiled(width // tile, later_hidden(3))
    keep(7).start()

    @pl.loop(0, count)
    def _(c):
        total = pair[c, seat].astype(F32)
        for s in range(1, pairs):
            k = lax.rem(seat + s, pairs)
            remote(pair.at[c, k], got.at[c, k], p_send.at[c, 0], p_recv.at[c, k],
                   at_plane(2 * k + core)).wait_recv()
            total = total + got[c, k].astype(F32)
        d_trunk[:, part_of(c)] = total.astype(BF16)

    keep(11).start()

    own(4).wait()
    for s in range(1, n_e):
        j = plane(s)
        remote(d_gate.at[j], gate_back.at[j], b_send.at[0], b_recv.at[j], at_plane(j)).wait_recv()
    for s in range(1, n_e):
        gate_out(s).wait_send()
        piece_out(s).wait_send()
        made_out(s).wait_send()
        back_out(s).wait_send()
    for g in range(n_d):
        for k in range(7):
            trunk_out(g, k).wait_send()
    keep(12).start()
    trunk_out(0, 7).wait_send()
    for h in range(2):
        line_out(0, 0, h).wait_send()

    @pl.when(inner)
    def _():
        trunk_out(0, 8).wait_send()
        trunk_out(1, 8).wait_send()
        for g in range(2, n_d):
            trunk_out(g, 7).wait_send()
        for h in range(2):
            line_out(0, 1, h).wait_send()
            line_out(1, 1, h).wait_send()
            for g in range(2, n_d):
                line_out(g, 0, h).wait_send()

    @pl.loop(0, count)
    def _(c):
        near_out(c).wait_send()
        for s in range(1, pairs):
            part_out(c, s).wait_send()

    for k in range(13):
        keep(k).wait()


def step_all(trunk, gates, cot, first, second):
    n_e, n_d = lax.axis_size("expert"), lax.axis_size("dp")
    share, depth = trunk.shape
    width = first.shape[1]
    out = second.shape[1]
    group = n_e * share
    count, pairs, tile = depth // 512, n_e // 2, 512
    hbm = pl.BlockSpec(memory_space=pltpu.HBM)
    dma = pltpu.SemaphoreType.DMA
    gate_shape = (n_e, share, LANES)
    return pl.pallas_call(
        functools.partial(step_kernel, n_e, n_d),
        out_shape=(
            jax.ShapeDtypeStruct((n_d, n_e, share, depth // n_d), BF16),
            jax.ShapeDtypeStruct((n_d, n_e, share, out), BF16),
            jax.ShapeDtypeStruct((n_d, group, width), BF16),
            jax.ShapeDtypeStruct((n_d, group, width // n_d), BF16),
            jax.ShapeDtypeStruct((cot.shape[0], out), BF16),
            jax.ShapeDtypeStruct((share, depth), BF16),
            jax.ShapeDtypeStruct(gate_shape, F32),
        ),
        in_specs=[hbm] * 5,
        out_specs=(hbm,) * 7,
        scratch_shapes=[
            pltpu.VMEM((n_d, n_e, share, depth), BF16),
            pltpu.VMEM((n_d, n_e, share, out), BF16),
            pltpu.VMEM((n_d, group, width), BF16),
            pltpu.VMEM((n_d, group, width // n_d), BF16),
            pltpu.VMEM((cot.shape[0], out), BF16),
            pltpu.VMEM((share, depth), BF16),
            pltpu.VMEM(gate_shape, F32),
            pltpu.VMEM(gates.shape, BF16),
            pltpu.VMEM(gate_shape, F32),
            pltpu.VMEM(first.shape, BF16),
            pltpu.VMEM(second.shape, BF16),
            pltpu.VMEM(second.shape[::-1], BF16),
            pltpu.VMEM(cot.shape, BF16),
            pltpu.VMEM(gate_shape, F32),
            pltpu.VMEM((group, cot.shape[0]), BF16),
            pltpu.VMEM((n_e, share, out), BF16),
            pltpu.VMEM((n_d, group, width), F32),
            pltpu.VMEM((group, width), BF16),
            pltpu.VMEM((n_e, share, out), BF16),
            pltpu.VMEM((n_e, share, out), BF16),
            pltpu.VMEM(gate_shape, F32),
            pltpu.VMEM((count, pairs, 2, share, tile), BF16),
            pltpu.VMEM((count, pairs, share, tile), BF16),
            pltpu.VMEM((count, pairs, share, tile), BF16),
            pltpu.VMEM((count, pairs, share, tile), BF16),
            dma((4,)), dma((5,)),
            dma((n_e,)), dma((n_e,)),
            dma((n_d, 9)), dma((n_d, n_e)),
            dma((n_e,)), dma((n_e,)),
            dma((n_d, 2, 2)), dma((n_d, 2)),
            dma((n_e,)), dma((n_e,)),
            dma((count,)), dma((count,)),
            dma((count, pairs)), dma((count, pairs)),
            dma((n_e,)), dma((n_e,)), dma((13,)),
        ],
        compiler_params=pltpu.CompilerParams(
            collective_id=2, has_side_effects=True, vmem_limit_bytes=VMEM_BYTES),
    )(trunk, gates, cot, first, second)


def finish_kernel(columns, d_pre, units, d_out, mixed, d_trunk, back,
                  d_first, d_second, mixed_out, d_trunk_out, d_gate,
                  columns_v, d_pre_v, units_v, d_out_v, mixed_v, d_trunk_v, back_v,
                  first_v, second_v, gate_v, in_sem, out_sem, tile_sem, wide_sem):
    pairs = [(units, units_v), (d_out, d_out_v), (columns, columns_v), (mixed, mixed_v),
             (d_trunk, d_trunk_v), (back, back_v)]
    steps = d_pre.shape[0]

    def take(k):
        return pltpu.make_async_copy(*pairs[k], in_sem.at[k])

    def wide(k):
        return pltpu.make_async_copy(d_pre.at[k], d_pre_v.at[k], wide_sem.at[k])

    def give(k):
        src, dst = [(second_v, d_second), (mixed_v, mixed_out), (d_trunk_v, d_trunk_out),
                    (gate_v, d_gate)][k]
        return pltpu.make_async_copy(src, dst, out_sem.at[k])

    for k in range(3):
        take(k).start()
    for k in range(steps):
        wide(k).start()
    for k in range(3, len(pairs)):
        take(k).start()
    take(0).wait()
    take(1).wait()
    second_v[...] = lax.dot_general(
        units_v[...], d_out_v[...], (((0,), (0,)), ((), ())),
        preferred_element_type=F32).astype(BF16)
    give(0).start()
    take(2).wait()
    for k in range(steps):
        wide(k).wait()
    tile = first_v.shape[1]
    count = first_v.shape[0]

    def store(c):
        here = pl.ds(pl.multiple_of(c * tile, tile), tile)
        return pltpu.make_async_copy(first_v.at[c], d_first.at[here], tile_sem.at[c])

    @pl.loop(0, count)
    def _(c):
        here = pl.ds(pl.multiple_of(c * tile, tile), tile)
        right = d_pre_v[...].reshape(-1, d_pre_v.shape[2])
        first_v[c] = lax.dot_general(
            columns_v[:, here], right, (((0,), (0,)), ((), ())),
            preferred_element_type=F32).astype(BF16)
        store(c).start()

        @pl.when(c == 0)
        def _():
            take(3).wait()
            give(1).start()
            take(4).wait()
            give(2).start()
            take(5).wait()
            tasks = d_gate.shape[0]
            eye = jnp.where(
                lax.broadcasted_iota(jnp.int32, (tasks, LANES), 0)
                == lax.broadcasted_iota(jnp.int32, (tasks, LANES), 1), 1.0, 0.0).astype(BF16)
            gate_v[...] = lax.dot_general(
                eye, back_v[...].astype(BF16), (((1,), (1,)), ((), ())),
                preferred_element_type=F32).astype(BF16)
            give(3).start()

    for k in range(4):
        give(k).wait()

    @pl.loop(0, count)
    def _(c):
        store(c).wait()


def finish_all(columns, d_pre, units, d_out, mixed, d_trunk, back, tasks):
    hbm = pl.BlockSpec(memory_space=pltpu.HBM)
    dma = pltpu.SemaphoreType.DMA
    rows, depth = columns.shape
    steps, group, width = d_pre.shape
    unit, out = units.shape[1], d_out.shape[1]
    tile = 256
    ins = (columns, d_pre, units, d_out, mixed, d_trunk, back)
    return pl.pallas_call(
        finish_kernel,
        out_shape=(
            jax.ShapeDtypeStruct((depth, width), BF16),
            jax.ShapeDtypeStruct((unit, out), BF16),
            jax.ShapeDtypeStruct(mixed.shape, BF16),
            jax.ShapeDtypeStruct(d_trunk.shape, BF16),
            jax.ShapeDtypeStruct((tasks, back.shape[0]), BF16),
        ),
        in_specs=[hbm] * 7,
        out_specs=(hbm,) * 5,
        scratch_shapes=[pltpu.VMEM(x.shape, x.dtype) for x in ins] + [
            pltpu.VMEM((depth // tile, tile, width), BF16),
            pltpu.VMEM((unit, out), BF16),
            pltpu.VMEM((tasks, back.shape[0]), BF16),
            dma((6,)), dma((4,)), dma((depth // tile,)), dma((steps,)),
        ],
        compiler_params=pltpu.CompilerParams(vmem_limit_bytes=VMEM_BYTES),
    )(*ins)


def on_square(trunk, w_first, w_second, gates, d_mixed):
    first, second, gate_here = w_first[0], w_second[0], gates[0]
    tasks, group = gate_here.shape
    columns, d_out, d_pre, units, mixed, d_trunk, back = step_all(
        trunk, gate_here, d_mixed.reshape(-1, d_mixed.shape[2]), first, second)
    d_first, d_second, mixed, d_trunk, d_gate = finish_all(
        columns.reshape(-1, columns.shape[3]), d_pre, units.reshape(-1, units.shape[2]),
        d_out.reshape(-1, d_out.shape[3]), mixed, d_trunk, back.reshape(group, -1), tasks)
    return (mixed.reshape(d_mixed.shape), d_trunk, d_gate[None], d_first[None], d_second[None])


def solution(mesh):
    in_specs = (
        P(("dp", "expert"), None),
        P("expert", None, None),
        P("expert", None, None),
        P("expert", None, "dp"),
        P(("dp", "expert"), None, None),
    )
    out_specs = (
        P(("dp", "expert"), None, None),
        P(("dp", "expert"), None),
        P("expert", None, "dp"),
        P("expert", "dp", None),
        P("expert", "dp", None),
    )
    fits = mesh.shape["expert"] == 2 * SIDE * SIDE and mesh.shape["dp"] == LINE
    return jax.shard_map(
        on_square if fits else on_device, mesh=mesh, in_specs=in_specs, out_specs=out_specs, check_vma=False
    )
```

```python
import functools

import jax
import jax.numpy as jnp
from jax import lax
from jax.experimental import pallas as pl
from jax.experimental.pallas import tpu as pltpu
from jax.sharding import PartitionSpec as P

F32 = jnp.float32
BF16 = jnp.bfloat16


MESH = pl.DeviceIdType.MESH


def gather_kernel(n_e, n_d, trunk, gates, cot, first, second, rows, d_out, pre, gate_each,
                  outs, weights, later, hidden, made, m_send, m_recv, later_sem, piece, block, tall, w_sem, load_sem, store_sem,
                  g_send, g_recv, t_send, t_recv, o_send, o_recv, z_send, z_recv,
                  own_sem):
    e = lax.axis_index("expert")
    z = lax.axis_index("dp")
    partner = e + 1 - 2 * lax.rem(e, 2)
    pairs = n_e // 2

    def plane(s):
        return lax.rem(e + s, n_e)

    def along(i):
        return lax.rem(z + i, n_d)

    def remote(src, dst, send, recv, where):
        return pltpu.make_async_remote_copy(
            src_ref=src, dst_ref=dst, send_sem=send, recv_sem=recv,
            device_id=where, device_id_type=MESH)

    load_weights = pltpu.make_async_copy(first, weights, w_sem)
    load_weights.start()
    load_later = pltpu.make_async_copy(second, later, later_sem)
    load_later.start()

    barrier = pltpu.get_barrier_semaphore()
    for s in range(1, n_e):
        pl.semaphore_signal(barrier, inc=1, device_id={"expert": plane(s)}, device_id_type=MESH)
    for i in range(1, n_d):
        pl.semaphore_signal(barrier, inc=1, device_id={"dp": along(i)}, device_id_type=MESH)
    pl.semaphore_wait(barrier, n_e - 1 + n_d - 1)

    sent = []

    def go(copy):
        copy.start()
        sent.append(copy)

    for s in range(1, n_e):
        j = plane(s)
        go(remote(gates.at[j], gate_each.at[e], g_send.at[s], g_recv.at[e], {"expert": j}))
    own_gate = pltpu.make_async_copy(gates.at[e], gate_each.at[e], own_sem.at[0])
    own_gate.start()
    own_rows = pltpu.make_async_copy(trunk, rows.at[z, e], own_sem.at[1])
    own_rows.start()

    def spread(i):
        zi = along(i)
        src = trunk if i == 0 else rows.at[zi, e]
        for s in range(1, pairs):
            go(remote(src, rows.at[zi, e], t_send.at[i, s], t_recv.at[zi, e],
                      {"expert": plane(2 * s)}))
        go(remote(src, rows.at[zi, e], t_send.at[i, 0], t_recv.at[zi, e], {"expert": partner}))

    def arrived(zi, j):
        remote(trunk, rows.at[zi, j], t_send.at[0, 0], t_recv.at[zi, j],
               {"expert": partner}).wait_recv()

    for i in range(1, n_d):
        go(remote(trunk, rows.at[z, e], t_send.at[i, n_e - 1], t_recv.at[z, e], {"dp": along(i)}))
    spread(0)

    for s in range(1, n_e):
        j = plane(s)
        remote(gates.at[j], gate_each.at[j], g_send.at[0], g_recv.at[j], {"expert": j}).wait_recv()
    own_gate.wait()
    tasks = cot.shape[0]

    @pl.loop(0, n_e)
    def _(j):
        weight = gate_each[j]
        total = weight[:, 0:1] * cot[0].astype(F32)
        for t in range(1, tasks):
            total = total + weight[:, t:t + 1] * cot[t].astype(F32)
        piece[j] = total.astype(BF16)

    own_piece = pltpu.make_async_copy(piece.at[e], d_out.at[z, e], own_sem.at[2])
    own_piece.start()
    for s in range(1, n_e):
        j = plane(s)
        go(remote(piece.at[j], d_out.at[z, e], o_send.at[s], o_recv.at[e], {"expert": j}))

    def send_outputs():
        own_made.start()
        for s in range(1, n_e):
            j = plane(s)
            go(remote(made.at[j], outs.at[e], m_send.at[s], m_recv.at[e], {"expert": j}))

    own_made = pltpu.make_async_copy(made.at[e], outs.at[e], own_sem.at[3])
    stores = []
    for i in range(n_d):
        zi = along(i)
        if i + 1 < n_d:
            arrived(along(i + 1), e)
            spread(i + 1)
        if i == 1:
            send_outputs()
        if i == 0:
            for s in range(1, n_e):
                j = plane(s)
                remote(piece.at[j], d_out.at[z, j], o_send.at[0], o_recv.at[j],
                       {"expert": j}).wait_recv()
            own_piece.wait()
            for k in range(1, n_d):
                go(remote(d_out.at[z], d_out.at[z], z_send.at[k], z_recv.at[z], {"dp": along(k)}))
            own_rows.wait()
        for s in range(1, pairs):
            j = plane(2 * s)
            arrived(zi, j)
            go(remote(rows.at[zi, j], rows.at[zi, j], t_send.at[i, pairs - 1 + s],
                      t_recv.at[zi, j], {"expert": partner}))
        for s in range(pairs):
            arrived(zi, lax.rem(partner + 2 * s, n_e))
        load = pltpu.make_async_copy(rows.at[zi], block, load_sem)
        load.start()
        if i == 0:
            load_weights.wait()
        else:
            stores[-1].wait()
        load.wait()
        height = block.shape[0] * block.shape[1]
        tile = 256
        left = block[...].reshape(height, block.shape[2])

        @pl.loop(0, tall.shape[1] // tile)
        def _(c):
            here = pl.ds(pl.multiple_of(c * tile, tile), tile)
            value = jnp.dot(left, weights[:, here], preferred_element_type=F32)
            tall[:, here] = value
            if i == 0:
                hidden[:, here] = (value * jax.nn.sigmoid(value)).astype(BF16)

        store = pltpu.make_async_copy(tall, pre.at[zi], store_sem)
        store.start()
        stores.append(store)
        if i == 0:
            load_later.wait()

            @pl.loop(0, made.shape[2] // tile)
            def _(c):
                here = pl.ds(pl.multiple_of(c * tile, tile), tile)
                value = jnp.dot(hidden[...], later[:, here], preferred_element_type=F32)
                made[:, :, here] = value.astype(BF16).reshape(n_e, -1, tile)

    stores[-1].wait()
    if n_d == 1:
        send_outputs()
    own_made.wait()
    for s in range(1, n_e):
        j = plane(s)
        remote(made.at[j], outs.at[j], m_send.at[0], m_recv.at[j], {"expert": j}).wait_recv()
    for i in range(1, n_d):
        zi = along(i)
        remote(d_out.at[zi], d_out.at[zi], z_send.at[0], z_recv.at[zi], {"dp": zi}).wait_recv()
    for copy in sent:
        copy.wait_send()


def gather_all(trunk, gates, cot, first, second):
    n_e, n_d = lax.axis_size("expert"), lax.axis_size("dp")
    share, depth = trunk.shape
    width = first.shape[1]
    out = cot.shape[2]
    anywhere = pl.BlockSpec(memory_space=pl.ANY)
    hbm = pl.BlockSpec(memory_space=pltpu.HBM)
    vmem = pl.BlockSpec(memory_space=pltpu.VMEM)
    dma = pltpu.SemaphoreType.DMA
    return pl.pallas_call(
        functools.partial(gather_kernel, n_e, n_d),
        out_shape=(
            jax.ShapeDtypeStruct((n_d, n_e, share, depth), BF16),
            jax.ShapeDtypeStruct((n_d, n_e, share, out), BF16),
            jax.ShapeDtypeStruct((n_d, n_e * share, width), F32),
            jax.ShapeDtypeStruct(gates.shape, F32),
            jax.ShapeDtypeStruct((n_e, share, out), BF16),
        ),
        in_specs=[vmem, vmem, vmem, hbm, hbm],
        out_specs=(hbm, hbm, hbm, vmem, hbm),
        scratch_shapes=[
            pltpu.VMEM(first.shape, BF16),
            pltpu.VMEM(second.shape, BF16),
            pltpu.VMEM((n_e * share, width), BF16),
            pltpu.VMEM((n_e, share, out), BF16),
            dma((n_e,)), dma((n_e,)), dma,
            pltpu.VMEM((n_e, share, out), BF16),
            pltpu.VMEM((n_e, share, depth), BF16),
            pltpu.VMEM((n_e * share, width), F32),
            dma, dma, dma,
            dma((n_e,)), dma((n_e,)),
            dma((n_d, n_e)), dma((n_d, n_e)),
            dma((n_e,)), dma((n_e,)),
            dma((n_d,)), dma((n_d,)),
            dma((4,)),
        ],
        compiler_params=pltpu.CompilerParams(
            collective_id=0, has_side_effects=True, vmem_limit_bytes=48 * 1024 * 1024),
    )(trunk, gates, cot, first, second)


def return_kernel(n_e, d_pre, first, d_gate, d_trunk, gate_back, weights, part, near, pair, got,
                  w_sem, n_send, n_recv, p_send, p_recv, g_send, g_recv, own_sem):
    e = lax.axis_index("expert")
    core, seat, pairs = lax.rem(e, 2), e // 2, n_e // 2
    partner = e + 1 - 2 * core
    tiles, tile, _ = weights.shape

    def plane(s):
        return lax.rem(e + s, n_e)

    def remote(src, dst, send, recv, j):
        return pltpu.make_async_remote_copy(
            src_ref=src, dst_ref=dst, send_sem=send, recv_sem=recv,
            device_id={"expert": j}, device_id_type=MESH)

    def load(c):
        return pltpu.make_async_copy(first.at[c], weights.at[c], w_sem.at[c])

    for c in range(tiles):
        load(c).start()
    barrier = pltpu.get_barrier_semaphore()
    for s in range(1, n_e):
        pl.semaphore_signal(barrier, inc=1, device_id={"expert": plane(s)}, device_id_type=MESH)
    pl.semaphore_wait(barrier, n_e - 1)

    own = pltpu.make_async_copy(d_gate.at[e], gate_back.at[e], own_sem)
    own.start()

    def gate_out(s):
        j = plane(s)
        return remote(d_gate.at[j], gate_back.at[e], g_send.at[s], g_recv.at[e], j)

    def near_out(c):
        return remote(part.at[c, :, 1 - core], near.at[c], n_send.at[c], n_recv.at[c], partner)

    def part_out(c, s):
        k = lax.rem(seat + s, pairs)
        return remote(pair.at[c, k], got.at[c, seat], p_send.at[c, s], p_recv.at[c, seat],
                      2 * k + core)

    for s in range(1, n_e):
        gate_out(s).start()

    def compute(c):
        load(c).wait()
        value = lax.dot_general(
            d_pre[...], weights[c], (((1,), (1,)), ((), ())), preferred_element_type=F32)
        part[c] = value.astype(BF16).reshape(pairs, 2, -1, tile)

    def combine(c):
        near_out(c).wait_recv()
        pair[c] = (part[c, :, core].astype(F32) + near[c].astype(F32)).astype(BF16)

    def send(c):
        for s in range(1, pairs):
            part_out(c, s).start()

    compute(0)
    near_out(0).start()
    compute(1)
    combine(0)

    @pl.loop(2, tiles)
    def _(c):
        near_out(c - 1).start()
        send(c - 2)
        compute(c)
        combine(c - 1)

    near_out(tiles - 1).start()
    send(tiles - 2)
    combine(tiles - 1)
    send(tiles - 1)

    @pl.loop(0, tiles)
    def _(c):
        total = pair[c, seat].astype(F32)
        for s in range(1, pairs):
            k = lax.rem(seat + s, pairs)
            remote(pair.at[c, k], got.at[c, k], p_send.at[c, 0], p_recv.at[c, k],
                   2 * k + core).wait_recv()
            total = total + got[c, k].astype(F32)
        d_trunk[:, pl.ds(pl.multiple_of(c * tile, tile), tile)] = total.astype(BF16)

    own.wait()
    for s in range(1, n_e):
        j = plane(s)
        remote(d_gate.at[j], gate_back.at[j], g_send.at[0], g_recv.at[j], j).wait_recv()
    for s in range(1, n_e):
        gate_out(s).wait_send()

    @pl.loop(0, tiles)
    def _(c):
        near_out(c).wait_send()
        for s in range(1, pairs):
            part_out(c, s).wait_send()


def return_all(d_pre, first, d_gate):
    n_e = lax.axis_size("expert")
    tile = 512
    depth, width = first.shape
    tiles = depth // tile
    share = d_pre.shape[0] // n_e
    hbm = pl.BlockSpec(memory_space=pltpu.HBM)
    vmem = pl.BlockSpec(memory_space=pltpu.VMEM)
    dma = pltpu.SemaphoreType.DMA
    return pl.pallas_call(
        functools.partial(return_kernel, n_e),
        out_shape=(
            jax.ShapeDtypeStruct((share, depth), BF16),
            jax.ShapeDtypeStruct(d_gate.shape, F32),
        ),
        in_specs=[vmem, hbm, vmem],
        out_specs=(vmem, vmem),
        scratch_shapes=[
            pltpu.VMEM((tiles, tile, width), BF16),
            pltpu.VMEM((tiles, n_e // 2, 2, share, tile), BF16),
            pltpu.VMEM((tiles, n_e // 2, share, tile), BF16),
            pltpu.VMEM((tiles, n_e // 2, share, tile), BF16),
            pltpu.VMEM((tiles, n_e // 2, share, tile), BF16),
            dma((tiles,)), dma((tiles,)), dma((tiles,)),
            dma((tiles, n_e // 2)), dma((tiles, n_e // 2)),
            dma((n_e,)), dma((n_e,)), dma,
        ],
        compiler_params=pltpu.CompilerParams(
            collective_id=1, has_side_effects=True, vmem_limit_bytes=48 * 1024 * 1024),
    )(d_pre, first.reshape(tiles, tile, width), d_gate)


def on_device(trunk, w_first, w_second, gates, d_mixed):
    rank = lax.axis_index("dp")
    first = w_first[0]
    second = w_second[0]
    gate_here = gates[0]
    n_dp = lax.axis_size("dp")
    depth = first.shape[0] // n_dp
    units = second.shape[0] // n_dp
    group = gate_here.shape[1]

    n_e = lax.axis_size("expert")
    gate_parts = gate_here.T.astype(F32).reshape(n_e, -1, gate_here.shape[0])
    rows_all, d_output_all, pre, gates_each, outs_each = gather_all(
        trunk, gate_parts, jnp.transpose(d_mixed, (1, 0, 2)), first, second)
    rows_all = rows_all.reshape(-1, trunk.shape[1])
    d_output_all = d_output_all.reshape(-1, second.shape[1])
    pre = pre.reshape(-1, first.shape[1])
    gates_each = gates_each.astype(BF16)
    d_hidden = lax.dot_general(
        d_output_all, second, (((1,), (1,)), ((), ())), preferred_element_type=F32
    )
    sig = jax.nn.sigmoid(pre)
    d_pre = (d_hidden * sig * (1.0 + pre * (1.0 - sig))).astype(BF16)
    d_pre_here = lax.dynamic_slice_in_dim(d_pre, rank * group, group, 0)
    mixed = jnp.einsum(
        "ert,ero->rto", gates_each, outs_each, preferred_element_type=F32
    ).astype(BF16)
    d_gate_each = jnp.einsum(
        "rto,ero->ert", d_mixed, outs_each, preferred_element_type=F32
    ).astype(BF16)
    d_trunk, back_gate = return_all(d_pre_here, first, d_gate_each.astype(F32))
    d_gate = back_gate.reshape(group, -1).T.astype(BF16)[None]

    columns = lax.dynamic_slice_in_dim(rows_all, rank * depth, depth, 1)
    d_first = lax.dot_general(
        columns, d_pre, (((0,), (0,)), ((), ())), preferred_element_type=F32
    ).astype(BF16)
    some_pre = lax.dynamic_slice_in_dim(pre, rank * units, units, 1)
    some_hidden = jax.nn.silu(some_pre).astype(BF16)
    d_second = lax.dot_general(
        some_hidden, d_output_all, (((0,), (0,)), ((), ())), preferred_element_type=F32
    ).astype(BF16)
    return (mixed, d_trunk, d_gate, d_first[None], d_second[None])


SIDE, LINE, LANES = 2, 4, 128
VMEM_BYTES = 62 * 1024 * 1024


def tiled(count, body, hooks=()):
    @pl.loop(0, count)
    def _(c):
        body(c)
        for at, hook in hooks:
            pl.when(c == at)(hook)


def step_kernel(n_e, n_d, trunk, gates, cot_in, first, second,
                columns_out, d_pre_out, second_out, mixed_out, d_trunk_out, back_out_ref,
                d_second,
                rows, d_out, d_pre, some_hidden, mixed, d_trunk, gate_back, gate_in, gate_piece,
                weights, later, turned, cot, gate_each, mix, piece, tall, hidden, made, outs, d_gate,
                part, near, pair, got,
                load_sem, own_sem, g_send, g_recv, t_send, t_recv, o_send, o_recv, z_send, z_recv,
                m_send, m_recv, n_send, n_recv, p_send, p_recv, b_send, b_recv, out_sem):
    e = lax.axis_index("expert")
    z = lax.axis_index("dp")
    core, seat, pairs = lax.rem(e, 2), e // 2, n_e // 2
    partner = e + 1 - 2 * core
    side, up = lax.rem(seat, SIDE), seat // SIDE
    across = e + 2 - 4 * side
    over = e + 2 * SIDE - 4 * SIDE * up
    corner = across + over - e
    bridge = across * (1 - core) + over * core
    other = across * core + over * (1 - core)
    middle = (z * (n_d - 1 - z)) // 2
    inner = middle == 1
    mate = z + 1 - 2 * lax.rem(z, 2)
    mirror = n_d - 1 - z
    skip = lax.rem(z + 2, n_d)
    order = [z, mate, middle * mirror + (1 - middle) * skip, middle * skip + (1 - middle) * mirror]
    tasks = cot.shape[0] // rows.shape[2]
    share, depth = rows.shape[2], rows.shape[3]
    width = tall.shape[2]
    group = n_e * share
    units = some_hidden.shape[2]
    part_depth = depth // n_d
    depth_here = pl.ds(pl.multiple_of(z * part_depth, part_depth), part_depth)

    def plane(s):
        return lax.rem(e + s, n_e)

    def remote(src, dst, send, recv, where):
        return pltpu.make_async_remote_copy(
            src_ref=src, dst_ref=dst, send_sem=send, recv_sem=recv,
            device_id=where, device_id_type=MESH)

    def load(k):
        src, dst = [(second, later), (cot_in, cot), (first, weights), (gates, gate_in)][k]
        return pltpu.make_async_copy(src, dst, load_sem.at[k])

    def own(k):
        src, dst = [(gate_piece.at[e], gate_each.at[e]), (trunk, rows.at[z, e]),
                    (piece.at[e], d_out.at[z, e]), (made.at[e], outs.at[e]),
                    (d_gate.at[e], gate_back.at[e])][k]
        return pltpu.make_async_copy(src, dst, own_sem.at[k])

    def at_plane(j):
        return {"expert": j}

    def gate_out(s):
        j = plane(s)
        return remote(gate_piece.at[j], gate_each.at[e], g_send.at[s], g_recv.at[e], at_plane(j))

    def trunk_out(g, k):
        zi = order[g]
        j, where = [
            (e, at_plane(across)), (e, at_plane(over)), (e, at_plane(partner)),
            (bridge, at_plane(over * (1 - core) + across * core)),
            (bridge, at_plane(partner)), (other, at_plane(partner)), (corner, at_plane(partner)),
            (e, {"dp": mate}), (e, {"dp": mirror})][k]
        src = trunk if g == 0 and k in (0, 1, 2, 7, 8) else rows.at[zi, j]
        return remote(src, rows.at[zi, j], t_send.at[g, k], t_recv.at[zi, j], where)

    def trunk_in(g, j):
        zi = order[g]
        remote(trunk, rows.at[zi, j], t_send.at[0, 0], t_recv.at[zi, j],
               at_plane(partner)).wait_recv()

    def piece_out(s):
        j = plane(s)
        return remote(piece.at[j], d_out.at[z, e], o_send.at[s], o_recv.at[e], at_plane(j))

    def half(zi, h):
        return d_out.at[zi, h * (n_e // 2):(h + 1) * (n_e // 2)]

    def line_out(g, k, h):
        zi = order[g]
        return remote(half(zi, h), half(zi, h), z_send.at[g, k, h], z_recv.at[zi, h],
                      {"dp": mate if k == 0 else mirror})

    def keep(k):
        src, dst = ([(rows.at[zi, :, :, depth_here], columns_out.at[zi]) for zi in order]
                    + [(d_pre.at[zi], d_pre_out.at[zi]) for zi in order]
                    + [(d_second, second_out), (mixed, mixed_out),
                       (d_trunk, d_trunk_out), (gate_back, back_out_ref)])[k]
        return pltpu.make_async_copy(src, dst, out_sem.at[k])

    def made_out(s):
        j = plane(s)
        return remote(made.at[j], outs.at[e], m_send.at[s], m_recv.at[e], at_plane(j))

    def back_out(s):
        j = plane(s)
        return remote(d_gate.at[j], gate_back.at[e], b_send.at[s], b_recv.at[e], at_plane(j))

    def near_out(c):
        return remote(part.at[c, :, 1 - core], near.at[c], n_send.at[c], n_recv.at[c],
                      at_plane(partner))

    def part_out(c, s):
        k = lax.rem(seat + s, pairs)
        return remote(pair.at[c, k], got.at[c, seat], p_send.at[c, s], p_recv.at[c, seat],
                      at_plane(2 * k + core))

    def spread(g):
        for k in range(3):
            trunk_out(g, k).start()

    def bridge_on(g):
        trunk_in(g, bridge)
        trunk_out(g, 3).start()
        trunk_out(g, 4).start()
        trunk_in(g, other)
        trunk_out(g, 5).start()

    def corner_on(g):
        trunk_in(g, corner)
        trunk_out(g, 6).start()

    def complete(g):
        for shift in (0, across - e, over - e, corner - e):
            trunk_in(g, partner + shift)

    def arrive(g):
        trunk_in(g, e)
        if g == 1:
            pl.when(inner)(lambda: trunk_out(1, 8).start())
        else:
            pl.when(inner)(lambda: trunk_out(g, 7).start())

    def line_arrive(g, h):
        zi = order[g]
        remote(half(zi, h), half(zi, h), z_send.at[0, 0, h], z_recv.at[zi, h],
               {"dp": mate}).wait_recv()
        pl.when(inner)(lambda: line_out(g, 1 if g == 1 else 0, h).start())

    def in_middle(call, *g):
        pl.when(inner)(lambda: call(*g))

    def at_end(call, *g):
        pl.when(middle == 0)(lambda: call(*g))

    for k in (3, 1, 0, 2):
        load(k).start()
    barrier = pltpu.get_barrier_semaphore()
    for s in range(1, n_e):
        pl.semaphore_signal(barrier, inc=1, device_id=at_plane(plane(s)), device_id_type=MESH)
    for i in range(1, n_d):
        pl.semaphore_signal(barrier, inc=1, device_id={"dp": lax.rem(z + i, n_d)},
                            device_id_type=MESH)
    load(3).wait()
    task_eye = jnp.where(
        lax.broadcasted_iota(jnp.int32, (tasks, LANES), 0)
        == lax.broadcasted_iota(jnp.int32, (tasks, LANES), 1), 1.0, 0.0).astype(BF16)
    gate_piece[...] = lax.dot_general(
        gate_in[...], task_eye, (((0,), (0,)), ((), ())),
        preferred_element_type=F32).reshape(gate_piece.shape)
    own(0).start()
    own(1).start()
    pl.semaphore_wait(barrier, n_e - 1 + n_d - 1)

    for s in range(1, n_e):
        gate_out(s).start()
    trunk_out(0, 7).start()
    pl.when(inner)(lambda: trunk_out(0, 8).start())
    spread(0)

    def turn(low, high):
        @pl.loop(low, high)
        def _(c):
            here = pl.ds(pl.multiple_of(c * 256, 256), 256)
            turned[:, here] = later[here, :].T

    turns = width // 256
    load(0).wait()
    turn(0, turns // 2)

    def task_of():
        shape = (LANES, share * tasks)
        return jnp.where(
            lax.broadcasted_iota(jnp.int32, shape, 0)
            == lax.rem(lax.broadcasted_iota(jnp.int32, shape, 1), tasks), 1.0, 0.0).astype(BF16)

    def same_sample():
        shape = (n_e, share, share * tasks)
        match = (lax.broadcasted_iota(jnp.int32, shape, 1)
                 == lax.div(lax.broadcasted_iota(jnp.int32, shape, 2), tasks))
        return jnp.where(match, 1.0, 0.0).reshape(group, share * tasks)

    for s in range(1, n_e):
        j = plane(s)
        remote(gate_piece.at[j], gate_each.at[j], g_send.at[0], g_recv.at[j],
               at_plane(j)).wait_recv()
    own(0).wait()
    load(1).wait()
    each = gate_each[...].reshape(group, LANES).astype(BF16)
    mix[...] = (jnp.dot(each, task_of(), preferred_element_type=F32)
                * same_sample()).astype(BF16)
    piece[...] = jnp.dot(mix[...], cot[...], preferred_element_type=F32).astype(BF16).reshape(
        piece.shape)
    for s in range(1, n_e):
        piece_out(s).start()
    own(2).start()

    turn(turns // 2, turns)
    bridge_on(0)
    arrive(1)
    in_middle(arrive, 2)
    for s in range(1, n_e):
        j = plane(s)
        remote(piece.at[j], d_out.at[z, j], o_send.at[0], o_recv.at[j], at_plane(j)).wait_recv()
    own(2).wait()
    for h in range(2):
        line_out(0, 0, h).start()
        in_middle(lambda: line_out(0, 1, h).start())

    tile = 512

    broad = 2 * tile

    def part_of(c, span=tile):
        return pl.ds(pl.multiple_of(c * span, span), span)

    def back_hidden(g, c, span=tile):
        left = d_out[order[g]].reshape(group, d_out.shape[3])
        return jnp.dot(left, turned[:, part_of(c, span)], preferred_element_type=F32)

    def forward_pre(g, c, span=tile):
        left = rows[order[g]].reshape(group, depth)
        return jnp.dot(left, weights[:, part_of(c, span)], preferred_element_type=F32)

    def store_d_pre(g, c, d_hidden, value, span=tile):
        sig = jax.nn.sigmoid(value)
        d_pre[order[g], :, part_of(c, span)] = (
            d_hidden * sig * (1.0 + value * (1.0 - sig))).astype(BF16)

    def first_hidden(c):
        tall[0, :, part_of(c, broad)] = back_hidden(0, c, broad)

    def first_pre(c):
        value = forward_pre(0, c)
        store_d_pre(0, c, tall[0, :, part_of(c)], value)
        hidden[:, part_of(c)] = (value * jax.nn.sigmoid(value)).astype(BF16)

    def later_pre(g, span=tile):
        def body(c):
            tall[g, :, part_of(c, span)] = forward_pre(g, c, span)
        return body

    def later_hidden(g):
        def body(c):
            store_d_pre(g, c, back_hidden(g, c), tall[g, :, part_of(c)])
        return body

    units_here = pl.ds(pl.multiple_of(z * units, units), units)

    def keep_units(g):
        value = tall[g, :, units_here]
        some_hidden[order[g]] = (value * jax.nn.sigmoid(value)).astype(BF16)

    tiled(width // broad, first_hidden)
    spread(1)
    corner_on(0)
    in_middle(arrive, 3)
    own(1).wait()
    complete(0)
    load(2).wait()

    def hook_a():
        at_end(arrive, 2)
        spread(2)

    tiled(width // tile, first_pre, [(2, hook_a)])
    keep(0).start()
    keep(4).start()
    some_hidden[z] = hidden[:, units_here]


    def compute(c):
        value = lax.dot_general(d_pre[z], weights[part_of(c), :], (((1,), (1,)), ((), ())),
                                preferred_element_type=F32)
        part[c] = value.astype(BF16).reshape(pairs, 2, share, tile)

    def combine(c):
        near_out(c).wait_recv()
        pair[c] = (part[c, :, core].astype(F32) + near[c].astype(F32)).astype(BF16)

    def send_parts(low, high):
        @pl.loop(low, high)
        def _(c):
            for s in range(1, pairs):
                part_out(c, s).start()

    count = depth // tile
    compute(0)
    near_out(0).start()
    bridge_on(1)
    compute(1)

    def hook_b():
        at_end(arrive, 3)
        at_end(spread, 3)

    def hook_c():
        for h in range(2):
            in_middle(line_arrive, 1, h)
            in_middle(line_arrive, 2, h)

    hooks = [(2, lambda: in_middle(spread, 3)), (4, hook_b), (5, hook_c), (6, lambda: bridge_on(2)),
             (7, lambda: corner_on(1))]

    @pl.loop(2, count)
    def _(c):
        near_out(c - 1).start()
        compute(c)
        combine(c - 2)
        for at, hook in hooks:
            pl.when(c == at)(hook)

    near_out(count - 1).start()

    def first_output(c):
        value = jnp.dot(hidden[...], later[:, part_of(c)], preferred_element_type=F32)
        made[:, :, part_of(c)] = value.astype(BF16).reshape(n_e, share, tile)

    tiled(made.shape[2] // tile, first_output)
    own(3).start()
    complete(1)
    keep(1).start()

    def hook_f():
        combine(count - 2)
        combine(count - 1)
        bridge_on(3)

    tiled(width // broad, later_pre(1, broad), [(0, hook_f)])
    keep_units(1)
    for h in range(2):
        at_end(line_arrive, 1, h)
    tiled(width // tile, later_hidden(1), [(1, lambda: corner_on(2))])
    send_parts(0, count // 2)
    keep(5).start()
    complete(2)
    keep(2).start()

    def hook_d():
        for h in range(2):
            in_middle(line_arrive, 3, h)

    def hook_e():
        for s in range(1, n_e):
            made_out(s).start()

    tiled(width // broad, later_pre(2, broad), [(0, hook_d), (1, hook_e)])
    keep_units(2)
    send_parts(count // 2, count)
    for h in range(2):
        at_end(line_arrive, 2, h)
    tiled(width // tile, later_hidden(2), [(1, lambda: corner_on(3))])
    keep(6).start()
    complete(3)
    keep(3).start()
    tiled(width // broad, later_pre(3, broad))
    keep_units(3)

    own(3).wait()
    for s in range(1, n_e):
        j = plane(s)
        remote(made.at[j], outs.at[j], m_send.at[0], m_recv.at[j], at_plane(j)).wait_recv()
    each_out = outs[...].reshape(group, outs.shape[2])
    product = lax.dot_general(each_out, cot[...], (((1,), (1,)), ((), ())),
                              preferred_element_type=F32)
    product = (product * same_sample()).astype(BF16)
    d_gate[...] = lax.dot_general(product, task_of(), (((1,), (1,)), ((), ())),
                                  preferred_element_type=F32).reshape(d_gate.shape)
    own(4).start()
    for s in range(1, n_e):
        back_out(s).start()
    mixed[...] = lax.dot_general(mix[...], each_out, (((0,), (0,)), ((), ())),
                                 preferred_element_type=F32).astype(BF16)

    keep(9).start()
    at_end(line_arrive, 3, 0)
    at_end(line_arrive, 3, 1)
    tiled(width // tile, later_hidden(3))
    keep(7).start()
    d_second[...] = lax.dot_general(
        some_hidden[...].reshape(-1, units), d_out[...].reshape(-1, d_out.shape[3]),
        (((0,), (0,)), ((), ())), preferred_element_type=F32).astype(BF16)
    keep(8).start()

    @pl.loop(0, count)
    def _(c):
        total = pair[c, seat].astype(F32)
        for s in range(1, pairs):
            k = lax.rem(seat + s, pairs)
            remote(pair.at[c, k], got.at[c, k], p_send.at[c, 0], p_recv.at[c, k],
                   at_plane(2 * k + core)).wait_recv()
            total = total + got[c, k].astype(F32)
        d_trunk[:, part_of(c)] = total.astype(BF16)

    keep(10).start()

    own(4).wait()
    for s in range(1, n_e):
        j = plane(s)
        remote(d_gate.at[j], gate_back.at[j], b_send.at[0], b_recv.at[j], at_plane(j)).wait_recv()
    for s in range(1, n_e):
        gate_out(s).wait_send()
        piece_out(s).wait_send()
        made_out(s).wait_send()
        back_out(s).wait_send()
    for g in range(n_d):
        for k in range(7):
            trunk_out(g, k).wait_send()
    keep(11).start()
    trunk_out(0, 7).wait_send()
    for h in range(2):
        line_out(0, 0, h).wait_send()

    @pl.when(inner)
    def _():
        trunk_out(0, 8).wait_send()
        trunk_out(1, 8).wait_send()
        for g in range(2, n_d):
            trunk_out(g, 7).wait_send()
        for h in range(2):
            line_out(0, 1, h).wait_send()
            line_out(1, 1, h).wait_send()
            for g in range(2, n_d):
                line_out(g, 0, h).wait_send()

    @pl.loop(0, count)
    def _(c):
        near_out(c).wait_send()
        for s in range(1, pairs):
            part_out(c, s).wait_send()

    for k in range(12):
        keep(k).wait()


def step_all(trunk, gates, cot, first, second):
    n_e, n_d = lax.axis_size("expert"), lax.axis_size("dp")
    share, depth = trunk.shape
    width = first.shape[1]
    out = second.shape[1]
    group = n_e * share
    count, pairs, tile = depth // 512, n_e // 2, 512
    hbm = pl.BlockSpec(memory_space=pltpu.HBM)
    dma = pltpu.SemaphoreType.DMA
    gate_shape = (n_e, share, LANES)
    return pl.pallas_call(
        functools.partial(step_kernel, n_e, n_d),
        out_shape=(
            jax.ShapeDtypeStruct((n_d, n_e, share, depth // n_d), BF16),
            jax.ShapeDtypeStruct((n_d, group, width), BF16),
            jax.ShapeDtypeStruct((width // n_d, out), BF16),
            jax.ShapeDtypeStruct((cot.shape[0], out), BF16),
            jax.ShapeDtypeStruct((share, depth), BF16),
            jax.ShapeDtypeStruct(gate_shape, F32),
        ),
        in_specs=[hbm] * 5,
        out_specs=(hbm,) * 6,
        scratch_shapes=[
            pltpu.VMEM((width // n_d, out), BF16),
            pltpu.VMEM((n_d, n_e, share, depth), BF16),
            pltpu.VMEM((n_d, n_e, share, out), BF16),
            pltpu.VMEM((n_d, group, width), BF16),
            pltpu.VMEM((n_d, group, width // n_d), BF16),
            pltpu.VMEM((cot.shape[0], out), BF16),
            pltpu.VMEM((share, depth), BF16),
            pltpu.VMEM(gate_shape, F32),
            pltpu.VMEM(gates.shape, BF16),
            pltpu.VMEM(gate_shape, F32),
            pltpu.VMEM(first.shape, BF16),
            pltpu.VMEM(second.shape, BF16),
            pltpu.VMEM(second.shape[::-1], BF16),
            pltpu.VMEM(cot.shape, BF16),
            pltpu.VMEM(gate_shape, F32),
            pltpu.VMEM((group, cot.shape[0]), BF16),
            pltpu.VMEM((n_e, share, out), BF16),
            pltpu.VMEM((n_d, group, width), F32),
            pltpu.VMEM((group, width), BF16),
            pltpu.VMEM((n_e, share, out), BF16),
            pltpu.VMEM((n_e, share, out), BF16),
            pltpu.VMEM(gate_shape, F32),
            pltpu.VMEM((count, pairs, 2, share, tile), BF16),
            pltpu.VMEM((count, pairs, share, tile), BF16),
            pltpu.VMEM((count, pairs, share, tile), BF16),
            pltpu.VMEM((count, pairs, share, tile), BF16),
            dma((4,)), dma((5,)),
            dma((n_e,)), dma((n_e,)),
            dma((n_d, 9)), dma((n_d, n_e)),
            dma((n_e,)), dma((n_e,)),
            dma((n_d, 2, 2)), dma((n_d, 2)),
            dma((n_e,)), dma((n_e,)),
            dma((count,)), dma((count,)),
            dma((count, pairs)), dma((count, pairs)),
            dma((n_e,)), dma((n_e,)), dma((12,)),
        ],
        compiler_params=pltpu.CompilerParams(
            collective_id=2, has_side_effects=True, vmem_limit_bytes=VMEM_BYTES),
    )(trunk, gates, cot, first, second)


def finish_kernel(columns, d_pre, second, mixed, d_trunk, back,
                  d_first, d_second, mixed_out, d_trunk_out, d_gate,
                  columns_v, d_pre_v, second_v, mixed_v, d_trunk_v, back_v,
                  first_v, gate_v, in_sem, out_sem, tile_sem, wide_sem):
    pairs = [(columns, columns_v), (second, second_v), (mixed, mixed_v),
             (d_trunk, d_trunk_v), (back, back_v)]
    steps = d_pre.shape[0]

    def take(k):
        return pltpu.make_async_copy(*pairs[k], in_sem.at[k])

    def wide(k):
        return pltpu.make_async_copy(d_pre.at[k], d_pre_v.at[k], wide_sem.at[k])

    def give(k):
        src, dst = [(second_v, d_second), (mixed_v, mixed_out), (d_trunk_v, d_trunk_out),
                    (gate_v, d_gate)][k]
        return pltpu.make_async_copy(src, dst, out_sem.at[k])

    take(0).start()
    for k in range(steps):
        wide(k).start()
    for k in range(1, len(pairs)):
        take(k).start()
    take(0).wait()
    for k in range(steps):
        wide(k).wait()
    tile = first_v.shape[1]
    count = first_v.shape[0]

    def store(c):
        here = pl.ds(pl.multiple_of(c * tile, tile), tile)
        return pltpu.make_async_copy(first_v.at[c], d_first.at[here], tile_sem.at[c])

    @pl.loop(0, count)
    def _(c):
        here = pl.ds(pl.multiple_of(c * tile, tile), tile)
        right = d_pre_v[...].reshape(-1, d_pre_v.shape[2])
        first_v[c] = lax.dot_general(
            columns_v[:, here], right, (((0,), (0,)), ((), ())),
            preferred_element_type=F32).astype(BF16)
        store(c).start()

        @pl.when(c == 0)
        def _():
            take(1).wait()
            give(0).start()
            take(2).wait()
            give(1).start()
            take(3).wait()
            give(2).start()
            take(4).wait()
            tasks = d_gate.shape[0]
            eye = jnp.where(
                lax.broadcasted_iota(jnp.int32, (tasks, LANES), 0)
                == lax.broadcasted_iota(jnp.int32, (tasks, LANES), 1), 1.0, 0.0).astype(BF16)
            gate_v[...] = lax.dot_general(
                eye, back_v[...].astype(BF16), (((1,), (1,)), ((), ())),
                preferred_element_type=F32).astype(BF16)
            give(3).start()

    for k in range(4):
        give(k).wait()

    @pl.loop(0, count)
    def _(c):
        store(c).wait()


def finish_all(columns, d_pre, second, mixed, d_trunk, back, tasks):
    hbm = pl.BlockSpec(memory_space=pltpu.HBM)
    dma = pltpu.SemaphoreType.DMA
    rows, depth = columns.shape
    steps, group, width = d_pre.shape
    tile = 256
    ins = (columns, d_pre, second, mixed, d_trunk, back)
    return pl.pallas_call(
        finish_kernel,
        out_shape=(
            jax.ShapeDtypeStruct((depth, width), BF16),
            jax.ShapeDtypeStruct(second.shape, BF16),
            jax.ShapeDtypeStruct(mixed.shape, BF16),
            jax.ShapeDtypeStruct(d_trunk.shape, BF16),
            jax.ShapeDtypeStruct((tasks, back.shape[0]), BF16),
        ),
        in_specs=[hbm] * 6,
        out_specs=(hbm,) * 5,
        scratch_shapes=[pltpu.VMEM(x.shape, x.dtype) for x in ins] + [
            pltpu.VMEM((depth // tile, tile, width), BF16),
            pltpu.VMEM((tasks, back.shape[0]), BF16),
            dma((5,)), dma((4,)), dma((depth // tile,)), dma((steps,)),
        ],
        compiler_params=pltpu.CompilerParams(vmem_limit_bytes=VMEM_BYTES),
    )(*ins)


def on_square(trunk, w_first, w_second, gates, d_mixed):
    first, second, gate_here = w_first[0], w_second[0], gates[0]
    tasks, group = gate_here.shape
    columns, d_pre, second_sum, mixed, d_trunk, back = step_all(
        trunk, gate_here, d_mixed.reshape(-1, d_mixed.shape[2]), first, second)
    d_first, d_second, mixed, d_trunk, d_gate = finish_all(
        columns.reshape(-1, columns.shape[3]), d_pre, second_sum, mixed, d_trunk,
        back.reshape(group, -1), tasks)
    return (mixed.reshape(d_mixed.shape), d_trunk, d_gate[None], d_first[None], d_second[None])


def solution(mesh):
    in_specs = (
        P(("dp", "expert"), None),
        P("expert", None, None),
        P("expert", None, None),
        P("expert", None, "dp"),
        P(("dp", "expert"), None, None),
    )
    out_specs = (
        P(("dp", "expert"), None, None),
        P(("dp", "expert"), None),
        P("expert", None, "dp"),
        P("expert", "dp", None),
        P("expert", "dp", None),
    )
    fits = mesh.shape["expert"] == 2 * SIDE * SIDE and mesh.shape["dp"] == LINE
    return jax.shard_map(
        on_square if fits else on_device, mesh=mesh, in_specs=in_specs, out_specs=out_specs, check_vma=False
    )
```
